32 devices in a mesh: fsdp: 8 (over z, y), tensor: 4 (over x, core).
Axes of the slice: x: 2, y: 2, z: 4, core: 2. Of those that a mesh axis runs over, the one named last changes fastest.
Arguments:
- block_input: bfloat16 [32768, 512], P(('fsdp', 'tensor')), may hold values from -6 to 6
- segments: int32 [32768], P('fsdp'), may hold values from 0 to 6, as said below
- ln_gain: bfloat16 [512], P('fsdp'), may hold values from 0.5 to 1.5
- ln_bias: bfloat16 [512], P('fsdp'), may hold values from -3 to 3
- b_real: bfloat16 [512, 256], P('fsdp', 'tensor'), may hold values from -0.1875 to 0.1875
- b_imag: bfloat16 [512, 256], P('fsdp', 'tensor'), may hold values from -0.1875 to 0.1875
- c_real: bfloat16 [512, 256], P('fsdp', 'tensor'), may hold values from -0.25 to 0.25
- c_imag: bfloat16 [512, 256], P('fsdp', 'tensor'), may hold values from -0.25 to 0.25
- nu_log: bfloat16 [256], P('fsdp'), may hold values from -9.1875 to -3
- theta_log: bfloat16 [256], P('fsdp'), may hold values from -4 to -1
- gamma_log: bfloat16 [256], P('fsdp'), may hold values from -0.5 to 0.5
- d_skip: bfloat16 [512], P('fsdp'), may hold values from -4 to 4
- w_value: bfloat16 [512, 512], P('fsdp', 'tensor'), may hold values from -0.25 to 0.25
- w_gate: bfloat16 [512, 512], P('fsdp', 'tensor'), may hold values from -0.25 to 0.25
- b_value: bfloat16 [512], P('fsdp'), may hold values from -3 to 3
- b_gate: bfloat16 [512], P('fsdp'), may hold values from -3 to 3
- out_grad: bfloat16 [32768, 512], P(('fsdp', 'tensor')), may hold values from -6 to 6
Outputs:
- mixed: bfloat16 [32768, 512], P(('fsdp', 'tensor'))
- input_grad: float32 [32768, 512], P(('fsdp', 'tensor'))
- ln_gain_grad: float32 [512], P('fsdp')
- ln_bias_grad: float32 [512], P('fsdp')
- b_real_grad: float32 [512, 256], P('fsdp', 'tensor')
- b_imag_grad: float32 [512, 256], P('fsdp', 'tensor')
- c_real_grad: float32 [512, 256], P('fsdp', 'tensor')
- c_imag_grad: float32 [512, 256], P('fsdp', 'tensor')
- nu_grad: float32 [256], P('fsdp')
- theta_grad: float32 [256], P('fsdp')
- gamma_grad: float32 [256], P('fsdp')
- skip_grad: float32 [512], P('fsdp')
- value_weight_grad: float32 [512, 512], P('fsdp', 'tensor')
- gate_weight_grad: float32 [512, 512], P('fsdp', 'tensor')
- value_bias_grad: float32 [512], P('fsdp')
- gate_bias_grad: float32 [512], P('fsdp')
The draws below stay inside these ranges and needn't reach their ends.
Inputs may be any that keep to these rules, and one draw needn't show every extreme that they name: `segments`: in each sequence of 2048 tokens the document numbers start at 1, rise by one at each of 5 boundaries that lie in the first three quarters, and all of 1 to 6 occur; the last 1 to 512 tokens are padding with number 0.
All inputs are finite; a program needn't handle non-finite values.
Results may differ from the reference program's by a relative error of at most 0.02.
Values may be sent and summed in bfloat16 or wider, within the bound.
No kernel may reach another device: no remote copies, remote signals or barrier semaphores. Data moves between devices by JAX's collectives and lax.ppermute only.
A program may use at most 128 MiB of HBM per device.

```python
import jax
import jax.numpy as jnp
from jax import lax

H = 512
N = 256
SEQ_LEN = 2048
DOCS = 6
TOKENS = 32768


def draw_segments(key, part):
    seq_count = TOKENS // SEQ_LEN
    pad_key, cut_key = jax.random.split(jax.random.fold_in(key, 11))
    padding = jax.random.randint(pad_key, (seq_count, 1), 1, SEQ_LEN // 4 + 1)
    valid = SEQ_LEN - padding
    cut_keys = jax.random.split(cut_key, seq_count)
    cuts = jax.vmap(lambda one_key: jax.random.permutation(one_key, SEQ_LEN * 3 // 4 - 1)[:DOCS - 1] + 1)(cut_keys)
    position = jnp.arange(SEQ_LEN)[None, :]
    document = 1 + jnp.sum(jnp.where(position[:, :, None] >= cuts[:, None, :], 1, 0), axis=2)
    labelled = jnp.where(position < valid, document, 0)
    return labelled.reshape(-1).astype(jnp.int32)


def block_levels(stream_key, dims, pieces, low, top_value):
    factor_of, own = 1.0, jax.random.fold_in(stream_key, 6)
    for dim, parts in pieces:
        heights = jnp.exp(jax.random.uniform(jax.random.fold_in(own, dim), (parts,), jnp.float32, low / len(pieces), top_value / len(pieces)))
        factor_of = factor_of * jnp.repeat(heights, dims[dim] // parts).reshape([-1 if axis == dim else 1 for axis in range(len(dims))])
    return factor_of


def bell_draw(stream_key, shape, deviation, bound, shards=(), dtype=jnp.bfloat16):
    drawn = deviation * jax.random.normal(stream_key, shape, jnp.float32)
    if shards:
        drawn = drawn * block_levels(stream_key, shape, shards, -0.22, 0.18)
    return jnp.clip(drawn, -bound, bound).astype(dtype)


def setup_inputs(seed: int = 0) -> dict:
    arg_keys = jax.random.split(jax.random.key(seed), 18)
    return {
        "block_input": bell_draw(arg_keys[0], (TOKENS, H), 1.0, 6.0, ((0, 32),)),
        "segments": draw_segments(jax.random.fold_in(arg_keys[17], 71), 0),
        "ln_gain": jnp.clip(1.0 + 0.1 * jax.random.normal(arg_keys[2], (H,), jnp.float32), 0.5, 1.5).astype(jnp.bfloat16),
        "ln_bias": bell_draw(arg_keys[3], (H,), 0.5, 3.0, ((0, 8),)),
        "b_real": bell_draw(arg_keys[4], (H, N), (2 * H) ** -0.5, 0.1875, ((0, 8), (1, 4))),
        "b_imag": bell_draw(arg_keys[5], (H, N), (2 * H) ** -0.5, 0.1875, ((0, 8), (1, 4))),
        "c_real": bell_draw(arg_keys[6], (H, N), (2 * N) ** -0.5, 0.25, ((0, 8), (1, 4))),
        "c_imag": bell_draw(arg_keys[7], (H, N), (2 * N) ** -0.5, 0.25, ((0, 8), (1, 4))),
        "nu_log": jnp.clip(-9.1875 + 6.1875 * jax.random.uniform(arg_keys[8], (N,), jnp.float32) ** block_levels(arg_keys[8], (N,), ((0, 8),), -0.2, 0.2), -9.1875, -3.0).astype(jnp.bfloat16),
        "theta_log": jnp.clip(-4.0 + 3.0 * jax.random.uniform(arg_keys[9], (N,), jnp.float32) ** block_levels(arg_keys[9], (N,), ((0, 8),), -0.2, 0.2), -4.0, -1.0).astype(jnp.bfloat16),
        "gamma_log": jnp.clip(jax.random.uniform(arg_keys[10], (N,), jnp.float32, -0.5, 0.5) * block_levels(arg_keys[10], (N,), ((0, 8),), -0.4, 0.0), -0.5, 0.5).astype(jnp.bfloat16),
        "d_skip": bell_draw(arg_keys[11], (H,), 1.0, 4.0, ((0, 8),)),
        "w_value": bell_draw(arg_keys[12], (H, H), H ** -0.5, 0.25, ((0, 8), (1, 4))),
        "w_gate": bell_draw(arg_keys[13], (H, H), H ** -0.5, 0.25, ((0, 8), (1, 4))),
        "b_value": bell_draw(arg_keys[14], (H,), 0.5, 3.0, ((0, 8),)),
        "b_gate": bell_draw(arg_keys[15], (H,), 0.5, 3.0, ((0, 8),)),
        "out_grad": bell_draw(arg_keys[16], (TOKENS, H), 1.0, 6.0, ((0, 32),)),
    }


@jax.custom_vjp
def low(v):
    return lax.optimization_barrier(v.astype(jnp.bfloat16)).astype(jnp.float32)

@jax.custom_vjp
def low_back(v):
    return v

def low_keep(v):
    return (low(v), None)

def low_pass(kept, grad):
    return (grad,)

def back_keep(v):
    return (v, None)

def back_low(kept, grad):
    return (low(grad),)
low.defvjp(low_keep, low_pass)
low_back.defvjp(back_keep, back_low)

def matmul(left, right):
    return jnp.dot(left, right, precision=lax.Precision.HIGHEST, preferred_element_type=jnp.float32)

def state_params(nu_part, theta_part, gamma_part):
    modulus = jnp.exp(-jnp.exp(nu_part))
    rotation = jnp.exp(theta_part)
    return (modulus * jnp.cos(rotation), modulus * jnp.sin(rotation), jnp.exp(gamma_part) * jnp.sqrt(1.0 - modulus * modulus))

def linear_chain(earlier, later):
    early_are, early_aim, early_bre, early_bim = earlier
    later_are, later_aim, later_bre, later_bim = later
    return (later_are * early_are - later_aim * early_aim, later_are * early_aim + later_aim * early_are, later_are * early_bre - later_aim * early_bim + later_bre, later_are * early_bim + later_aim * early_bre + later_bim)

def one_sequence(params, tokens, seg_ids):
    gain, shift, breal, bimag, creal, cimag, nu_part, theta_part, gamma_part, skip, wvalue, wgate, bias_value, bias_gate = params
    length = tokens.shape[0]
    live = jnp.where(seg_ids > 0, 1.0, 0.0).astype(jnp.float32)[:, None]
    earlier_ids = jnp.concatenate([seg_ids[:1], seg_ids[:-1]])
    keep = jnp.where((jnp.arange(length) > 0) & (seg_ids == earlier_ids), 1.0, 0.0).astype(jnp.float32)[:, None]
    centred = tokens - lax.optimization_barrier(jnp.mean(tokens, axis=1, keepdims=True))
    standard = centred * lax.rsqrt(lax.optimization_barrier(jnp.mean(centred * centred, axis=1, keepdims=True)) + 1e-05)
    normed = low(standard * gain + shift)
    drive_re = low_back(matmul(normed, breal))
    drive_im = low_back(matmul(normed, bimag))
    decay_re, decay_im, gamma = state_params(nu_part, theta_part, gamma_part)
    scanned = lax.associative_scan(linear_chain, (keep * decay_re, keep * decay_im, gamma * live * drive_re, gamma * live * drive_im))
    state_re = low(scanned[2])
    state_im = low(scanned[3])
    lru_out = low_back(matmul(state_re, creal.T) - matmul(state_im, cimag.T) + skip * normed)
    act = low(jax.nn.gelu(lru_out))
    value = low_back(matmul(act, wvalue) + bias_value)
    gate = low_back(matmul(act, wgate) + bias_gate)
    gated = low_back(low(value * jax.nn.sigmoid(gate)))
    return tokens + live * gated

def reference(block_input, segments, ln_gain, ln_bias, b_real, b_imag, c_real, c_imag, nu_log, theta_log, gamma_log, d_skip, w_value, w_gate, b_value, b_gate, out_grad):
    params = tuple((p.astype(jnp.float32) for p in (ln_gain, ln_bias, b_real, b_imag, c_real, c_imag, nu_log, theta_log, gamma_log, d_skip, w_value, w_gate, b_value, b_gate)))
    seq_count = block_input.shape[0] // SEQ_LEN
    tokens = block_input.astype(jnp.float32).reshape(seq_count, SEQ_LEN, H)
    seg_blocks = segments.reshape(seq_count, SEQ_LEN)
    checked = jax.checkpoint(one_sequence)

    def forward(weights, rows_all):

        def step(carry, item):
            return (carry, checked(weights, item[0], item[1]))
        _, outcome = lax.scan(step, jnp.zeros((), jnp.float32), (rows_all, seg_blocks))
        return outcome
    outcome, back = jax.vjp(forward, params, tokens)
    grads, input_grad = back(out_grad.astype(jnp.float32).reshape(seq_count, SEQ_LEN, H))
    return (outcome.reshape(-1, H).astype(jnp.bfloat16), input_grad.reshape(-1, H), grads[0], grads[1], grads[2], grads[3], grads[4], grads[5], grads[6], grads[7], grads[8], grads[9], grads[10], grads[11], grads[12], grads[13])
```

```python
import functools
import math

import jax
import jax.numpy as jnp
from jax import lax
from jax.experimental import pallas as pl
from jax.experimental.pallas import tpu as pltpu
from jax.sharding import PartitionSpec as P

SEQ_LEN = 2048
LANES = 128
AXES = ("fsdp", "tensor")
norm_epsilon = 1e-05
GELU_SCALE = math.sqrt(2.0 / math.pi)
GELU_CUBE = 0.044715
F32 = jnp.float32
BF16 = jnp.bfloat16


def bit_reversed(value, bits):
    out = 0
    for _ in range(bits):
        out = out * 2 + value % 2
        value //= 2
    return out


def flip(value, bit, count):
    return lax.ppermute(value, AXES, [(i, i ^ (1 << bit)) for i in range(count)])


def dot(left, right, left_dim=1, right_dim=0):
    return lax.dot_general(
        left, right, (((left_dim,), (right_dim,)), ((), ())), preferred_element_type=F32
    )


def fold_rows(value):
    rows, width = value.shape
    return jnp.sum(value.reshape(rows // 8, 8, width), axis=0)


def wide(mask, width):
    return jnp.concatenate([mask] * (width // LANES), axis=1)


def regroup_matrix(states, shards):
    own = states // shards
    width = 2 * states
    source = lax.broadcasted_iota(jnp.int32, (width, width), 0)
    target = lax.broadcasted_iota(jnp.int32, (width, width), 1)
    shard = source // (2 * own)
    part = (source % (2 * own)) // own
    place = part * states + shard * own + source % own
    return jnp.where(place == target, 1.0, 0.0).astype(BF16)


class Plan:
    def __init__(self, mesh, rows, group_rows, features, states, units):
        self.fsdp = mesh.shape["fsdp"]
        self.tensor = mesh.shape["tensor"]
        self.count = self.fsdp * self.tensor
        self.bits = self.count.bit_length() - 1
        self.rows = rows
        self.features = features
        self.states = states
        self.units = units
        self.own_rows = features // self.fsdp
        self.pieces = SEQ_LEN // rows
        self.chunks = 16
        self.span = rows // self.chunks
        self.tile = 256

    def slot_owner(self, slot, me):
        owner = me ^ bit_reversed(slot, self.bits)
        return owner // self.tensor, owner % self.tensor


def groups_of(value):
    return [value[..., at : at + LANES] for at in range(0, value.shape[-1], LANES)]


def put_groups(ref, at, value):
    for place, part in enumerate(groups_of(value)):
        ref[place, at, :] = part


def take_groups(ref, at):
    return jnp.concatenate([ref[place, at, :] for place in range(ref.shape[0])], axis=1)


def scan_pass(plan, keep_ref, rate, start, reverse, visit):
    chunks, span = plan.chunks, plan.span
    rate_re = groups_of(jnp.broadcast_to(rate[0], (chunks, plan.states)))
    rate_im = groups_of(jnp.broadcast_to(rate[1], (chunks, plan.states)))

    def step(index, carried):
        place = span - 1 - index if reverse else index
        at = pl.ds(place, chunks, stride=span)
        return visit(at, keep_ref[at, :], rate_re, rate_im, carried)

    return lax.fori_loop(0, span, step, start, unroll=4)


def advance(source_ref, at, keep, rate_re, rate_im, now):
    half = len(rate_re)
    following = [None] * (2 * half)
    for place in range(half):
        pass_re = keep * rate_re[place]
        pass_im = keep * rate_im[place]
        now_re, now_im = now[place], now[half + place]
        following[place] = (source_ref[place, at, :] + pass_re * now_re) - pass_im * now_im
        following[half + place] = (source_ref[half + place, at, :] + pass_re * now_im) + pass_im * now_re
    return following


def local_ends(plan, source_ref, keep_ref, rate, reverse):
    zero = jnp.zeros((plan.chunks, LANES), F32)
    groups = 2 * plan.states // LANES

    def visit(at, keep, rate_re, rate_im, carried):
        now, hold = carried
        return advance(source_ref, at, keep, rate_re, rate_im, now), hold * keep

    now, hold = scan_pass(plan, keep_ref, rate, ([zero] * groups, zero + 1.0), reverse, visit)
    half = groups // 2
    return jnp.concatenate(now[:half], axis=1), jnp.concatenate(now[half:], axis=1), hold


def rate_power(rate, times):
    re, im = rate
    while times > 1:
        re, im = re * re - im * im, 2.0 * re * im
        times //= 2
    return re, im


def chunk_entries(plan, ends_re, ends_im, hold, rate, start, reverse):
    power = rate_power(rate, plan.span)
    order = list(range(plan.chunks))
    if reverse:
        order.reverse()
    now_re, now_im = start
    rows_re, rows_im = [None] * plan.chunks, [None] * plan.chunks
    held = wide(hold, plan.states)
    for chunk in order:
        rows_re[chunk], rows_im[chunk] = now_re, now_im
        at = slice(chunk, chunk + 1)
        pass_re, pass_im = held[at] * power[0], held[at] * power[1]
        now_re, now_im = (
            pass_re * now_re - pass_im * now_im + ends_re[at],
            pass_re * now_im + pass_im * now_re + ends_im[at],
        )
    return (
        jnp.concatenate(rows_re, axis=0),
        jnp.concatenate(rows_im, axis=0),
        jnp.concatenate([now_re, now_im], axis=1),
    )


def collect(plan, me, refs, out_ref, parts):
    slot = 0
    rows = plan.own_rows
    for ref in refs:
        for place in range(ref.shape[0]):
            band, shard = plan.slot_owner(slot, me)
            slot += 1
            block = ref[place].astype(out_ref.dtype)
            at = pl.ds(pl.multiple_of(band * rows, rows), rows)
            width = block.shape[1] // parts
            for part in range(parts):
                base = part * plan.tensor * width
                column = pl.multiple_of(base + shard * width, LANES)
                out_ref[at, pl.ds(column, width)] = block[:, part * width : (part + 1) * width]


def distribute(plan, me, full_ref, refs, parts):
    slot = 0
    rows = plan.own_rows
    for ref in refs:
        width = ref.shape[2] // parts
        for place in range(ref.shape[0]):
            band, shard = plan.slot_owner(slot, me)
            slot += 1
            at = pl.ds(pl.multiple_of(band * rows, rows), rows)
            for part in range(parts):
                base = part * plan.tensor * width
                column = pl.multiple_of(base + shard * width, LANES)
                ref[place, :, part * width : (part + 1) * width] = full_ref[
                    at, pl.ds(column, width)
                ].astype(ref.dtype)


def normal_rows(values, gain, shift):
    wide_values = values.astype(F32)
    centred = wide_values - jnp.mean(wide_values, axis=1, keepdims=True)
    inverse = lax.rsqrt(jnp.mean(centred * centred, axis=1, keepdims=True) + norm_epsilon)
    standard = centred * inverse
    return standard, inverse


def state_rates(vec_ref, states):
    nu = vec_ref[5:6, :states].astype(F32)
    theta = vec_ref[6:7, :states].astype(F32)
    scale = vec_ref[7:8, :states].astype(F32)
    speed = jnp.exp(nu)
    modulus = jnp.exp(-speed)
    rotation = jnp.exp(theta)
    rate = (modulus * jnp.cos(rotation), modulus * jnp.sin(rotation))
    rest = 1.0 - modulus * modulus
    gamma = jnp.exp(scale) * jnp.sqrt(rest)
    return rate, gamma, speed, modulus, rest, rotation


def enter_kernel(
    plan, me_ref, x_ref, b0_ref, b1_ref, vec_ref, keep_ref, live_ref,
    normed_ref, source_ref, carry_ref, input_map_ref, pack_ref,
):
    me = me_ref[0]
    states = plan.states
    collect(plan, me, (b0_ref, b1_ref), pack_ref, 1)
    input_map_ref[...] = dot(pack_ref[...].astype(BF16), regroup_matrix(states, plan.tensor)).astype(BF16)
    gain = vec_ref[0:1, :].astype(F32)
    shift = vec_ref[1:2, :].astype(F32)
    rate, gamma, *_ = state_rates(vec_ref, states)
    gamma_pair = jnp.concatenate([gamma, gamma], axis=1)

    def rows_step(index, _):
        at = pl.ds(pl.multiple_of(index * plan.tile, plan.tile), plan.tile)
        standard, inverse = normal_rows(x_ref[at, :], gain, shift)
        normed = (standard * gain + shift).astype(BF16)
        normed_ref[at, :] = normed
        drive = dot(normed, input_map_ref[...])
        put_groups(source_ref, at, drive * gamma_pair * wide(live_ref[at, :], 2 * states))
        return 0

    lax.fori_loop(0, plan.rows // plan.tile, rows_step, 0)
    ends_re, ends_im, hold = local_ends(plan, source_ref, keep_ref, rate, False)
    zero = jnp.zeros((1, states), F32)
    _, _, leaving = chunk_entries(plan, ends_re, ends_im, hold, rate, (zero, zero), False)
    carry_ref[...] = jnp.broadcast_to(leaving, carry_ref.shape)


def middle_kernel(
    plan, me_ref, x_ref, grad_ref, normed_ref, source_ref, carry_ref,
    c0_ref, c1_ref, w0_ref, w1_ref, vec_ref, keep_ref, next_ref, live_ref,
    mixed_ref, hidden_ref, lru_grad_ref, state_grad_ref, back_ref,
    cs_ref, ck_ref, ws_ref, wk_ref, sums_ref,
    pack_ref, wpack_ref, out_map_ref, act_ref, unit_grad_ref, full_ref, low_ref,
):
    me = me_ref[0]
    states, features = plan.states, plan.features
    collect(plan, me, (c0_ref, c1_ref), pack_ref, 1)
    collect(plan, me, (w0_ref, w1_ref), wpack_ref, 2)
    regroup = regroup_matrix(states, plan.tensor)
    sign = jnp.where(
        lax.broadcasted_iota(jnp.int32, (1, 2 * states), 1) < states, 1.0, -1.0
    )
    out_map_ref[...] = (dot(pack_ref[...].astype(BF16), regroup) * sign).astype(BF16)
    rate, *_ = state_rates(vec_ref, states)
    ends_re, ends_im, hold = local_ends(plan, source_ref, keep_ref, rate, False)
    start = (carry_ref[0:1, :states], carry_ref[0:1, states:])
    entry_re, entry_im, _ = chunk_entries(plan, ends_re, ends_im, hold, rate, start, False)

    def visit(at, keep, rate_re, rate_im, now):
        now = advance(source_ref, at, keep, rate_re, rate_im, now)
        for place, part in enumerate(now):
            hidden_ref[place, at, :] = part
        return now

    scan_pass(plan, keep_ref, rate, groups_of(entry_re) + groups_of(entry_im), False, visit)
    skip = vec_ref[2:3, :].astype(F32)
    biases = jnp.concatenate([vec_ref[3:4, :], vec_ref[4:5, :]], axis=1).astype(F32)
    sums_ref[...] = jnp.zeros_like(sums_ref)

    def rows_step(index, _):
        at = pl.ds(pl.multiple_of(index * plan.tile, plan.tile), plan.tile)
        low = take_groups(hidden_ref, at).astype(BF16)
        low_ref[at, :] = low
        normed = normed_ref[at, :].astype(F32)
        lru = dot(low, out_map_ref[...], 1, 1) + skip * normed
        square = lru * lru
        bent = jnp.tanh(GELU_SCALE * lru * (1.0 + GELU_CUBE * square))
        half = 0.5 * (1.0 + bent)
        act = (lru * half).astype(BF16)
        slope = half + (0.5 * GELU_SCALE) * lru * (1.0 - bent * bent) * (
            1.0 + (3.0 * GELU_CUBE) * square
        )
        act_ref[at, :] = act
        mapped = dot(act, wpack_ref[...].astype(BF16)) + biases
        value = mapped[:, :features]
        opening = 0.5 + 0.5 * jnp.tanh(0.5 * mapped[:, features:])
        live = wide(live_ref[at, :], features)
        gated = value * opening
        mixed_ref[at, :] = (
            x_ref[at, :].astype(F32) + live * gated.astype(BF16).astype(F32)
        ).astype(BF16)
        gated_grad = live * grad_ref[at, :].astype(F32)
        value_grad = gated_grad * opening
        gate_grad = value_grad * value * (1.0 - opening)
        sums_ref[8:16, :] += fold_rows(value_grad)
        sums_ref[16:24, :] += fold_rows(gate_grad)
        unit_grad = jnp.concatenate([value_grad, gate_grad], axis=1).astype(BF16)
        unit_grad_ref[at, :] = unit_grad
        act_grad = dot(unit_grad, wpack_ref[...].astype(BF16), 1, 1)
        lru_grad = act_grad * slope
        sums_ref[0:8, :] += fold_rows(lru_grad * normed)
        lru_grad = lru_grad.astype(BF16)
        lru_grad_ref[at, :] = lru_grad
        put_groups(state_grad_ref, at, dot(lru_grad, out_map_ref[...]))
        return 0

    lax.fori_loop(0, plan.rows // plan.tile, rows_step, 0)
    back_rate = (rate[0], -rate[1])
    ends_re, ends_im, hold = local_ends(plan, state_grad_ref, next_ref, back_rate, True)
    zero = jnp.zeros((1, states), F32)
    _, _, leaving = chunk_entries(plan, ends_re, ends_im, hold, back_rate, (zero, zero), True)
    back_ref[...] = jnp.broadcast_to(leaving, back_ref.shape)
    full_ref[...] = dot(act_ref[...], unit_grad_ref[...], 0, 0)
    distribute(plan, me, full_ref, (wk_ref, ws_ref), 2)
    out_grad = dot(lru_grad_ref[...], low_ref[...], 0, 0) * sign
    full_ref[:, : 2 * states] = dot(out_grad.astype(BF16), regroup, 1, 1)
    distribute(plan, me, full_ref, (ck_ref, cs_ref), 1)


def leave_kernel(
    plan, me_ref, x_ref, grad_ref, normed_ref, source_ref, carry_ref, hidden_ref,
    state_grad_ref, lru_grad_ref, input_map_ref, vec_ref, next_ref, live_ref, sums_ref,
    input_grad_ref, bs_ref, bk_ref, out_sums_ref,
    drive_grad_ref, low_ref, full_ref,
):
    me = me_ref[0]
    states, features, chunks = plan.states, plan.features, plan.chunks
    rate, gamma, speed, modulus, rest, rotation = state_rates(vec_ref, states)
    back_rate = (rate[0], -rate[1])
    ends_re, ends_im, hold = local_ends(plan, state_grad_ref, next_ref, back_rate, True)
    start = (carry_ref[0:1, :states], carry_ref[0:1, states:])
    entry_re, entry_im, _ = chunk_entries(plan, ends_re, ends_im, hold, back_rate, start, True)
    zero = jnp.zeros((chunks, LANES), F32)
    gamma_wide = groups_of(jnp.broadcast_to(gamma, (chunks, states)))
    half = states // LANES

    def visit(at, keep, rate_re, rate_im, carried):
        now, rate_sum_re, rate_sum_im, gamma_sum = carried
        live = live_ref[at, :]
        after = [None] * (2 * half)
        sums = ([], [], [])
        for place in range(half):
            other = half + place
            next_re, next_im = keep * now[place], keep * now[other]
            hidden_re, hidden_im = hidden_ref[place, at, :], hidden_ref[other, at, :]
            sums[0].append(rate_sum_re[place] + (hidden_re * next_re + hidden_im * next_im))
            sums[1].append(rate_sum_im[place] + (hidden_re * next_im - hidden_im * next_re))
            rate_a, rate_b = rate_re[place], rate_im[place]
            now_re = (state_grad_ref[place, at, :] + rate_a * next_re) - rate_b * next_im
            now_im = (state_grad_ref[other, at, :] + rate_a * next_im) + rate_b * next_re
            driven = source_ref[place, at, :] * now_re + source_ref[other, at, :] * now_im
            sums[2].append(gamma_sum[place] + driven)
            scale = gamma_wide[place] * live
            drive_grad_ref[place, at, :] = scale * now_re
            drive_grad_ref[other, at, :] = scale * now_im
            after[place], after[other] = now_re, now_im
        return after, *sums

    _, rate_sum_re, rate_sum_im, gamma_sum = scan_pass(
        plan,
        next_ref,
        back_rate,
        (groups_of(entry_re) + groups_of(entry_im), [zero] * half, [zero] * half, [zero] * half),
        True,
        visit,
    )

    def total(parts):
        return jnp.sum(jnp.concatenate(parts, axis=1), axis=0, keepdims=True)

    rate_sum_re, rate_sum_im, gamma_sum = total(rate_sum_re), total(rate_sum_im), total(gamma_sum)
    nu_grad = speed * (
        gamma_sum * modulus * modulus / rest - (rate_sum_re * rate[0] + rate_sum_im * rate[1])
    )
    theta_grad = rotation * (rate_sum_im * rate[0] - rate_sum_re * rate[1])
    gain = vec_ref[0:1, :].astype(F32)
    shift = vec_ref[1:2, :].astype(F32)
    skip = vec_ref[2:3, :].astype(F32)
    gain_sum = jnp.zeros((8, features), F32)

    def rows_step(index, sums):
        gain_sum, shift_sum = sums
        at = pl.ds(pl.multiple_of(index * plan.tile, plan.tile), plan.tile)
        low = take_groups(drive_grad_ref, at).astype(BF16)
        low_ref[at, :] = low
        normed_grad = dot(low, input_map_ref[...], 1, 1) + skip * lru_grad_ref[at, :].astype(F32)
        standard, inverse = normal_rows(x_ref[at, :], gain, shift)
        gain_sum += fold_rows(normed_grad * standard)
        shift_sum += fold_rows(normed_grad)
        scaled = normed_grad * gain
        input_grad_ref[at, :] = grad_ref[at, :].astype(F32) + inverse * (
            scaled
            - jnp.mean(scaled, axis=1, keepdims=True)
            - standard * jnp.mean(scaled * standard, axis=1, keepdims=True)
        )
        return gain_sum, shift_sum

    gain_sum, shift_sum = lax.fori_loop(
        0, plan.rows // plan.tile, rows_step, (gain_sum, gain_sum)
    )
    into = dot(normed_ref[...], low_ref[...], 0, 0)
    full_ref[...] = dot(into.astype(BF16), regroup_matrix(states, plan.tensor), 1, 1)
    distribute(plan, me, full_ref, (bk_ref, bs_ref), 1)
    out_sums_ref[...] = jnp.zeros_like(out_sums_ref)
    out_sums_ref[0:1, :] = jnp.sum(gain_sum, axis=0, keepdims=True)
    out_sums_ref[1:2, :] = jnp.sum(shift_sum, axis=0, keepdims=True)
    for place in range(3):
        out_sums_ref[2 + place : 3 + place, :] = jnp.sum(
            sums_ref[8 * place : 8 * place + 8, :], axis=0, keepdims=True
        )
    out_sums_ref[5:6, :states] = nu_grad
    out_sums_ref[6:7, :states] = theta_grad
    out_sums_ref[7:8, :states] = gamma_sum


def call(kernel, plan, outs, scratch, *args):
    whole = pl.BlockSpec(memory_space=pltpu.VMEM)
    return pl.pallas_call(
        functools.partial(kernel, plan),
        out_shape=outs,
        in_specs=[pl.BlockSpec(memory_space=pltpu.SMEM)] + [whole] * (len(args) - 1),
        out_specs=[whole] * len(outs),
        scratch_shapes=scratch,
        compiler_params=pltpu.CompilerParams(vmem_limit_bytes=48 * 1024 * 1024),
    )(*args)


def shape(dims, dtype=F32):
    return jax.ShapeDtypeStruct(dims, dtype)


def gather_blocks(plan, block, summed=None):
    held = block[None]
    tensor_bits = plan.tensor.bit_length() - 1
    for stage in range(plan.bits):
        bit = plan.bits - 1 - stage
        if summed is not None and bit >= tensor_bits:
            count = held.shape[0] * held.shape[1]
            joined = jnp.concatenate([held.reshape(count, -1), summed], axis=0)
            other = flip(joined, bit, plan.count)
            summed = summed + other[count:]
            other = other[:count].reshape(held.shape)
        else:
            other = flip(held, bit, plan.count)
        if stage == plan.bits - 1:
            return held, other, summed
        held = jnp.concatenate([held, other], axis=0)


def split_high_low(value):
    high = value.astype(BF16)
    return jnp.concatenate([high, (value - high.astype(F32)).astype(BF16)], axis=0)


def scatter_blocks(plan, keep, send, summed=None):
    for stage in range(plan.bits):
        if summed is not None:
            count = send.shape[0] * send.shape[1]
            pair = split_high_low(summed)
            other = flip(jnp.concatenate([send.reshape(count, -1), pair], axis=0), stage, plan.count)
            rows = summed.shape[0]
            tail = other[count:].astype(F32)
            summed = summed + (tail[:rows] + tail[rows:])
            other = other[:count].reshape(send.shape)
        else:
            other = flip(send, stage, plan.count)
        total = keep.astype(F32) + other.astype(F32)
        half = total.shape[0] // 2
        if half:
            keep, send = total[:half].astype(BF16), total[half:].astype(BF16)
    return total[0], summed


def shards(
    mesh,
    block_input,
    segments,
    ln_gain,
    ln_bias,
    b_real,
    b_imag,
    c_real,
    c_imag,
    nu_log,
    theta_log,
    gamma_log,
    d_skip,
    w_value,
    w_gate,
    b_value,
    b_gate,
    out_grad,
):
    band = lax.axis_index("fsdp")
    shard = lax.axis_index("tensor")
    rows, features = block_input.shape
    own = b_real.shape[1]
    plan = Plan(
        mesh, rows, segments.shape[0], features, own * mesh.shape["tensor"], w_value.shape[1]
    )
    states, half = plan.states, plan.count // 2
    me = (band * plan.tensor + shard).astype(jnp.int32).reshape(1)

    position = jnp.arange(segments.shape[0])
    earlier = jnp.concatenate([segments[:1], segments[:-1]])
    keep = jnp.where((position % SEQ_LEN > 0) & (segments == earlier), 1.0, 0.0).astype(F32)
    following = jnp.concatenate([keep[1:], jnp.zeros((1,), F32)])
    live = jnp.where(segments > 0, 1.0, 0.0).astype(F32)

    def mine(mask):
        part = lax.dynamic_slice_in_dim(mask, shard * rows, rows, 0)
        return jnp.broadcast_to(part[:, None], (rows, LANES))

    keep, following, live = mine(keep), mine(following), mine(live)

    def placed(vector):
        length = vector.shape[0] * plan.fsdp
        spread = jnp.tile(vector, plan.fsdp)
        spread = jnp.where(jnp.arange(length) // vector.shape[0] == band, spread, 0)
        return jnp.pad(spread, (0, features - length))

    vectors = jnp.stack(
        [
            placed(v)
            for v in (
                ln_gain, ln_bias, d_skip, b_value, b_gate, nu_log, theta_log, gamma_log,
            )
        ]
    )
    b0, b1, vectors = gather_blocks(
        plan, jnp.concatenate([b_real, b_imag], axis=1), vectors.reshape(-1, 2 * own)
    )
    vectors = vectors.reshape(8, features)
    c0, c1, _ = gather_blocks(plan, jnp.concatenate([c_real, c_imag], axis=1))
    w0, w1, _ = gather_blocks(plan, jnp.concatenate([w_value, w_gate], axis=1))

    pack_type = BF16 if plan.own_rows % 16 == 0 else F32
    normed, source, carry, input_map = call(
        enter_kernel,
        plan,
        [
            shape((rows, features), BF16),
            shape((2 * states // LANES, rows, LANES)),
            shape((8, 2 * states)),
            shape((features, 2 * states), BF16),
        ],
        [pltpu.VMEM((features, 2 * states), pack_type)],
        me, block_input, b0, b1, vectors, keep, live,
    )

    def pass_on(value, forward):
        pairs = []
        for first in range(0, plan.tensor, 2):
            pairs.append((first, first + 1) if forward else (first + 1, first))
        return lax.ppermute(value, "tensor", pairs)

    if plan.pieces == 2:
        carry = pass_on(carry, True)
    else:
        carry = jnp.zeros_like(carry)
    half_block = (half, plan.own_rows)
    (
        mixed, hidden, lru_grad, state_grad, back,
        c_send, c_keep, w_send, w_keep, sums,
    ) = call(
        middle_kernel,
        plan,
        [
            shape((rows, features), BF16),
            shape((2 * states // LANES, rows, LANES)),
            shape((rows, features), BF16),
            shape((2 * states // LANES, rows, LANES)),
            shape((8, 2 * states)),
            shape((*half_block, 2 * own), BF16),
            shape((*half_block, 2 * own), BF16),
            shape((*half_block, 2 * plan.units), BF16),
            shape((*half_block, 2 * plan.units), BF16),
            shape((24, features)),
        ],
        [
            pltpu.VMEM((features, 2 * states), pack_type),
            pltpu.VMEM((features, 2 * features), pack_type),
            pltpu.VMEM((features, 2 * states), BF16),
            pltpu.VMEM((rows, features), BF16),
            pltpu.VMEM((rows, 2 * features), BF16),
            pltpu.VMEM((features, 2 * features), F32),
            pltpu.VMEM((rows, 2 * states), BF16),
        ],
        me, block_input, out_grad, normed, source, carry,
        c0, c1, w0, w1, vectors, keep, following, live,
    )
    back = pass_on(back, False) if plan.pieces == 2 else jnp.zeros_like(back)
    w_mine, _ = scatter_blocks(plan, w_keep, w_send)
    c_mine, _ = scatter_blocks(plan, c_keep, c_send)
    input_grad, b_send, b_keep, vector_sums = call(
        leave_kernel,
        plan,
        [
            shape((rows, features)),
            shape((*half_block, 2 * own), BF16),
            shape((*half_block, 2 * own), BF16),
            shape((8, features)),
        ],
        [
            pltpu.VMEM((2 * states // LANES, rows, LANES), F32),
            pltpu.VMEM((rows, 2 * states), BF16),
            pltpu.VMEM((features, 2 * states), F32),
        ],
        me, block_input, out_grad, normed, source, back, hidden,
        state_grad, lru_grad, input_map, vectors, following, live, sums,
    )
    b_mine, vector_sums = scatter_blocks(plan, b_keep, b_send, vector_sums.reshape(-1, 2 * own))
    vector_sums = vector_sums.reshape(8, features)

    def vector(place, length):
        return lax.dynamic_slice(vector_sums[place], (band * length,), (length,))

    units = plan.units
    long, short = plan.own_rows, states // plan.fsdp
    return (
        mixed,
        input_grad,
        vector(0, long),
        vector(1, long),
        b_mine[:, :own],
        b_mine[:, own:],
        c_mine[:, :own],
        c_mine[:, own:],
        vector(5, short),
        vector(6, short),
        vector(7, short),
        vector(2, long),
        w_mine[:, :units],
        w_mine[:, units:],
        vector(3, long),
        vector(4, long),
    )


def solution(mesh):
    in_specs = (
        P(("fsdp", "tensor"), None),
        P("fsdp"),
        P("fsdp"),
        P("fsdp"),
        P("fsdp", "tensor"),
        P("fsdp", "tensor"),
        P("fsdp", "tensor"),
        P("fsdp", "tensor"),
        P("fsdp"),
        P("fsdp"),
        P("fsdp"),
        P("fsdp"),
        P("fsdp", "tensor"),
        P("fsdp", "tensor"),
        P("fsdp"),
        P("fsdp"),
        P(("fsdp", "tensor"), None),
    )
    out_specs = (
        P(("fsdp", "tensor"), None),
        P(("fsdp", "tensor"), None),
        P("fsdp"),
        P("fsdp"),
        P("fsdp", "tensor"),
        P("fsdp", "tensor"),
        P("fsdp", "tensor"),
        P("fsdp", "tensor"),
        P("fsdp"),
        P("fsdp"),
        P("fsdp"),
        P("fsdp"),
        P("fsdp", "tensor"),
        P("fsdp", "tensor"),
        P("fsdp"),
        P("fsdp"),
    )
    return jax.shard_map(
        functools.partial(shards, mesh),
        mesh=mesh,
        in_specs=in_specs,
        out_specs=out_specs,
        check_vma=False,
    )
```

```python
import functools
import math

import jax
import jax.numpy as jnp
from jax import lax
from jax.experimental import pallas as pl
from jax.experimental.pallas import tpu as pltpu
from jax.sharding import PartitionSpec as P

SEQ_LEN = 2048
LANES = 128
TILE = 256
SIDE = 16
AXES = ("fsdp", "tensor")
norm_epsilon = 1e-05
GELU_SCALE = math.sqrt(2.0 / math.pi)
GELU_CUBE = 0.044715
F32 = jnp.float32
BF16 = jnp.bfloat16
MIB = 1024 * 1024


def log2(value):
    return value.bit_length() - 1


def flip(value, bit, count):
    return lax.ppermute(value, AXES, [(i, i ^ (1 << bit)) for i in range(count)])


def dot(left, right, left_dim=1, right_dim=0):
    return lax.dot_general(
        left, right, (((left_dim,), (right_dim,)), ((), ())), preferred_element_type=F32
    )


def fold_rows(value):
    rows, width = value.shape
    return jnp.sum(value.reshape(rows // 8, 8, width), axis=0)


def wide(mask, width):
    return jnp.concatenate([mask] * (width // LANES), axis=1)


def grid_index(dims, axis):
    return lax.broadcasted_iota(jnp.int32, dims, axis)


def regroup_matrix(states, shards):
    own = log2(states // shards)
    width = 2 * states
    source = grid_index((width, width), 0)
    target = grid_index((width, width), 1)
    part = (source >> own) & 1
    place = part * states + ((source >> (own + 1)) << own) + (source & ((1 << own) - 1))
    return jnp.where(place == target, 1.0, 0.0).astype(BF16)


def turn_matrix():
    source = grid_index((TILE, TILE), 0)
    target = grid_index((TILE, TILE), 1)
    bits = log2(SIDE)
    place = ((source & (SIDE - 1)) << bits) + (source >> bits)
    return jnp.where(place == target, 1.0, 0.0)


class Plan:
    def __init__(self, mesh, rows, group_rows, features, states, units):
        self.fsdp = mesh.shape["fsdp"]
        self.tensor = mesh.shape["tensor"]
        self.count = self.fsdp * self.tensor
        self.bits = log2(self.count)
        outer = list(range(self.bits - 1, 2, -1))
        self.outer = outer
        self.up = [*outer, 2, 1, 0]
        self.up_crossed = [*outer, 1, 2, 0]
        self.down = [0, 1, 2, *outer[::-1]]
        self.down_crossed = [0, 2, 1, *outer[::-1]]
        self.halves = 2 if features // self.fsdp >= 32 else 1
        self.rows = rows
        self.group_rows = group_rows
        self.features = features
        self.states = states
        self.units = units
        self.own_states = states // self.tensor
        self.own_rows = features // self.fsdp
        self.pieces = SEQ_LEN // rows
        self.tiles = rows // TILE
        self.chunks = self.tiles * SIDE

    def slot_owner(self, slot, me, order):
        owner = me
        for place, bit in enumerate(order):
            owner = owner ^ (((slot >> (self.bits - 1 - place)) & 1) << bit)
        shift = log2(self.tensor)
        return owner >> shift, owner & (self.tensor - 1)

    def tile_rows(self, index):
        return pl.ds(pl.multiple_of(index * TILE, TILE), TILE)


def step_rows(tile, place):
    return pl.ds(pl.multiple_of(tile * TILE + place * SIDE, SIDE), SIDE)


def scan_pass(plan, keep_ref, start, extra, reverse, visit):
    def step(index, carried):
        now, extra = carried
        place = SIDE - 1 - index if reverse else index
        after = []
        for tile in range(plan.tiles):
            at = step_rows(tile, place)
            state, extra = visit(tile, at, keep_ref[at, :], now[tile], extra)
            after.append(state)
        return after, extra

    return lax.fori_loop(0, SIDE, step, (start, extra), unroll=2)


def local_ends(plan, source_ref, keep_ref, rate, reverse):
    states = plan.states
    zero = jnp.zeros((SIDE, states), F32)
    rate_re = jnp.broadcast_to(rate[0], zero.shape)
    rate_im = jnp.broadcast_to(rate[1], zero.shape)
    one = jnp.ones((SIDE, LANES), F32)

    def visit(tile, at, keep, state, extra):
        now_re, now_im, hold = state
        held = wide(keep, states)
        pass_re, pass_im = held * rate_re, held * rate_im
        source = source_ref[at, :]
        next_re = (source[:, :states] + pass_re * now_re) - pass_im * now_im
        next_im = (source[:, states:] + pass_re * now_im) + pass_im * now_re
        return (next_re, next_im, hold * keep), extra

    ends, _ = scan_pass(plan, keep_ref, [(zero, zero, one)] * plan.tiles, 0, reverse, visit)
    return tuple(jnp.concatenate([end[part] for end in ends], axis=0) for part in range(3))


def shifted(value, distance, reverse):
    count = value.shape[0]
    row = grid_index(value.shape, 0)
    if reverse:
        moved = pltpu.roll(value, count - distance, 0)
        return jnp.where(row < count - distance, moved, 0.0)
    moved = pltpu.roll(value, distance, 0)
    return jnp.where(row >= distance, moved, 0.0)


def chunk_entries(plan, ends_re, ends_im, hold, rate, start, reverse):
    states, count = plan.states, plan.chunks
    power_re, power_im = rate
    for _ in range(log2(SIDE)):
        power_re, power_im = power_re * power_re - power_im * power_im, 2.0 * power_re * power_im
    first = count - 1 if reverse else 0
    if start is not None:
        at_first = grid_index((count, states), 0) == first
        held = jnp.where(at_first, wide(hold, states), 0.0)
        pass_re, pass_im = held * power_re, held * power_im
        ends_re = ends_re + (pass_re * start[0] - pass_im * start[1])
        ends_im = ends_im + (pass_re * start[1] + pass_im * start[0])
    distance = 1
    while distance < count:
        earlier_re = shifted(ends_re, distance, reverse)
        earlier_im = shifted(ends_im, distance, reverse)
        held = wide(hold, states)
        pass_re, pass_im = held * power_re, held * power_im
        ends_re = ends_re + (pass_re * earlier_re - pass_im * earlier_im)
        ends_im = ends_im + (pass_re * earlier_im + pass_im * earlier_re)
        hold = hold * shifted(hold, distance, reverse)
        power_re, power_im = power_re * power_re - power_im * power_im, 2.0 * power_re * power_im
        distance *= 2
    last = slice(0, 1) if reverse else slice(count - 1, count)
    leaving = jnp.concatenate([ends_re[last], ends_im[last]], axis=1)
    if start is None:
        return None, leaving
    entry_re = shifted(ends_re, 1, reverse) + jnp.where(at_first, start[0], 0.0)
    entry_im = shifted(ends_im, 1, reverse) + jnp.where(at_first, start[1], 0.0)
    entries = []
    for tile in range(plan.tiles):
        at = slice(tile * SIDE, (tile + 1) * SIDE)
        entries.append((entry_re[at], entry_im[at]))
    return entries, leaving


def block_places(plan, me, order, refs, base, rows, start):
    slot = 0
    for ref in refs:
        for place in range(plan.count // 2):
            band, shard = plan.slot_owner(slot, me, order)
            slot += 1
            first = pl.multiple_of(band * plan.own_rows + start, rows)
            yield ref, base + place * rows, pl.ds(first, rows), shard


def collect(plan, me, order, refs, base, rows, start, targets):
    for ref, row, at, shard in block_places(plan, me, order, refs, base, rows, start):
        for first, width, out_ref, lanes in targets:
            column = pl.multiple_of(lanes + shard * width, LANES)
            out_ref[at, pl.ds(column, width)] = ref[row : row + rows, first : first + width].astype(
                out_ref.dtype
            )


def distribute(plan, me, order, refs, base, rows, start, targets):
    for ref, row, at, shard in block_places(plan, me, order, refs, base, rows, start):
        for first, width, full_ref, lanes in targets:
            column = pl.multiple_of(lanes + shard * width, LANES)
            ref[row : row + rows, first : first + width] = full_ref[at, pl.ds(column, width)].astype(
                ref.dtype
            )


def half_blocks(plan, straight, crossed):
    rows = plan.own_rows // plan.halves
    for half in range(plan.halves):
        yield (straight, crossed)[half], half * plan.count // 2 * rows, rows, half * rows


def start_copies(pairs, sems):
    copies = [
        pltpu.make_async_copy(source, target, sems.at[place])
        for place, (source, target) in enumerate(pairs)
    ]
    for copy in copies:
        copy.start()
    return copies


def pack_kernel(plan, me_ref, *refs):
    sources, outs, held, sems = refs[:14], refs[14:16], refs[16:30], refs[30]
    copies = start_copies(list(zip(sources, held)), sems)
    first_ref, second_ref = outs
    band = me_ref[0] >> log2(plan.tensor)
    rows, features = plan.own_rows, plan.features
    for copy in copies:
        copy.wait()
    first_ref[:rows, :] = jnp.concatenate([held[0][...], held[1][...]], axis=1)
    second_ref[...] = jnp.concatenate([ref[...] for ref in held[2:6]], axis=1)
    placed = []
    lane = grid_index((1, features), 1)
    for ref in held[6:]:
        length = ref.shape[1]
        value = ref[...].astype(F32)
        value = jnp.concatenate([value] * (features // length), axis=1)
        placed.append(jnp.where((lane >> log2(length)) == band, value, 0.0))
    placed = jnp.concatenate(placed, axis=0).astype(BF16)
    for part in range(features // LANES):
        first_ref[rows + 8 * part : rows + 8 * part + 8, :] = placed[
            :, part * LANES : (part + 1) * LANES
        ]


def token_kernel(plan, me_ref, x_ref, segments_ref, stats_ref, masks_ref, flags_ref):
    shard = me_ref[0] & (plan.tensor - 1)
    ids = segments_ref[...]
    count = ids.shape[0]
    lane = grid_index(ids.shape, 1)
    position = (grid_index(ids.shape, 0) * LANES + lane) & (SEQ_LEN - 1)
    turned = pltpu.roll(ids, 1, 1)
    before = jnp.where(lane == 0, pltpu.roll(turned, 1, 0), turned)
    turned = pltpu.roll(ids, LANES - 1, 1)
    after = jnp.where(lane == LANES - 1, pltpu.roll(turned, count - 1, 0), turned)
    flags_ref[0] = jnp.where((position > 0) & (ids == before), 1.0, 0.0)
    flags_ref[1] = jnp.where((position < SEQ_LEN - 1) & (ids == after), 1.0, 0.0)
    flags_ref[2] = jnp.where(ids > 0, 1.0, 0.0)
    turn = turn_matrix()
    plain = jnp.where(grid_index((TILE, TILE), 0) == grid_index((TILE, TILE), 1), 1.0, 0.0)
    ones = jnp.ones((TILE, LANES), BF16)
    per_tile = TILE // LANES
    own = plan.rows // LANES
    flags = [flags_ref[kind, pl.ds(pl.multiple_of(shard * own, own), own), :] for kind in range(3)]
    for tile in range(plan.tiles):
        at = slice(tile * TILE, (tile + 1) * TILE)
        for kind in range(4):
            rows = flags[min(kind, 2)][tile * per_tile : (tile + 1) * per_tile, :]
            line = jnp.concatenate([rows[part : part + 1, :] for part in range(per_tile)], axis=1)
            spread = (plain if kind == 3 else turn) * line
            masks_ref[kind, at, :] = dot(spread.astype(BF16), ones)

    def rows_step(index, _):
        at = plan.tile_rows(index)
        values = x_ref[at, :].astype(F32)
        mean = jnp.mean(values, axis=1, keepdims=True)
        centred = values - mean
        inverse = lax.rsqrt(jnp.mean(centred * centred, axis=1, keepdims=True) + norm_epsilon)
        stats_ref[0, at, :] = jnp.broadcast_to(mean, (TILE, LANES))
        stats_ref[1, at, :] = jnp.broadcast_to(inverse, (TILE, LANES))
        return 0

    lax.fori_loop(0, plan.tiles, rows_step, 0)


def standard_rows(plan, x_ref, stats_ref, at):
    mean = wide(stats_ref[0, at, :], plan.features)
    inverse = wide(stats_ref[1, at, :], plan.features)
    return (x_ref[at, :].astype(F32) - mean) * inverse, inverse


def read_vectors(vec_ref):
    count = vec_ref.shape[0] // 8
    parts = [vec_ref[8 * part : 8 * part + 8, :].astype(F32) for part in range(count)]
    return jnp.concatenate(parts, axis=1)


def enter_kernel(
    plan, me_ref, x_ref, stats_ref, b0_ref, b1_ref, vec_ref, masks_ref,
    normed_ref, source_ref, ends_ref, hold_ref, carry_ref, input_map_ref, params_ref,
    pack_ref,
):
    states = plan.states
    collect(
        plan, me_ref[0], plan.up[::-1], (b0_ref, b1_ref), 0, plan.own_rows, 0,
        [(0, 2 * plan.own_states, pack_ref, 0)],
    )
    input_map_ref[...] = dot(
        pack_ref[...].astype(BF16), regroup_matrix(states, plan.tensor)
    ).astype(BF16)
    vectors = read_vectors(vec_ref)
    gain, shift = vectors[0:1], vectors[1:2]
    speed = jnp.exp(vectors[5:6, :states])
    modulus = jnp.exp(-speed)
    rotation = jnp.exp(vectors[6:7, :states])
    rate = (modulus * jnp.cos(rotation), modulus * jnp.sin(rotation))
    rest = 1.0 - modulus * modulus
    gamma = jnp.exp(vectors[7:8, :states]) * jnp.sqrt(rest)
    params_ref[...] = jnp.concatenate(
        [
            jnp.concatenate(rate, axis=1),
            jnp.concatenate([gamma, speed], axis=1),
            jnp.concatenate([modulus, rest], axis=1),
            jnp.concatenate([rotation, rotation], axis=1),
            jnp.zeros((4, 2 * states), F32),
        ],
        axis=0,
    )
    gamma_pair = jnp.concatenate([gamma, gamma], axis=1)
    turn = turn_matrix().astype(BF16)

    def rows_step(index, _):
        at = plan.tile_rows(index)
        standard, _ = standard_rows(plan, x_ref, stats_ref, at)
        normed = (standard * gain + shift).astype(BF16)
        normed_ref[at, :] = normed
        turned = dot(turn, normed).astype(BF16)
        drive = dot(turned, input_map_ref[...])
        source_ref[at, :] = drive * gamma_pair * wide(masks_ref[2, at, :], 2 * states)
        return 0

    lax.fori_loop(0, plan.tiles, rows_step, 0)
    ends_re, ends_im, hold = local_ends(plan, source_ref, masks_ref.at[0], rate, False)
    ends_ref[...] = jnp.concatenate([ends_re, ends_im], axis=1)
    hold_ref[...] = hold
    _, leaving = chunk_entries(plan, ends_re, ends_im, hold, rate, None, False)
    carry_ref[...] = jnp.broadcast_to(leaving, carry_ref.shape)


def middle_kernel(
    plan, me_ref, x_ref, grad_ref, normed_ref, source_ref, ends_ref, hold_ref, carry_ref,
    g0_ref, g1_ref, vec_ref, params_ref, masks_ref,
    mixed_ref, hidden_ref, lru_grad_ref, state_grad_ref, act_ref, unit_grad_ref, low_ref, sums_ref,
    pack_ref, wpack_ref, out_map_ref,
):
    states, features, units = plan.states, plan.features, plan.units
    pair = 2 * plan.own_states
    targets = [
        (0, pair, pack_ref, 0),
        (pair, units, wpack_ref, 0),
        (pair + units, units, wpack_ref, features),
    ]
    for order, base, rows, first in half_blocks(plan, plan.up[::-1], plan.up_crossed[::-1]):
        collect(plan, me_ref[0], order, (g0_ref, g1_ref), base, rows, first, targets)
    sign = jnp.where(grid_index((1, 2 * states), 1) < states, 1.0, -1.0)
    regroup = regroup_matrix(states, plan.tensor)
    out_map_ref[...] = (dot(pack_ref[...].astype(BF16), regroup) * sign).astype(BF16)
    rate = (params_ref[0:1, :states], params_ref[0:1, states:])
    start = (carry_ref[0:1, :states], carry_ref[0:1, states:])
    entries, _ = chunk_entries(
        plan, ends_ref[:, :states], ends_ref[:, states:], hold_ref[...], rate, start, False
    )
    rate_re = jnp.broadcast_to(rate[0], (SIDE, states))
    rate_im = jnp.broadcast_to(rate[1], (SIDE, states))

    def visit(tile, at, keep, state, extra):
        now_re, now_im = state
        held = wide(keep, states)
        pass_re, pass_im = held * rate_re, held * rate_im
        source = source_ref[at, :]
        next_re = (source[:, :states] + pass_re * now_re) - pass_im * now_im
        next_im = (source[:, states:] + pass_re * now_im) + pass_im * now_re
        hidden_ref[at, :states] = next_re
        hidden_ref[at, states:] = next_im
        return (next_re, next_im), extra

    scan_pass(plan, masks_ref.at[0], entries, 0, False, visit)
    vectors = read_vectors(vec_ref)
    skip = vectors[2:3]
    biases = jnp.concatenate([vectors[3:4], vectors[4:5]], axis=1)
    sums_ref[...] = jnp.zeros_like(sums_ref)
    turn = turn_matrix().astype(BF16)

    def rows_step(index, _):
        at = plan.tile_rows(index)
        low = dot(turn, hidden_ref[at, :].astype(BF16)).astype(BF16)
        low_ref[at, :] = low
        normed = normed_ref[at, :].astype(F32)
        lru = dot(low, out_map_ref[...], 1, 1) + skip * normed
        square = lru * lru
        bent = jnp.tanh(lru * (GELU_SCALE + (GELU_SCALE * GELU_CUBE) * square))
        half = 0.5 + 0.5 * bent
        act = (lru * half).astype(BF16)
        slope = half + lru * (1.0 - bent * bent) * (
            0.5 * GELU_SCALE + (1.5 * GELU_SCALE * GELU_CUBE) * square
        )
        act_ref[at, :] = act
        mapped = dot(act, wpack_ref[...].astype(BF16)) + biases
        value = mapped[:, :features]
        opening = 0.5 + 0.5 * jnp.tanh(0.5 * mapped[:, features:])
        live = wide(masks_ref[3, at, :], features)
        gated = value * opening
        mixed_ref[at, :] = (
            x_ref[at, :].astype(F32) + live * gated.astype(BF16).astype(F32)
        ).astype(BF16)
        value_grad = live * grad_ref[at, :].astype(F32) * opening
        gate_grad = value_grad * (value - gated)
        sums_ref[8:16, :] += fold_rows(value_grad)
        sums_ref[16:24, :] += fold_rows(gate_grad)
        unit_grad = jnp.concatenate([value_grad, gate_grad], axis=1).astype(BF16)
        unit_grad_ref[at, :] = unit_grad
        act_grad = dot(unit_grad, wpack_ref[...].astype(BF16), 1, 1)
        lru_grad = act_grad * slope
        sums_ref[0:8, :] += fold_rows(lru_grad * normed)
        lru_grad = lru_grad.astype(BF16)
        lru_grad_ref[at, :] = lru_grad
        turned = dot(turn, lru_grad).astype(BF16)
        state_grad_ref[at, :] = dot(turned, out_map_ref[...])
        return 0

    lax.fori_loop(0, plan.tiles, rows_step, 0)


def back_kernel(
    plan, me_ref, state_grad_ref, params_ref, masks_ref, back_ends_ref, back_hold_ref, back_ref
):
    states = plan.states
    back_rate = (params_ref[0:1, :states], -params_ref[0:1, states:])
    ends_re, ends_im, hold = local_ends(plan, state_grad_ref, masks_ref.at[1], back_rate, True)
    back_ends_ref[...] = jnp.concatenate([ends_re, ends_im], axis=1)
    back_hold_ref[...] = hold
    _, leaving = chunk_entries(plan, ends_re, ends_im, hold, back_rate, None, True)
    back_ref[...] = jnp.broadcast_to(leaving, back_ref.shape)


def weight_kernel(
    plan, me_ref, act_ref, unit_grad_ref, lru_grad_ref, low_ref, keep_ref, send_ref, full_ref, out_ref
):
    states, features, units = plan.states, plan.features, plan.units
    pair = 2 * plan.own_states
    sign = jnp.where(grid_index((1, 2 * states), 1) < states, 1.0, -1.0)
    full_ref[...] = dot(act_ref[...], unit_grad_ref[...], 0, 0)
    out_grad = dot(lru_grad_ref[...], low_ref[...], 0, 0) * sign
    out_ref[...] = dot(out_grad.astype(BF16), regroup_matrix(states, plan.tensor), 1, 1)
    targets = [
        (0, pair, out_ref, 0),
        (pair, units, full_ref, 0),
        (pair + units, units, full_ref, features),
    ]
    for order, base, rows, first in half_blocks(plan, plan.down_crossed, plan.down):
        distribute(plan, me_ref[0], order, (keep_ref, send_ref), base, rows, first, targets)


def leave_kernel(
    plan, me_ref, x_ref, stats_ref, normed_ref, source_ref, ends_ref, hold_ref, carry_ref, hidden_ref,
    state_grad_ref, lru_grad_ref, input_map_ref, vec_ref, params_ref, masks_ref, sums_ref,
    keep_ref, send_ref, normed_grad_ref, out_sums_ref,
    drive_grad_ref, low_ref, full_ref,
):
    states, features = plan.states, plan.features
    params = params_ref[...]
    rate = (params[0:1, :states], params[0:1, states:])
    gamma, speed = params[1:2, :states], params[1:2, states:]
    modulus, rest = params[2:3, :states], params[2:3, states:]
    rotation = params[3:4, :states]
    back_rate = (rate[0], -rate[1])
    start = (carry_ref[0:1, :states], carry_ref[0:1, states:])
    entries, _ = chunk_entries(
        plan, ends_ref[:, :states], ends_ref[:, states:], hold_ref[...], back_rate, start, True
    )
    zero = jnp.zeros((SIDE, states), F32)
    rate_re = jnp.broadcast_to(back_rate[0], zero.shape)
    rate_im = jnp.broadcast_to(back_rate[1], zero.shape)
    gamma_wide = jnp.broadcast_to(gamma, zero.shape)

    def visit(tile, at, keep, state, sums):
        now_re, now_im = state
        held = wide(keep, states)
        next_re, next_im = held * now_re, held * now_im
        hidden_re, hidden_im = hidden_ref[at, :states], hidden_ref[at, states:]
        now_re = (state_grad_ref[at, :states] + rate_re * next_re) - rate_im * next_im
        now_im = (state_grad_ref[at, states:] + rate_re * next_im) + rate_im * next_re
        sums = (
            sums[0] + (hidden_re * next_re + hidden_im * next_im),
            sums[1] + (hidden_re * next_im - hidden_im * next_re),
            sums[2] + (source_ref[at, :states] * now_re + source_ref[at, states:] * now_im),
        )
        scale = gamma_wide * wide(masks_ref[2, at, :], states)
        drive_grad_ref[at, :states] = scale * now_re
        drive_grad_ref[at, states:] = scale * now_im
        return (now_re, now_im), sums

    _, sums = scan_pass(plan, masks_ref.at[1], entries, (zero, zero, zero), True, visit)
    rate_sum_re, rate_sum_im, gamma_sum = (jnp.sum(part, axis=0, keepdims=True) for part in sums)
    nu_grad = speed * (
        gamma_sum * modulus * modulus / rest - (rate_sum_re * rate[0] + rate_sum_im * rate[1])
    )
    theta_grad = rotation * (rate_sum_im * rate[0] - rate_sum_re * rate[1])
    vectors = read_vectors(vec_ref)
    skip = vectors[2:3]
    gain_sum = jnp.zeros((8, features), F32)
    turn = turn_matrix().astype(BF16)

    def rows_step(index, sums):
        gain_sum, shift_sum = sums
        at = plan.tile_rows(index)
        low = dot(turn, drive_grad_ref[at, :].astype(BF16)).astype(BF16)
        low_ref[at, :] = low
        normed_grad = dot(low, input_map_ref[...], 1, 1) + skip * lru_grad_ref[at, :].astype(F32)
        normed_grad_ref[at, :] = normed_grad
        standard, _ = standard_rows(plan, x_ref, stats_ref, at)
        return gain_sum + fold_rows(normed_grad * standard), shift_sum + fold_rows(normed_grad)

    gain_sum, shift_sum = lax.fori_loop(0, plan.tiles, rows_step, (gain_sum, gain_sum))
    into = dot(normed_ref[...], low_ref[...], 0, 0)
    full_ref[...] = dot(into.astype(BF16), regroup_matrix(states, plan.tensor), 1, 1)
    distribute(
        plan, me_ref[0], plan.down, (keep_ref, send_ref), 0, plan.own_rows, 0,
        [(0, 2 * plan.own_states, full_ref, 0)],
    )
    empty = jnp.zeros((1, features - states), F32)
    vector_sums = jnp.concatenate(
        [jnp.sum(part, axis=0, keepdims=True) for part in (gain_sum, shift_sum)]
        + [
            jnp.sum(sums_ref[8 * place : 8 * place + 8, :], axis=0, keepdims=True)
            for place in range(3)
        ]
        + [jnp.concatenate([part, empty], axis=1) for part in (nu_grad, theta_grad, gamma_sum)],
        axis=0,
    )
    base = plan.own_rows * plan.count // 2
    parts = features // LANES
    for part in range(parts):
        piece = vector_sums[:, part * LANES : (part + 1) * LANES]
        out_sums_ref[8 * part : 8 * part + 8, :] = piece
        high = piece.astype(BF16)
        low = (piece - high.astype(F32)).astype(BF16)
        send_ref[base + 8 * part : base + 8 * part + 8, :] = high
        send_ref[base + 8 * (parts + part) : base + 8 * (parts + part) + 8, :] = low


def last_kernel(plan, me_ref, *refs):
    b_keep, b_other, w_keep, w_other, summed_ref, tail_ref = refs[:6]
    outs, held, sems = refs[6:20], refs[20:34], refs[34]
    own, units = plan.own_states, plan.units
    b_mine = b_keep[...].astype(F32) + b_other[...].astype(F32)
    w_mine = w_keep[...].astype(F32) + w_other[...].astype(F32)
    half = summed_ref.shape[0]
    tail = tail_ref[...].astype(F32)
    vectors = summed_ref[...] + (tail[:half] + tail[half:])
    count = half // 8
    vectors = jnp.concatenate([vectors[8 * part : 8 * part + 8] for part in range(count)], axis=1)
    band = me_ref[0] >> log2(plan.tensor)
    at = grid_index((plan.features, LANES), 0)
    lane = grid_index((plan.features, LANES), 1)

    def pick(length):
        chosen = jnp.where(at == band * length + lane, 1.0, 0.0)
        return lax.dot_general(
            vectors,
            chosen,
            (((1,), (0,)), ((), ())),
            precision=lax.Precision.HIGHEST,
            preferred_element_type=F32,
        )

    long, short = plan.own_rows, plan.states // plan.fsdp
    long_part, short_part = pick(long), pick(short)
    held[0][...] = b_mine[:, :own]
    held[1][...] = b_mine[:, own:]
    held[2][...] = w_mine[:, :own]
    held[3][...] = w_mine[:, own : 2 * own]
    held[4][...] = w_mine[:, 2 * own : 2 * own + units]
    held[5][...] = w_mine[:, 2 * own + units :]
    for place in range(8):
        part, length = (long_part, long) if place < 5 else (short_part, short)
        held[6 + place][...] = part[place : place + 1, :length]
    for copy in start_copies(list(zip(held, outs)), sems):
        copy.wait()


def input_kernel(plan, me_ref, x_ref, stats_ref, grad_ref, normed_grad_ref, vec_ref, input_grad_ref):
    gain = read_vectors(vec_ref)[0:1]

    def rows_step(index, _):
        at = plan.tile_rows(index)
        standard, inverse = standard_rows(plan, x_ref, stats_ref, at)
        scaled = normed_grad_ref[at, :] * gain
        input_grad_ref[at, :] = grad_ref[at, :].astype(F32) + inverse * (
            scaled
            - jnp.mean(scaled, axis=1, keepdims=True)
            - standard * jnp.mean(scaled * standard, axis=1, keepdims=True)
        )
        return 0

    lax.fori_loop(0, plan.tiles, rows_step, 0)


def call(kernel, plan, outs, scratch, limit, time, *args, far_in=0, far_out=False):
    whole = pl.BlockSpec(memory_space=pltpu.VMEM)
    far = pl.BlockSpec(memory_space=pltpu.HBM)
    return pl.pallas_call(
        functools.partial(kernel, plan),
        out_shape=outs,
        in_specs=[pl.BlockSpec(memory_space=pltpu.SMEM)]
        + [far] * far_in
        + [whole] * (len(args) - 1 - far_in),
        out_specs=[far if far_out else whole] * len(outs),
        scratch_shapes=scratch,
        compiler_params=pltpu.CompilerParams(vmem_limit_bytes=limit * MIB),
        cost_estimate=pl.CostEstimate(
            flops=int(time * 1e9), bytes_accessed=int(time * 3.5e6), transcendentals=0
        ),
    )(*args)


def shape(dims, dtype=F32):
    return jax.ShapeDtypeStruct(dims, dtype)


def after(value, *others):
    return lax.optimization_barrier((value, *others))[0]


def joined(*parts):
    return jnp.concatenate(parts, axis=0)


def gather_blocks(plan, first, summed, second, cover):
    count = plan.count
    other = None
    for bit in plan.outer:
        second = joined(second, flip(second if other is None else after(second, other), bit, count))
        rows = first.shape[0]
        got = flip(joined(first, summed), bit, count)
        if other is None:
            got = after(got, cover)
        other = got
        summed = summed + other[rows:]
        first = joined(first, other[:rows])
    blocks = second.reshape(-1, plan.own_rows, second.shape[1])
    size = plan.own_rows // plan.halves
    halves = [
        after(blocks[:, half * size : half * size + size].reshape(-1, second.shape[1]), other)
        for half in range(plan.halves)
    ]
    halves = [joined(part, flip(part, bit, count)) for part, bit in zip(halves, (2, 1))]
    if plan.tensor <= 4:
        rows = first.shape[0]
        other = flip(joined(first, summed), 2, count)
        summed = summed + other[rows:]
        other = other[:rows]
    else:
        other = flip(first, 2, count)
    first = joined(first, other)
    other = flip(first, 1, count)
    halves = [
        (part, flip(after(part, other), bit, count)) for part, bit in zip(halves, (1, 2))
    ]
    first = joined(first, other)
    return first, flip(first, 0, count), summed, halves


def split_high_low(value):
    high = value.astype(BF16)
    return jnp.concatenate([high, (value - high.astype(F32)).astype(BF16)], axis=0)


def cut(value):
    count = value.shape[0] // 2
    return value[:count].astype(BF16), value[count:].astype(BF16)


def added(keep, other):
    return keep.astype(F32) + other.astype(F32)


def scatter_summed(plan, keep, send, summed, bit):
    other = flip(send, bit, plan.count)
    count, rows = keep.shape[0], summed.shape[0]
    tail = other[count:].astype(F32)
    summed = summed + (tail[:rows] + tail[rows:])
    keep, send = cut(added(keep, other[:count]))
    return keep, joined(send, split_high_low(summed)), summed, other


def scatter_halves(plan, keeps, sends, bits):
    others = [flip(send, bit, plan.count) for send, bit in zip(sends, bits)]
    pairs = [cut(added(keep, other)) for keep, other in zip(keeps, others)]
    return [pair[0] for pair in pairs], [pair[1] for pair in pairs], others


def shards(
    mesh,
    block_input,
    segments,
    ln_gain,
    ln_bias,
    b_real,
    b_imag,
    c_real,
    c_imag,
    nu_log,
    theta_log,
    gamma_log,
    d_skip,
    w_value,
    w_gate,
    b_value,
    b_gate,
    out_grad,
):
    band = lax.axis_index("fsdp")
    shard = lax.axis_index("tensor")
    rows, features = block_input.shape
    own = b_real.shape[1]
    plan = Plan(
        mesh, rows, segments.shape[0], features, own * mesh.shape["tensor"], w_value.shape[1]
    )
    states, units, chunks = plan.states, plan.units, plan.chunks
    me = (band * plan.tensor + shard).astype(jnp.int32).reshape(1)
    long, short = plan.own_rows, states // plan.fsdp
    vector_rows = 8 * features // LANES
    matrices = (b_real, b_imag, c_real, c_imag, w_value, w_gate)
    lines = [
        v.reshape(1, -1)
        for v in (ln_gain, ln_bias, d_skip, b_value, b_gate, nu_log, theta_log, gamma_log)
    ]
    block = 2 * own + 2 * units
    first, second = call(
        pack_kernel,
        plan,
        [shape((long + vector_rows, 2 * own), BF16), shape((long, block), BF16)],
        [pltpu.VMEM(v.shape, BF16) for v in (*matrices, *lines)] + [pltpu.SemaphoreType.DMA((14,))],
        60,
        1.5,
        me, *matrices, *lines,
        far_in=14,
    )
    stats, masks = call(
        token_kernel,
        plan,
        [shape((2, rows, LANES)), shape((4, rows, LANES))],
        [pltpu.VMEM((3, plan.group_rows // LANES, LANES), F32)],
        8,
        2,
        me, block_input, segments.reshape(-1, LANES),
    )
    b0, b1, vectors, halves = gather_blocks(plan, first[:long], first[long:], second, masks)

    pack_type = BF16 if long % 16 == 0 else F32
    full = (rows, 2 * states)
    normed, source, ends, hold, carry, input_map, params = call(
        enter_kernel,
        plan,
        [
            shape((rows, features), BF16),
            shape(full),
            shape((chunks, 2 * states)),
            shape((chunks, LANES)),
            shape((8, 2 * states)),
            shape((features, 2 * states), BF16),
            shape((8, 2 * states)),
        ],
        [pltpu.VMEM((features, 2 * states), pack_type)],
        8,
        3,
        me, block_input, stats, b0, b1, vectors, masks,
    )

    def pass_on(value, forward):
        pairs = []
        for one in range(0, plan.tensor, 2):
            pairs.append((one, one + 1) if forward else (one + 1, one))
        return lax.ppermute(value, "tensor", pairs)

    g0 = joined(*(joined(part, after(got, carry)) for part, got in halves))
    g1 = flip(g0, 0, plan.count)
    carry = pass_on(carry, True) if plan.pieces == 2 else jnp.zeros_like(carry)
    (
        mixed, hidden, lru_grad, state_grad, act, unit_grad, low, sums,
    ) = call(
        middle_kernel,
        plan,
        [
            shape((rows, features), BF16),
            shape(full),
            shape((rows, features), BF16),
            shape(full),
            shape((rows, features), BF16),
            shape((rows, 2 * features), BF16),
            shape(full, BF16),
            shape((24, features)),
        ],
        [
            pltpu.VMEM((features, 2 * states), pack_type),
            pltpu.VMEM((features, 2 * features), pack_type),
            pltpu.VMEM((features, 2 * states), BF16),
        ],
        14,
        10,
        me, block_input, out_grad, normed, source, ends, hold, carry, g0, g1, vectors, params, masks,
    )
    half_rows = plan.count // 2 * long
    w_keep, w_send = call(
        weight_kernel,
        plan,
        [shape((half_rows, block), BF16)] * 2,
        [
            pltpu.VMEM((features, 2 * features), F32),
            pltpu.VMEM((features, 2 * states), F32),
        ],
        10,
        2.5,
        me, act, unit_grad, lru_grad, low,
    )
    w_other = flip(w_send, 0, plan.count)
    back_ends, back_hold, back = call(
        back_kernel,
        plan,
        [shape((chunks, 2 * states)), shape((chunks, LANES)), shape((8, 2 * states))],
        [],
        8,
        1.5,
        me, after(state_grad, w_send), params, masks,
    )
    back = pass_on(back, False) if plan.pieces == 2 else jnp.zeros_like(back)
    pieces = plan.halves
    w_other = after(w_other, back_ends)
    w_total = added(w_keep, w_other)
    size = w_total.shape[0] // pieces
    halves = [cut(w_total[half * size : half * size + size]) for half in range(pieces)]
    w_keeps = [half[0] for half in halves]
    w_others = [flip(half[1], bit, plan.count) for half, bit in zip(halves, (2, 1))]
    back_ends = after(back_ends, w_other)
    b_keep, b_send, normed_grad, summed = call(
        leave_kernel,
        plan,
        [
            shape((half_rows, 2 * own), BF16),
            shape((half_rows + 2 * vector_rows, 2 * own), BF16),
            shape((rows, features)),
            shape((vector_rows, LANES)),
        ],
        [
            pltpu.VMEM(full, F32),
            pltpu.VMEM(full, BF16),
            pltpu.VMEM((features, 2 * states), F32),
        ],
        14,
        4.5,
        me, block_input, stats, normed, source, back_ends, back_hold, back, hidden,
        state_grad, lru_grad, input_map, vectors, params, masks, sums,
    )
    b_send = after(b_send, *w_others)
    w_others = [after(other, summed) for other in w_others]
    halves = [cut(added(keep, other)) for keep, other in zip(w_keeps, w_others)]
    w_keeps, w_sends = [half[0] for half in halves], [half[1] for half in halves]
    b_keep, b_send, summed, b_other = scatter_summed(plan, b_keep, b_send, summed, 0)
    w_keeps, w_sends, w_others = scatter_halves(plan, w_keeps, w_sends, (1, 2))
    b_keep, b_send, summed, b_next = scatter_summed(plan, b_keep, b_send, summed, 1)
    waited = w_others
    width = block
    w_keep, w_send = joined(*w_keeps), joined(*w_sends)
    for place, bit in enumerate([2, *plan.outer[::-1]]):
        last = bit == plan.bits - 1
        if not last:
            w_send = after(w_send, b_other)
            b_other = b_next
            w_next = flip(w_send, bit + 1, plan.count)
            if bit + 1 < plan.bits - 1:
                total = added(w_keep, w_next).reshape(pieces, -1, width)
                size = total.shape[1] // 2
                w_keep = total[:, :size].reshape(-1, width).astype(BF16)
                w_send = total[:, size:].reshape(-1, width).astype(BF16)
            else:
                w_other = w_next
        b_send = after(b_send, *waited)
        if last:
            got = flip(b_send, bit, plan.count)
            b_other, tail = got[: b_keep.shape[0]], got[b_keep.shape[0] :]
        else:
            b_keep, b_send, summed, b_next = scatter_summed(plan, b_keep, b_send, summed, bit)
        waited = [w_next]
    (input_grad,) = call(
        input_kernel,
        plan,
        [shape((rows, features))],
        [],
        8,
        2.5,
        me, block_input, stats, out_grad, normed_grad, vectors,
    )
    small = (
        [(long, own)] * 4 + [(long, units)] * 2 + [(1, long)] * 5 + [(1, short)] * 3
    )
    (
        b_real_grad, b_imag_grad, c_real_grad, c_imag_grad, value_grad, gate_grad, *lines
    ) = call(
        last_kernel,
        plan,
        [shape(dims) for dims in small],
        [pltpu.VMEM(dims, F32) for dims in small] + [pltpu.SemaphoreType.DMA((14,))],
        4,
        2,
        me, b_keep, b_other, w_keep, w_other, summed, tail,
        far_out=True,
    )
    gain_grad, bias_grad, skip_grad, value_line, gate_line, nu_grad, theta_grad, gamma_grad = (
        line.reshape(-1) for line in lines
    )
    return (
        mixed,
        input_grad,
        gain_grad,
        bias_grad,
        b_real_grad,
        b_imag_grad,
        c_real_grad,
        c_imag_grad,
        nu_grad,
        theta_grad,
        gamma_grad,
        skip_grad,
        value_grad,
        gate_grad,
        value_line,
        gate_line,
    )


def solution(mesh):
    in_specs = (
        P(("fsdp", "tensor"), None),
        P("fsdp"),
        P("fsdp"),
        P("fsdp"),
        P("fsdp", "tensor"),
        P("fsdp", "tensor"),
        P("fsdp", "tensor"),
        P("fsdp", "tensor"),
        P("fsdp"),
        P("fsdp"),
        P("fsdp"),
        P("fsdp"),
        P("fsdp", "tensor"),
        P("fsdp", "tensor"),
        P("fsdp"),
        P("fsdp"),
        P(("fsdp", "tensor"), None),
    )
    out_specs = (
        P(("fsdp", "tensor"), None),
        P(("fsdp", "tensor"), None),
        P("fsdp"),
        P("fsdp"),
        P("fsdp", "tensor"),
        P("fsdp", "tensor"),
        P("fsdp", "tensor"),
        P("fsdp", "tensor"),
        P("fsdp"),
        P("fsdp"),
        P("fsdp"),
        P("fsdp"),
        P("fsdp", "tensor"),
        P("fsdp", "tensor"),
        P("fsdp"),
        P("fsdp"),
    )
    return jax.shard_map(
        functools.partial(shards, mesh),
        mesh=mesh,
        in_specs=in_specs,
        out_specs=out_specs,
        check_vma=False,
    )
```

```python
import functools
import math

import jax
import jax.numpy as jnp
from jax import lax
from jax.experimental import pallas as pl
from jax.experimental.pallas import tpu as pltpu
from jax.sharding import PartitionSpec as P

SEQ_LEN = 2048
LANES = 128
TILE = 256
SIDE = 16
BLOCK = 1024
AXES = ("fsdp", "tensor")
norm_epsilon = 1e-05
GELU_SCALE = math.sqrt(2.0 / math.pi)
GELU_CUBE = 0.044715
F32 = jnp.float32
BF16 = jnp.bfloat16
MIB = 1024 * 1024


def log2(value):
    return value.bit_length() - 1


def flip(value, bit, count):
    return lax.ppermute(value, AXES, [(i, i ^ (1 << bit)) for i in range(count)])


def dot(left, right, left_dim=1, right_dim=0):
    return lax.dot_general(
        left, right, (((left_dim,), (right_dim,)), ((), ())), preferred_element_type=F32
    )


def fold_rows(value):
    rows, width = value.shape
    return jnp.sum(value.reshape(rows // 8, 8, width), axis=0)


def wide(mask, width):
    return jnp.concatenate([mask] * (width // LANES), axis=1)


def grid_index(dims, axis):
    return lax.broadcasted_iota(jnp.int32, dims, axis)


def regroup_matrix(states, shards):
    own = log2(states // shards)
    width = 2 * states
    source = grid_index((width, width), 0)
    target = grid_index((width, width), 1)
    part = (source >> own) & 1
    place = part * states + ((source >> (own + 1)) << own) + (source & ((1 << own) - 1))
    return jnp.where(place == target, 1.0, 0.0).astype(BF16)


def turn_matrix():
    source = grid_index((TILE, TILE), 0)
    target = grid_index((TILE, TILE), 1)
    bits = log2(SIDE)
    place = ((source & (SIDE - 1)) << bits) + (source >> bits)
    return jnp.where(place == target, 1.0, 0.0)


def turn_rows(turn, value):
    parts = [dot(turn, value[at : at + TILE]) for at in range(0, value.shape[0], TILE)]
    return jnp.concatenate(parts, axis=0).astype(BF16)


class Plan:
    def __init__(self, mesh, rows, group_rows, features, states, units):
        self.fsdp = mesh.shape["fsdp"]
        self.tensor = mesh.shape["tensor"]
        self.count = self.fsdp * self.tensor
        self.bits = log2(self.count)
        far = list(range(self.bits - 1, 3, -1))
        self.far = far
        self.up = [*far, 3, 2, 1, 0]
        self.up_crossed = ([*far, 1, 3, 2, 0], [*far, 1, 2, 3, 0])
        self.down = [0, 1, 2, 3, *far[::-1]]
        self.down_crossed = ([0, 2, 3, 1, *far[::-1]], [0, 3, 2, 1, *far[::-1]])
        self.halves = 2 if features // self.fsdp >= 32 else 1
        self.rows = rows
        self.group_rows = group_rows
        self.features = features
        self.states = states
        self.units = units
        self.own_states = states // self.tensor
        self.own_rows = features // self.fsdp
        self.pieces = SEQ_LEN // rows
        self.tiles = rows // TILE
        self.chunks = self.tiles * SIDE
        self.block = BLOCK if rows % BLOCK == 0 else TILE
        self.blocks = rows // self.block

    def slot_owner(self, slot, me, order):
        owner = me
        for place, bit in enumerate(order):
            owner = owner ^ (((slot >> (self.bits - 1 - place)) & 1) << bit)
        shift = log2(self.tensor)
        return owner >> shift, owner & (self.tensor - 1)

    def block_rows(self, index):
        return pl.ds(pl.multiple_of(index * self.block, self.block), self.block)


def step_rows(tile, place):
    return pl.ds(pl.multiple_of(tile * TILE + place * SIDE, SIDE), SIDE)


def scan_pass(plan, keep_ref, start, extra, reverse, visit):
    def step(index, carried):
        now, extra = carried
        place = SIDE - 1 - index if reverse else index
        after = []
        for tile in range(plan.tiles):
            at = step_rows(tile, place)
            state, extra = visit(tile, at, keep_ref[at, :], now[tile], extra)
            after.append(state)
        return after, extra

    return lax.fori_loop(0, SIDE, step, (start, extra), unroll=2)


def local_ends(plan, source_ref, keep_ref, rate, reverse):
    states = plan.states
    zero = jnp.zeros((SIDE, states), F32)
    rate_re = jnp.broadcast_to(rate[0], zero.shape)
    rate_im = jnp.broadcast_to(rate[1], zero.shape)
    one = jnp.ones((SIDE, LANES), F32)

    def visit(tile, at, keep, state, extra):
        now_re, now_im, hold = state
        held = wide(keep, states)
        pass_re, pass_im = held * rate_re, held * rate_im
        source = source_ref[at, :]
        next_re = (source[:, :states] + pass_re * now_re) - pass_im * now_im
        next_im = (source[:, states:] + pass_re * now_im) + pass_im * now_re
        return (next_re, next_im, hold * keep), extra

    ends, _ = scan_pass(plan, keep_ref, [(zero, zero, one)] * plan.tiles, 0, reverse, visit)
    return tuple(jnp.concatenate([end[part] for end in ends], axis=0) for part in range(3))


def shifted(value, distance, reverse):
    count = value.shape[0]
    row = grid_index(value.shape, 0)
    if reverse:
        moved = pltpu.roll(value, count - distance, 0)
        return jnp.where(row < count - distance, moved, 0.0)
    moved = pltpu.roll(value, distance, 0)
    return jnp.where(row >= distance, moved, 0.0)


def chunk_entries(plan, ends_re, ends_im, hold, rate, start, reverse):
    states, count = plan.states, plan.chunks
    power_re, power_im = rate
    for _ in range(log2(SIDE)):
        power_re, power_im = power_re * power_re - power_im * power_im, 2.0 * power_re * power_im
    first = count - 1 if reverse else 0
    if start is not None:
        at_first = grid_index((count, states), 0) == first
        held = jnp.where(at_first, wide(hold, states), 0.0)
        pass_re, pass_im = held * power_re, held * power_im
        ends_re = ends_re + (pass_re * start[0] - pass_im * start[1])
        ends_im = ends_im + (pass_re * start[1] + pass_im * start[0])
    distance = 1
    while distance < count:
        earlier_re = shifted(ends_re, distance, reverse)
        earlier_im = shifted(ends_im, distance, reverse)
        held = wide(hold, states)
        pass_re, pass_im = held * power_re, held * power_im
        ends_re = ends_re + (pass_re * earlier_re - pass_im * earlier_im)
        ends_im = ends_im + (pass_re * earlier_im + pass_im * earlier_re)
        hold = hold * shifted(hold, distance, reverse)
        power_re, power_im = power_re * power_re - power_im * power_im, 2.0 * power_re * power_im
        distance *= 2
    last = slice(0, 1) if reverse else slice(count - 1, count)
    leaving = jnp.concatenate([ends_re[last], ends_im[last]], axis=1)
    if start is None:
        return None, leaving
    entry_re = shifted(ends_re, 1, reverse) + jnp.where(at_first, start[0], 0.0)
    entry_im = shifted(ends_im, 1, reverse) + jnp.where(at_first, start[1], 0.0)
    entries = []
    for tile in range(plan.tiles):
        at = slice(tile * SIDE, (tile + 1) * SIDE)
        entries.append((entry_re[at], entry_im[at]))
    return entries, leaving


def block_places(plan, me, order, refs, base, rows, start):
    slot = 0
    for ref in refs:
        for place in range(plan.count // 2):
            band, shard = plan.slot_owner(slot, me, order)
            slot += 1
            first = pl.multiple_of(band * plan.own_rows + start, rows)
            yield ref, base + place * rows, pl.ds(first, rows), shard


def collect(plan, me, order, refs, base, rows, start, targets):
    for ref, row, at, shard in block_places(plan, me, order, refs, base, rows, start):
        for first, width, out_ref, lanes in targets:
            column = pl.multiple_of(lanes + shard * width, LANES)
            out_ref[at, pl.ds(column, width)] = ref[row : row + rows, first : first + width].astype(
                out_ref.dtype
            )


def distribute(plan, me, order, refs, base, rows, start, targets):
    for ref, row, at, shard in block_places(plan, me, order, refs, base, rows, start):
        for first, width, full_ref, lanes in targets:
            column = pl.multiple_of(lanes + shard * width, LANES)
            ref[row : row + rows, first : first + width] = full_ref[at, pl.ds(column, width)].astype(
                ref.dtype
            )


def half_blocks(plan, orders):
    rows = plan.own_rows // plan.halves
    for half in range(plan.halves):
        yield orders[half], half * plan.count // 2 * rows, rows, half * rows


def start_copies(pairs, sems):
    copies = [
        pltpu.make_async_copy(source, target, sems.at[place])
        for place, (source, target) in enumerate(pairs)
    ]
    for copy in copies:
        copy.start()
    return copies


def pack_kernel(plan, me_ref, *refs):
    sources, outs, held, sems = refs[:14], refs[14:16], refs[16:30], refs[30]
    copies = start_copies(list(zip(sources, held)), sems)
    first_ref, second_ref = outs
    band = me_ref[0] >> log2(plan.tensor)
    rows, features = plan.own_rows, plan.features
    for copy in copies:
        copy.wait()
    first_ref[:rows, :] = jnp.concatenate([held[0][...], held[1][...]], axis=1)
    second_ref[...] = jnp.concatenate([ref[...] for ref in held[2:6]], axis=1)
    placed = []
    lane = grid_index((1, features), 1)
    for ref in held[6:]:
        length = ref.shape[1]
        value = ref[...].astype(F32)
        value = jnp.concatenate([value] * (features // length), axis=1)
        placed.append(jnp.where((lane >> log2(length)) == band, value, 0.0))
    placed = jnp.concatenate(placed, axis=0).astype(BF16)
    for part in range(features // LANES):
        first_ref[rows + 8 * part : rows + 8 * part + 8, :] = placed[
            :, part * LANES : (part + 1) * LANES
        ]


def token_kernel(plan, me_ref, x_ref, segments_ref, stats_ref, masks_ref, flags_ref):
    shard = me_ref[0] & (plan.tensor - 1)
    ids = segments_ref[...]
    count = ids.shape[0]
    lane = grid_index(ids.shape, 1)
    position = (grid_index(ids.shape, 0) * LANES + lane) & (SEQ_LEN - 1)
    turned = pltpu.roll(ids, 1, 1)
    before = jnp.where(lane == 0, pltpu.roll(turned, 1, 0), turned)
    turned = pltpu.roll(ids, LANES - 1, 1)
    after = jnp.where(lane == LANES - 1, pltpu.roll(turned, count - 1, 0), turned)
    flags_ref[0] = jnp.where((position > 0) & (ids == before), 1.0, 0.0)
    flags_ref[1] = jnp.where((position < SEQ_LEN - 1) & (ids == after), 1.0, 0.0)
    flags_ref[2] = jnp.where(ids > 0, 1.0, 0.0)
    turn = turn_matrix()
    plain = jnp.where(grid_index((TILE, TILE), 0) == grid_index((TILE, TILE), 1), 1.0, 0.0)
    ones = jnp.ones((TILE, LANES), BF16)
    per_tile = TILE // LANES
    own = plan.rows // LANES
    flags = [flags_ref[kind, pl.ds(pl.multiple_of(shard * own, own), own), :] for kind in range(3)]
    for tile in range(plan.tiles):
        at = slice(tile * TILE, (tile + 1) * TILE)
        for kind in range(4):
            rows = flags[min(kind, 2)][tile * per_tile : (tile + 1) * per_tile, :]
            line = jnp.concatenate([rows[part : part + 1, :] for part in range(per_tile)], axis=1)
            spread = (plain if kind == 3 else turn) * line
            masks_ref[kind, at, :] = dot(spread.astype(BF16), ones)

    def rows_step(index, _):
        at = plan.block_rows(index)
        values = x_ref[at, :].astype(F32)
        mean = jnp.mean(values, axis=1, keepdims=True)
        centred = values - mean
        inverse = lax.rsqrt(jnp.mean(centred * centred, axis=1, keepdims=True) + norm_epsilon)
        stats_ref[0, at, :] = jnp.broadcast_to(mean, (plan.block, LANES))
        stats_ref[1, at, :] = jnp.broadcast_to(inverse, (plan.block, LANES))
        return 0

    lax.fori_loop(0, plan.blocks, rows_step, 0)


def standard_rows(plan, x_ref, stats_ref, at):
    mean = wide(stats_ref[0, at, :], plan.features)
    inverse = wide(stats_ref[1, at, :], plan.features)
    return (x_ref[at, :].astype(F32) - mean) * inverse, inverse


def read_vectors(vec_ref):
    count = vec_ref.shape[0] // 8
    parts = [vec_ref[8 * part : 8 * part + 8, :].astype(F32) for part in range(count)]
    return jnp.concatenate(parts, axis=1)


def enter_kernel(
    plan, me_ref, x_ref, stats_ref, b0_ref, b1_ref, vec_ref, masks_ref,
    normed_ref, source_ref, ends_ref, hold_ref, carry_ref, input_map_ref, params_ref,
    pack_ref,
):
    states = plan.states
    collect(
        plan, me_ref[0], plan.up[::-1], (b0_ref, b1_ref), 0, plan.own_rows, 0,
        [(0, 2 * plan.own_states, pack_ref, 0)],
    )
    input_map_ref[...] = dot(
        pack_ref[...].astype(BF16), regroup_matrix(states, plan.tensor)
    ).astype(BF16)
    vectors = read_vectors(vec_ref)
    gain, shift = vectors[0:1], vectors[1:2]
    speed = jnp.exp(vectors[5:6, :states])
    modulus = jnp.exp(-speed)
    rotation = jnp.exp(vectors[6:7, :states])
    rate = (modulus * jnp.cos(rotation), modulus * jnp.sin(rotation))
    rest = 1.0 - modulus * modulus
    gamma = jnp.exp(vectors[7:8, :states]) * jnp.sqrt(rest)
    params_ref[...] = jnp.concatenate(
        [
            jnp.concatenate(rate, axis=1),
            jnp.concatenate([gamma, speed], axis=1),
            jnp.concatenate([modulus, rest], axis=1),
            jnp.concatenate([rotation, rotation], axis=1),
            jnp.zeros((4, 2 * states), F32),
        ],
        axis=0,
    )
    gamma_pair = jnp.concatenate([gamma, gamma], axis=1)
    turn = turn_matrix().astype(BF16)

    def rows_step(index, _):
        at = plan.block_rows(index)
        standard, _ = standard_rows(plan, x_ref, stats_ref, at)
        normed = (standard * gain + shift).astype(BF16)
        normed_ref[at, :] = normed
        turned = turn_rows(turn, normed)
        drive = dot(turned, input_map_ref[...])
        source_ref[at, :] = drive * gamma_pair * wide(masks_ref[2, at, :], 2 * states)
        return 0

    lax.fori_loop(0, plan.blocks, rows_step, 0)
    ends_re, ends_im, hold = local_ends(plan, source_ref, masks_ref.at[0], rate, False)
    ends_ref[...] = jnp.concatenate([ends_re, ends_im], axis=1)
    hold_ref[...] = hold
    _, leaving = chunk_entries(plan, ends_re, ends_im, hold, rate, None, False)
    carry_ref[...] = jnp.broadcast_to(leaving, carry_ref.shape)


def middle_kernel(
    plan, me_ref, x_ref, grad_ref, normed_ref, source_ref, ends_ref, hold_ref, carry_ref,
    g0_ref, g1_ref, vec_ref, params_ref, masks_ref,
    mixed_ref, hidden_ref, lru_grad_ref, state_grad_ref, act_ref, unit_grad_ref, low_ref, sums_ref,
    pack_ref, wpack_ref, out_map_ref,
):
    states, features, units = plan.states, plan.features, plan.units
    pair = 2 * plan.own_states
    targets = [
        (0, pair, pack_ref, 0),
        (pair, units, wpack_ref, 0),
        (pair + units, units, wpack_ref, features),
    ]
    for order, base, rows, first in half_blocks(plan, plan.up_crossed):
        collect(plan, me_ref[0], order[::-1], (g0_ref, g1_ref), base, rows, first, targets)
    sign = jnp.where(grid_index((1, 2 * states), 1) < states, 1.0, -1.0)
    regroup = regroup_matrix(states, plan.tensor)
    out_map_ref[...] = (dot(pack_ref[...].astype(BF16), regroup) * sign).astype(BF16)
    rate = (params_ref[0:1, :states], params_ref[0:1, states:])
    start = (carry_ref[0:1, :states], carry_ref[0:1, states:])
    entries, _ = chunk_entries(
        plan, ends_ref[:, :states], ends_ref[:, states:], hold_ref[...], rate, start, False
    )
    rate_re = jnp.broadcast_to(rate[0], (SIDE, states))
    rate_im = jnp.broadcast_to(rate[1], (SIDE, states))

    def visit(tile, at, keep, state, extra):
        now_re, now_im = state
        held = wide(keep, states)
        pass_re, pass_im = held * rate_re, held * rate_im
        source = source_ref[at, :]
        next_re = (source[:, :states] + pass_re * now_re) - pass_im * now_im
        next_im = (source[:, states:] + pass_re * now_im) + pass_im * now_re
        hidden_ref[at, :states] = next_re
        hidden_ref[at, states:] = next_im
        return (next_re, next_im), extra

    scan_pass(plan, masks_ref.at[0], entries, 0, False, visit)
    vectors = read_vectors(vec_ref)
    skip = vectors[2:3]
    biases = jnp.concatenate([vectors[3:4], vectors[4:5]], axis=1)
    sums_ref[...] = jnp.zeros_like(sums_ref)
    turn = turn_matrix().astype(BF16)

    def rows_step(index, _):
        at = plan.block_rows(index)
        low = turn_rows(turn, hidden_ref[at, :].astype(BF16))
        low_ref[at, :] = low
        normed = normed_ref[at, :].astype(F32)
        lru = dot(low, out_map_ref[...], 1, 1) + skip * normed
        square = lru * lru
        bent = jnp.tanh(lru * (GELU_SCALE + (GELU_SCALE * GELU_CUBE) * square))
        half = 0.5 + 0.5 * bent
        act_wide = lru * half
        slope = half + act_wide * (1.0 - half) * (
            2.0 * GELU_SCALE + (6.0 * GELU_SCALE * GELU_CUBE) * square
        )
        act = act_wide.astype(BF16)
        act_ref[at, :] = act
        mapped = dot(act, wpack_ref[...].astype(BF16)) + biases
        value = mapped[:, :features]
        live_half = wide(0.5 * masks_ref[3, at, :], features)
        opening = live_half + live_half * jnp.tanh(0.5 * mapped[:, features:])
        gated = value * opening
        mixed_ref[at, :] = (x_ref[at, :].astype(F32) + gated).astype(BF16)
        value_grad = grad_ref[at, :].astype(F32) * opening
        gate_grad = value_grad * (value - gated)
        sums_ref[8:16, :] += fold_rows(value_grad)
        sums_ref[16:24, :] += fold_rows(gate_grad)
        unit_grad = jnp.concatenate([value_grad, gate_grad], axis=1).astype(BF16)
        unit_grad_ref[at, :] = unit_grad
        act_grad = dot(unit_grad, wpack_ref[...].astype(BF16), 1, 1)
        lru_grad = act_grad * slope
        sums_ref[0:8, :] += fold_rows(lru_grad * normed)
        lru_grad = lru_grad.astype(BF16)
        lru_grad_ref[at, :] = lru_grad
        turned = turn_rows(turn, lru_grad)
        state_grad_ref[at, :] = dot(turned, out_map_ref[...])
        return 0

    lax.fori_loop(0, plan.blocks, rows_step, 0)


def back_kernel(
    plan, me_ref, state_grad_ref, params_ref, masks_ref, back_ends_ref, back_hold_ref, back_ref
):
    states = plan.states
    back_rate = (params_ref[0:1, :states], -params_ref[0:1, states:])
    ends_re, ends_im, hold = local_ends(plan, state_grad_ref, masks_ref.at[1], back_rate, True)
    back_ends_ref[...] = jnp.concatenate([ends_re, ends_im], axis=1)
    back_hold_ref[...] = hold
    _, leaving = chunk_entries(plan, ends_re, ends_im, hold, back_rate, None, True)
    back_ref[...] = jnp.broadcast_to(leaving, back_ref.shape)


def weight_kernel(
    plan, me_ref, act_ref, unit_grad_ref, lru_grad_ref, low_ref, keep_ref, send_ref, full_ref, out_ref
):
    states, features, units = plan.states, plan.features, plan.units
    pair = 2 * plan.own_states
    sign = jnp.where(grid_index((1, 2 * states), 1) < states, 1.0, -1.0)
    full_ref[...] = dot(act_ref[...], unit_grad_ref[...], 0, 0)
    out_grad = dot(lru_grad_ref[...], low_ref[...], 0, 0) * sign
    out_ref[...] = dot(out_grad.astype(BF16), regroup_matrix(states, plan.tensor), 1, 1)
    targets = [
        (0, pair, out_ref, 0),
        (pair, units, full_ref, 0),
        (pair + units, units, full_ref, features),
    ]
    for order, base, rows, first in half_blocks(plan, plan.down_crossed):
        distribute(plan, me_ref[0], order, (keep_ref, send_ref), base, rows, first, targets)


def leave_kernel(
    plan, me_ref, x_ref, stats_ref, normed_ref, source_ref, ends_ref, hold_ref, carry_ref, hidden_ref,
    state_grad_ref, lru_grad_ref, input_map_ref, vec_ref, params_ref, masks_ref, sums_ref,
    keep_ref, send_ref, normed_grad_ref,
    drive_grad_ref, low_ref, full_ref,
):
    states, features = plan.states, plan.features
    params = params_ref[...]
    rate = (params[0:1, :states], params[0:1, states:])
    gamma, speed = params[1:2, :states], params[1:2, states:]
    modulus, rest = params[2:3, :states], params[2:3, states:]
    rotation = params[3:4, :states]
    back_rate = (rate[0], -rate[1])
    start = (carry_ref[0:1, :states], carry_ref[0:1, states:])
    entries, _ = chunk_entries(
        plan, ends_ref[:, :states], ends_ref[:, states:], hold_ref[...], back_rate, start, True
    )
    zero = jnp.zeros((SIDE, states), F32)
    rate_re = jnp.broadcast_to(back_rate[0], zero.shape)
    rate_im = jnp.broadcast_to(back_rate[1], zero.shape)
    gamma_wide = jnp.broadcast_to(gamma, zero.shape)

    def visit(tile, at, keep, state, sums):
        now_re, now_im = state
        held = wide(keep, states)
        next_re, next_im = held * now_re, held * now_im
        hidden_re, hidden_im = hidden_ref[at, :states], hidden_ref[at, states:]
        now_re = (state_grad_ref[at, :states] + rate_re * next_re) - rate_im * next_im
        now_im = (state_grad_ref[at, states:] + rate_re * next_im) + rate_im * next_re
        sums = (
            sums[0] + (hidden_re * next_re + hidden_im * next_im),
            sums[1] + (hidden_re * next_im - hidden_im * next_re),
            sums[2] + (source_ref[at, :states] * now_re + source_ref[at, states:] * now_im),
        )
        scale = gamma_wide * wide(masks_ref[2, at, :], states)
        drive_grad_ref[at, :states] = scale * now_re
        drive_grad_ref[at, states:] = scale * now_im
        return (now_re, now_im), sums

    _, sums = scan_pass(plan, masks_ref.at[1], entries, (zero, zero, zero), True, visit)
    rate_sum_re, rate_sum_im, gamma_sum = (jnp.sum(part, axis=0, keepdims=True) for part in sums)
    nu_grad = speed * (
        gamma_sum * modulus * modulus / rest - (rate_sum_re * rate[0] + rate_sum_im * rate[1])
    )
    theta_grad = rotation * (rate_sum_im * rate[0] - rate_sum_re * rate[1])
    vectors = read_vectors(vec_ref)
    skip = vectors[2:3]
    gain_sum = jnp.zeros((8, features), F32)
    turn = turn_matrix().astype(BF16)

    def rows_step(index, sums):
        gain_sum, shift_sum = sums
        at = plan.block_rows(index)
        low = turn_rows(turn, drive_grad_ref[at, :].astype(BF16))
        low_ref[at, :] = low
        normed_grad = dot(low, input_map_ref[...], 1, 1) + skip * lru_grad_ref[at, :].astype(F32)
        normed_grad_ref[at, :] = normed_grad
        standard, _ = standard_rows(plan, x_ref, stats_ref, at)
        return gain_sum + fold_rows(normed_grad * standard), shift_sum + fold_rows(normed_grad)

    gain_sum, shift_sum = lax.fori_loop(0, plan.blocks, rows_step, (gain_sum, gain_sum))
    into = dot(normed_ref[...], low_ref[...], 0, 0)
    full_ref[...] = dot(into.astype(BF16), regroup_matrix(states, plan.tensor), 1, 1)
    distribute(
        plan, me_ref[0], plan.down, (keep_ref, send_ref), 0, plan.own_rows, 0,
        [(0, 2 * plan.own_states, full_ref, 0)],
    )
    empty = jnp.zeros((1, features - states), F32)
    vector_sums = jnp.concatenate(
        [jnp.sum(part, axis=0, keepdims=True) for part in (gain_sum, shift_sum)]
        + [
            jnp.sum(sums_ref[8 * place : 8 * place + 8, :], axis=0, keepdims=True)
            for place in range(3)
        ]
        + [jnp.concatenate([part, empty], axis=1) for part in (nu_grad, theta_grad, gamma_sum)],
        axis=0,
    )
    base = plan.own_rows * plan.count // 2
    parts = features // LANES
    for part in range(parts):
        piece = vector_sums[:, part * LANES : (part + 1) * LANES]
        high = piece.astype(BF16)
        low = (piece - high.astype(F32)).astype(BF16)
        send_ref[base + 8 * part : base + 8 * part + 8, :] = high
        send_ref[base + 8 * (parts + part) : base + 8 * (parts + part) + 8, :] = low


def last_kernel(plan, me_ref, *refs):
    b_keep, b_other, w_keep, w_other, tail_ref = refs[:5]
    outs, held, sems = refs[5:19], refs[19:33], refs[33]
    own, units = plan.own_states, plan.units
    b_mine = b_keep[...].astype(F32) + b_other[...].astype(F32)
    w_mine = w_keep[...].astype(F32) + w_other[...].astype(F32)
    half = tail_ref.shape[0] // 4
    tail = [tail_ref[part * half : part * half + half, :].astype(F32) for part in range(4)]
    vectors = (tail[0] + tail[1]) + (tail[2] + tail[3])
    count = half // 8
    vectors = jnp.concatenate([vectors[8 * part : 8 * part + 8] for part in range(count)], axis=1)
    band = me_ref[0] >> log2(plan.tensor)
    at = grid_index((plan.features, LANES), 0)
    lane = grid_index((plan.features, LANES), 1)

    def pick(length):
        chosen = jnp.where(at == band * length + lane, 1.0, 0.0)
        return lax.dot_general(
            vectors,
            chosen,
            (((1,), (0,)), ((), ())),
            precision=lax.Precision.HIGHEST,
            preferred_element_type=F32,
        )

    long, short = plan.own_rows, plan.states // plan.fsdp
    long_part, short_part = pick(long), pick(short)
    held[0][...] = b_mine[:, :own]
    held[1][...] = b_mine[:, own:]
    held[2][...] = w_mine[:, :own]
    held[3][...] = w_mine[:, own : 2 * own]
    held[4][...] = w_mine[:, 2 * own : 2 * own + units]
    held[5][...] = w_mine[:, 2 * own + units :]
    for place in range(8):
        part, length = (long_part, long) if place < 5 else (short_part, short)
        held[6 + place][...] = part[place : place + 1, :length]
    for copy in start_copies(list(zip(held, outs)), sems):
        copy.wait()


def input_kernel(plan, me_ref, x_ref, stats_ref, grad_ref, normed_grad_ref, vec_ref, input_grad_ref):
    gain = read_vectors(vec_ref)[0:1]

    def rows_step(index, _):
        at = plan.block_rows(index)
        standard, inverse = standard_rows(plan, x_ref, stats_ref, at)
        scaled = normed_grad_ref[at, :] * gain
        input_grad_ref[at, :] = grad_ref[at, :].astype(F32) + inverse * (
            scaled
            - jnp.mean(scaled, axis=1, keepdims=True)
            - standard * jnp.mean(scaled * standard, axis=1, keepdims=True)
        )
        return 0

    lax.fori_loop(0, plan.blocks, rows_step, 0)


def call(kernel, plan, outs, scratch, limit, time, *args, far_in=0, far_out=False):
    args = [*args[:1], *(pltpu.with_memory_space_constraint(a, pltpu.HBM) for a in args[1 : 1 + far_in]), *args[1 + far_in :]]
    whole = pl.BlockSpec(memory_space=pltpu.VMEM)
    far = pl.BlockSpec(memory_space=pltpu.HBM)
    return pl.pallas_call(
        functools.partial(kernel, plan),
        out_shape=outs,
        in_specs=[pl.BlockSpec(memory_space=pltpu.SMEM)]
        + [far] * far_in
        + [whole] * (len(args) - 1 - far_in),
        out_specs=[far if far_out else whole] * len(outs),
        scratch_shapes=scratch,
        compiler_params=pltpu.CompilerParams(vmem_limit_bytes=limit * MIB),
        cost_estimate=pl.CostEstimate(
            flops=int(time * 1e9), bytes_accessed=int(time * 3.5e6), transcendentals=0
        ),
    )(*args)


def shape(dims, dtype=F32):
    return jax.ShapeDtypeStruct(dims, dtype)


def after(value, *others):
    return lax.optimization_barrier((value, *others))[0]


def joined(*parts):
    return jnp.concatenate(parts, axis=0)


def gather_blocks(plan, first, summed, second, cover):
    count, width = plan.count, second.shape[1]
    tensor_bits = log2(plan.tensor)
    other = None

    def first_step(bit):
        rows = first.shape[0]
        if bit < tensor_bits:
            got = flip(first, bit, count)
            return got, joined(first, got), summed
        got = flip(joined(first, summed), bit, count)
        if other is None:
            got = after(got, cover, second_other)
        return got, joined(first, got[:rows]), summed + got[rows:]

    for bit in plan.far:
        second_other = flip(second if other is None else after(second, other), bit, count)
        other, first, summed = first_step(bit)
        second = joined(second, second_other)
    second = joined(second, flip(after(second, other), 1, count))
    other, first, summed = first_step(3)
    blocks = second.reshape(-1, plan.own_rows, width)
    size = plan.own_rows // plan.halves
    halves = [
        after(blocks[:, half * size : half * size + size].reshape(-1, width), other)
        for half in range(plan.halves)
    ]
    halves = [joined(part, flip(part, bit, count)) for part, bit in zip(halves, (3, 2))]
    other, first, summed = first_step(2)
    halves = [(part, flip(part, bit, count)) for part, bit in zip(halves, (2, 3))]
    other, first, summed = first_step(1)
    return first, flip(first, 0, count), summed, halves


def split_high_low(value):
    high = lax.reduce_precision(value, 8, 7)
    return jnp.concatenate([high, value - high], axis=0).astype(BF16)


def cut(value):
    count = value.shape[0] // 2
    return value[:count].astype(BF16), value[count:].astype(BF16)


def added(keep, other):
    return keep.astype(F32) + other.astype(F32)


def summed_step(keep, send, other):
    count = keep.shape[0]
    rows = (send.shape[0] - count) // 2
    pairs = [part[count:].astype(F32) for part in (send, other)]
    summed = sum(pair[:rows] + pair[rows:] for pair in pairs)
    keep, send = cut(added(keep, other[:count]))
    return keep, joined(send, split_high_low(summed))


def together(*values):
    return lax.optimization_barrier(values)


def shards(
    mesh,
    block_input,
    segments,
    ln_gain,
    ln_bias,
    b_real,
    b_imag,
    c_real,
    c_imag,
    nu_log,
    theta_log,
    gamma_log,
    d_skip,
    w_value,
    w_gate,
    b_value,
    b_gate,
    out_grad,
):
    band = lax.axis_index("fsdp")
    shard = lax.axis_index("tensor")
    rows, features = block_input.shape
    own = b_real.shape[1]
    plan = Plan(
        mesh, rows, segments.shape[0], features, own * mesh.shape["tensor"], w_value.shape[1]
    )
    states, units, chunks = plan.states, plan.units, plan.chunks
    me = (band * plan.tensor + shard).astype(jnp.int32).reshape(1)
    long, short = plan.own_rows, states // plan.fsdp
    vector_rows = 8 * features // LANES
    matrices = (b_real, b_imag, c_real, c_imag, w_value, w_gate)
    lines = [
        v.reshape(1, -1)
        for v in (ln_gain, ln_bias, d_skip, b_value, b_gate, nu_log, theta_log, gamma_log)
    ]
    block = 2 * own + 2 * units
    first, second = call(
        pack_kernel,
        plan,
        [shape((long + vector_rows, 2 * own), BF16), shape((long, block), BF16)],
        [pltpu.VMEM(v.shape, BF16) for v in (*matrices, *lines)] + [pltpu.SemaphoreType.DMA((14,))],
        4,
        1.5,
        me, *matrices, *lines,
        far_in=14,
    )
    stats, masks = call(
        token_kernel,
        plan,
        [shape((2, rows, LANES)), shape((4, rows, LANES))],
        [pltpu.VMEM((3, plan.group_rows // LANES, LANES), F32)],
        8,
        2,
        me, block_input, segments.reshape(-1, LANES),
    )
    b0, b1, vectors, halves = gather_blocks(plan, first[:long], first[long:], second, masks)

    pack_type = BF16 if long % 16 == 0 else F32
    full = (rows, 2 * states)
    normed, source, ends, hold, carry, input_map, params = call(
        enter_kernel,
        plan,
        [
            shape((rows, features), BF16),
            shape(full),
            shape((chunks, 2 * states)),
            shape((chunks, LANES)),
            shape((8, 2 * states)),
            shape((features, 2 * states), BF16),
            shape((8, 2 * states)),
        ],
        [pltpu.VMEM((features, 2 * states), pack_type)],
        8,
        3,
        me, block_input, stats, b0, b1, vectors, masks,
    )

    def pass_on(value, forward):
        pairs = []
        for one in range(0, plan.tensor, 2):
            pairs.append((one, one + 1) if forward else (one + 1, one))
        return lax.ppermute(value, "tensor", pairs)

    left = carry
    carry = pass_on(carry, True) if plan.pieces == 2 else jnp.zeros_like(carry)
    g0 = joined(*(joined(part, after(got, left)) for part, got in halves))
    g1 = flip(after(g0, carry), 0, plan.count)
    (
        mixed, hidden, lru_grad, state_grad, act, unit_grad, low, sums,
    ) = call(
        middle_kernel,
        plan,
        [
            shape((rows, features), BF16),
            shape(full),
            shape((rows, features), BF16),
            shape(full),
            shape((rows, features), BF16),
            shape((rows, 2 * features), BF16),
            shape(full, BF16),
            shape((24, features)),
        ],
        [
            pltpu.VMEM((features, 2 * states), pack_type),
            pltpu.VMEM((features, 2 * features), pack_type),
            pltpu.VMEM((features, 2 * states), BF16),
        ],
        24,
        10,
        me, block_input, out_grad, normed, source, ends, hold, carry, g0, g1, vectors, params, masks,
    )
    half_rows = plan.count // 2 * long
    w_keep, w_send = call(
        weight_kernel,
        plan,
        [shape((half_rows, block), BF16)] * 2,
        [
            pltpu.VMEM((features, 2 * features), F32),
            pltpu.VMEM((features, 2 * states), F32),
        ],
        10,
        2.5,
        me, act, unit_grad, lru_grad, low,
    )
    w_other = flip(w_send, 0, plan.count)
    back_ends, back_hold, back = call(
        back_kernel,
        plan,
        [shape((chunks, 2 * states)), shape((chunks, LANES)), shape((8, 2 * states))],
        [],
        8,
        1.5,
        me, after(state_grad, w_send), params, masks,
    )
    back = pass_on(back, False) if plan.pieces == 2 else jnp.zeros_like(back)
    pieces = plan.halves
    w_other = after(w_other, back_ends)
    w_total = added(w_keep, w_other)
    size = w_total.shape[0] // pieces
    halves = [cut(w_total[half * size : half * size + size]) for half in range(pieces)]
    w_keeps = [half[0] for half in halves]
    w_others = [flip(half[1], bit, plan.count) for half, bit in zip(halves, (2, 3))]
    back_ends = after(back_ends, w_other)
    b_keep, b_send, normed_grad = call(
        leave_kernel,
        plan,
        [
            shape((half_rows, 2 * own), BF16),
            shape((half_rows + 2 * vector_rows, 2 * own), BF16),
            shape((rows, features)),
        ],
        [
            pltpu.VMEM(full, F32),
            pltpu.VMEM(full, BF16),
            pltpu.VMEM((features, 2 * states), F32),
        ],
        14,
        4.5,
        me, block_input, stats, normed, source, back_ends, back_hold, back, hidden,
        state_grad, lru_grad, input_map, vectors, params, masks, sums,
    )
    (input_grad,) = call(
        input_kernel,
        plan,
        [shape((rows, features))],
        [],
        8,
        2.5,
        me, block_input, stats, out_grad, normed_grad, vectors,
    )
    b_keep, b_send, input_grad, w_others = together(b_keep, b_send, input_grad, w_others)
    parts = [cut(added(keep, other)) for keep, other in zip(w_keeps, w_others)]
    w_others = [flip(part[1], bit, plan.count) for part, bit in zip(parts, (3, 2))]
    b_other = flip(b_send, 0, plan.count)
    b_keep, b_send = summed_step(b_keep, b_send, b_other)
    b_other = flip(b_send, 1, plan.count)
    b_other, w_others = together(b_other, w_others)
    b_keep, b_send = summed_step(b_keep, b_send, b_other)
    halves = [cut(added(part[0], other)) for part, other in zip(parts, w_others)]
    w_keep = joined(*(half[0] for half in halves))
    w_send = joined(*(half[1] for half in halves))
    for bit, w_bit in zip(plan.down[2:-1], [1, *plan.down[4:]]):
        b_send, w_send = together(b_send, w_send)
        b_other = flip(b_send, bit, plan.count)
        w_other = flip(w_send, w_bit, plan.count)
        if bit < plan.bits - 2:
            b_other, w_other = together(b_other, w_other)
        b_keep, b_send = summed_step(b_keep, b_send, b_other)
        if w_bit < plan.bits - 1:
            total = added(w_keep, w_other).reshape(pieces, -1, block)
            size = total.shape[1] // 2
            w_keep = total[:, :size].reshape(-1, block).astype(BF16)
            w_send = total[:, size:].reshape(-1, block).astype(BF16)
    b_other = flip(b_send, plan.bits - 1, plan.count)
    b_other, tail = b_other[:long], joined(b_send[long:], b_other[long:])
    small = (
        [(long, own)] * 4 + [(long, units)] * 2 + [(1, long)] * 5 + [(1, short)] * 3
    )
    (
        b_real_grad, b_imag_grad, c_real_grad, c_imag_grad, value_grad, gate_grad, *lines
    ) = call(
        last_kernel,
        plan,
        [shape(dims) for dims in small],
        [pltpu.VMEM(dims, F32) for dims in small] + [pltpu.SemaphoreType.DMA((14,))],
        4,
        2,
        me, b_keep, b_other, w_keep, w_other, tail,
        far_out=True,
    )
    gain_grad, bias_grad, skip_grad, value_line, gate_line, nu_grad, theta_grad, gamma_grad = (
        line.reshape(-1) for line in lines
    )
    return (
        mixed,
        input_grad,
        gain_grad,
        bias_grad,
        b_real_grad,
        b_imag_grad,
        c_real_grad,
        c_imag_grad,
        nu_grad,
        theta_grad,
        gamma_grad,
        skip_grad,
        value_grad,
        gate_grad,
        value_line,
        gate_line,
    )


def solution(mesh):
    in_specs = (
        P(("fsdp", "tensor"), None),
        P("fsdp"),
        P("fsdp"),
        P("fsdp"),
        P("fsdp", "tensor"),
        P("fsdp", "tensor"),
        P("fsdp", "tensor"),
        P("fsdp", "tensor"),
        P("fsdp"),
        P("fsdp"),
        P("fsdp"),
        P("fsdp"),
        P("fsdp", "tensor"),
        P("fsdp", "tensor"),
        P("fsdp"),
        P("fsdp"),
        P(("fsdp", "tensor"), None),
    )
    out_specs = (
        P(("fsdp", "tensor"), None),
        P(("fsdp", "tensor"), None),
        P("fsdp"),
        P("fsdp"),
        P("fsdp", "tensor"),
        P("fsdp", "tensor"),
        P("fsdp", "tensor"),
        P("fsdp", "tensor"),
        P("fsdp"),
        P("fsdp"),
        P("fsdp"),
        P("fsdp"),
        P("fsdp", "tensor"),
        P("fsdp", "tensor"),
        P("fsdp"),
        P("fsdp"),
    )
    return jax.shard_map(
        functools.partial(shards, mesh),
        mesh=mesh,
        in_specs=in_specs,
        out_specs=out_specs,
        check_vma=False,
    )
```

```python
import functools
import math

import jax
import jax.numpy as jnp
from jax import lax
from jax.experimental import pallas as pl
from jax.experimental.pallas import tpu as pltpu
from jax.sharding import PartitionSpec as P

SEQ_LEN = 2048
LANES = 128
TILE = 256
SIDE = 16
BLOCK = 1024
AXES = ("fsdp", "tensor")
norm_epsilon = 1e-05
GELU_SCALE = math.sqrt(2.0 / math.pi)
GELU_CUBE = 0.044715
F32 = jnp.float32
BF16 = jnp.bfloat16
MIB = 1024 * 1024


def log2(value):
    return value.bit_length() - 1


def flip(value, bit, count):
    return lax.ppermute(value, AXES, [(i, i ^ (1 << bit)) for i in range(count)])


def dot(left, right, left_dim=1, right_dim=0):
    return lax.dot_general(
        left, right, (((left_dim,), (right_dim,)), ((), ())), preferred_element_type=F32
    )


def fold_rows(value):
    rows, width = value.shape
    return jnp.sum(value.reshape(rows // 8, 8, width), axis=0)


def wide(mask, width):
    return jnp.concatenate([mask] * (width // LANES), axis=1)


def grid_index(dims, axis):
    return lax.broadcasted_iota(jnp.int32, dims, axis)


def regroup_matrix(states, shards):
    own = log2(states // shards)
    width = 2 * states
    source = grid_index((width, width), 0)
    target = grid_index((width, width), 1)
    part = (source >> own) & 1
    place = part * states + ((source >> (own + 1)) << own) + (source & ((1 << own) - 1))
    return jnp.where(place == target, 1.0, 0.0).astype(BF16)


def turn_matrix():
    source = grid_index((TILE, TILE), 0)
    target = grid_index((TILE, TILE), 1)
    bits = log2(SIDE)
    place = ((source & (SIDE - 1)) << bits) + (source >> bits)
    return jnp.where(place == target, 1.0, 0.0)


def turn_rows(turn, value):
    parts = [dot(turn, value[at : at + TILE]) for at in range(0, value.shape[0], TILE)]
    return jnp.concatenate(parts, axis=0).astype(BF16)


class Plan:
    def __init__(self, mesh, rows, group_rows, features, states, units):
        self.fsdp = mesh.shape["fsdp"]
        self.tensor = mesh.shape["tensor"]
        self.count = self.fsdp * self.tensor
        self.bits = log2(self.count)
        far = list(range(self.bits - 1, 3, -1))
        self.far = far
        self.up = [*far, 3, 2, 1, 0]
        self.up_crossed = ([*far, 1, 3, 2, 0], [*far, 1, 2, 3, 0])
        self.down = [0, 1, 2, 3, *far[::-1]]
        self.down_crossed = ([0, 2, 3, 1, *far[::-1]], [0, 3, 2, 1, *far[::-1]])
        self.halves = 2 if features // self.fsdp >= 32 else 1
        self.rows = rows
        self.group_rows = group_rows
        self.features = features
        self.states = states
        self.units = units
        self.own_states = states // self.tensor
        self.own_rows = features // self.fsdp
        self.pieces = SEQ_LEN // rows
        self.tiles = rows // TILE
        self.chunks = self.tiles * SIDE
        self.block = BLOCK if rows % BLOCK == 0 else TILE
        self.blocks = rows // self.block

    def slot_owner(self, slot, me, order):
        owner = me
        for place, bit in enumerate(order):
            owner = owner ^ (((slot >> (self.bits - 1 - place)) & 1) << bit)
        shift = log2(self.tensor)
        return owner >> shift, owner & (self.tensor - 1)

    def block_rows(self, index):
        return pl.ds(pl.multiple_of(index * self.block, self.block), self.block)


def step_rows(tile, place):
    return pl.ds(pl.multiple_of(tile * TILE + place * SIDE, SIDE), SIDE)


def scan_pass(plan, keep_ref, start, extra, reverse, visit):
    def step(index, carried):
        now, extra = carried
        place = SIDE - 1 - index if reverse else index
        after = []
        for tile in range(plan.tiles):
            at = step_rows(tile, place)
            state, extra = visit(tile, at, keep_ref[at, :], now[tile], extra)
            after.append(state)
        return after, extra

    return lax.fori_loop(0, SIDE, step, (start, extra), unroll=2)


def local_ends(plan, source_ref, keep_ref, rate, reverse):
    states = plan.states
    zero = jnp.zeros((SIDE, states), F32)
    rate_re = jnp.broadcast_to(rate[0], zero.shape)
    rate_im = jnp.broadcast_to(rate[1], zero.shape)
    one = jnp.ones((SIDE, LANES), F32)

    def visit(tile, at, keep, state, extra):
        now_re, now_im, hold = state
        held = wide(keep, states)
        pass_re, pass_im = held * rate_re, held * rate_im
        source = source_ref[at, :]
        next_re = (source[:, :states] + pass_re * now_re) - pass_im * now_im
        next_im = (source[:, states:] + pass_re * now_im) + pass_im * now_re
        return (next_re, next_im, hold * keep), extra

    ends, _ = scan_pass(plan, keep_ref, [(zero, zero, one)] * plan.tiles, 0, reverse, visit)
    return tuple(jnp.concatenate([end[part] for end in ends], axis=0) for part in range(3))


def shifted(value, distance, reverse):
    count = value.shape[0]
    row = grid_index(value.shape, 0)
    if reverse:
        moved = pltpu.roll(value, count - distance, 0)
        return jnp.where(row < count - distance, moved, 0.0)
    moved = pltpu.roll(value, distance, 0)
    return jnp.where(row >= distance, moved, 0.0)


def chunk_entries(plan, ends_re, ends_im, hold, rate, start, reverse):
    states, count = plan.states, plan.chunks
    power_re, power_im = rate
    for _ in range(log2(SIDE)):
        power_re, power_im = power_re * power_re - power_im * power_im, 2.0 * power_re * power_im
    first = count - 1 if reverse else 0
    if start is not None:
        at_first = grid_index((count, states), 0) == first
        held = jnp.where(at_first, wide(hold, states), 0.0)
        pass_re, pass_im = held * power_re, held * power_im
        ends_re = ends_re + (pass_re * start[0] - pass_im * start[1])
        ends_im = ends_im + (pass_re * start[1] + pass_im * start[0])
    distance = 1
    while distance < count:
        earlier_re = shifted(ends_re, distance, reverse)
        earlier_im = shifted(ends_im, distance, reverse)
        held = wide(hold, states)
        pass_re, pass_im = held * power_re, held * power_im
        ends_re = ends_re + (pass_re * earlier_re - pass_im * earlier_im)
        ends_im = ends_im + (pass_re * earlier_im + pass_im * earlier_re)
        hold = hold * shifted(hold, distance, reverse)
        power_re, power_im = power_re * power_re - power_im * power_im, 2.0 * power_re * power_im
        distance *= 2
    last = slice(0, 1) if reverse else slice(count - 1, count)
    leaving = jnp.concatenate([ends_re[last], ends_im[last]], axis=1)
    if start is None:
        return None, leaving
    entry_re = shifted(ends_re, 1, reverse) + jnp.where(at_first, start[0], 0.0)
    entry_im = shifted(ends_im, 1, reverse) + jnp.where(at_first, start[1], 0.0)
    entries = []
    for tile in range(plan.tiles):
        at = slice(tile * SIDE, (tile + 1) * SIDE)
        entries.append((entry_re[at], entry_im[at]))
    return entries, leaving


def block_places(plan, me, order, refs, base, rows, start):
    slot = 0
    for ref in refs:
        for place in range(plan.count // 2):
            band, shard = plan.slot_owner(slot, me, order)
            slot += 1
            first = pl.multiple_of(band * plan.own_rows + start, rows)
            yield ref, base + place * rows, pl.ds(first, rows), shard


def collect(plan, me, order, refs, base, rows, start, targets):
    for ref, row, at, shard in block_places(plan, me, order, refs, base, rows, start):
        for first, width, out_ref, lanes in targets:
            column = pl.multiple_of(lanes + shard * width, LANES)
            out_ref[at, pl.ds(column, width)] = ref[row : row + rows, first : first + width].astype(
                out_ref.dtype
            )


def distribute(plan, me, order, refs, base, rows, start, targets):
    for ref, row, at, shard in block_places(plan, me, order, refs, base, rows, start):
        for first, width, full_ref, lanes in targets:
            column = pl.multiple_of(lanes + shard * width, LANES)
            ref[row : row + rows, first : first + width] = full_ref[at, pl.ds(column, width)].astype(
                ref.dtype
            )


def half_blocks(plan, orders):
    rows = plan.own_rows // plan.halves
    for half in range(plan.halves):
        yield orders[half], half * plan.count // 2 * rows, rows, half * rows


def start_copies(pairs, sems):
    copies = [
        pltpu.make_async_copy(source, target, sems.at[place])
        for place, (source, target) in enumerate(pairs)
    ]
    for copy in copies:
        copy.start()
    return copies


def pack_kernel(plan, me_ref, *refs):
    sources, outs, held, sems = refs[:14], refs[14:16], refs[16:30], refs[30]
    copies = start_copies(list(zip(sources, held)), sems)
    first_ref, second_ref = outs
    band = me_ref[0] >> log2(plan.tensor)
    rows, features = plan.own_rows, plan.features
    for copy in copies:
        copy.wait()
    first_ref[:rows, :] = jnp.concatenate([held[0][...], held[1][...]], axis=1)
    second_ref[...] = jnp.concatenate([ref[...] for ref in held[2:6]], axis=1)
    placed = []
    lane = grid_index((1, features), 1)
    for ref in held[6:]:
        length = ref.shape[1]
        value = ref[...].astype(F32)
        value = jnp.concatenate([value] * (features // length), axis=1)
        placed.append(jnp.where((lane >> log2(length)) == band, value, 0.0))
    placed = jnp.concatenate(placed, axis=0).astype(BF16)
    for part in range(features // LANES):
        first_ref[rows + 8 * part : rows + 8 * part + 8, :] = placed[
            :, part * LANES : (part + 1) * LANES
        ]


def token_kernel(plan, me_ref, x_ref, segments_ref, stats_ref, masks_ref, flags_ref):
    shard = me_ref[0] & (plan.tensor - 1)
    ids = segments_ref[...]
    count = ids.shape[0]
    lane = grid_index(ids.shape, 1)
    position = (grid_index(ids.shape, 0) * LANES + lane) & (SEQ_LEN - 1)
    turned = pltpu.roll(ids, 1, 1)
    before = jnp.where(lane == 0, pltpu.roll(turned, 1, 0), turned)
    turned = pltpu.roll(ids, LANES - 1, 1)
    after = jnp.where(lane == LANES - 1, pltpu.roll(turned, count - 1, 0), turned)
    flags_ref[0] = jnp.where((position > 0) & (ids == before), 1.0, 0.0)
    flags_ref[1] = jnp.where((position < SEQ_LEN - 1) & (ids == after), 1.0, 0.0)
    flags_ref[2] = jnp.where(ids > 0, 1.0, 0.0)
    turn = turn_matrix()
    plain = jnp.where(grid_index((TILE, TILE), 0) == grid_index((TILE, TILE), 1), 1.0, 0.0)
    ones = jnp.ones((TILE, LANES), BF16)
    per_tile = TILE // LANES
    own = plan.rows // LANES
    flags = [flags_ref[kind, pl.ds(pl.multiple_of(shard * own, own), own), :] for kind in range(3)]
    for tile in range(plan.tiles):
        at = slice(tile * TILE, (tile + 1) * TILE)
        for kind in range(4):
            rows = flags[min(kind, 2)][tile * per_tile : (tile + 1) * per_tile, :]
            line = jnp.concatenate([rows[part : part + 1, :] for part in range(per_tile)], axis=1)
            spread = (plain if kind == 3 else turn) * line
            masks_ref[kind, at, :] = dot(spread.astype(BF16), ones)

    def rows_step(index, _):
        at = plan.block_rows(index)
        values = x_ref[at, :].astype(F32)
        mean = jnp.mean(values, axis=1, keepdims=True)
        centred = values - mean
        inverse = lax.rsqrt(jnp.mean(centred * centred, axis=1, keepdims=True) + norm_epsilon)
        stats_ref[0, at, :] = jnp.broadcast_to(mean, (plan.block, LANES))
        stats_ref[1, at, :] = jnp.broadcast_to(inverse, (plan.block, LANES))
        return 0

    lax.fori_loop(0, plan.blocks, rows_step, 0)


def standard_rows(plan, x_ref, stats_ref, at):
    mean = wide(stats_ref[0, at, :], plan.features)
    inverse = wide(stats_ref[1, at, :], plan.features)
    return (x_ref[at, :].astype(F32) - mean) * inverse, inverse


def read_vectors(vec_ref):
    count = vec_ref.shape[0] // 8
    parts = [vec_ref[8 * part : 8 * part + 8, :].astype(F32) for part in range(count)]
    return jnp.concatenate(parts, axis=1)


def enter_kernel(
    plan, me_ref, x_ref, stats_ref, b0_ref, b1_ref, vec_ref, masks_ref,
    normed_ref, source_ref, ends_ref, hold_ref, carry_ref, input_map_ref, params_ref,
    pack_ref,
):
    states = plan.states
    collect(
        plan, me_ref[0], plan.up[::-1], (b0_ref, b1_ref), 0, plan.own_rows, 0,
        [(0, 2 * plan.own_states, pack_ref, 0)],
    )
    input_map_ref[...] = dot(
        pack_ref[...].astype(BF16), regroup_matrix(states, plan.tensor)
    ).astype(BF16)
    vectors = read_vectors(vec_ref)
    gain, shift = vectors[0:1], vectors[1:2]
    speed = jnp.exp(vectors[5:6, :states])
    modulus = jnp.exp(-speed)
    rotation = jnp.exp(vectors[6:7, :states])
    rate = (modulus * jnp.cos(rotation), modulus * jnp.sin(rotation))
    rest = 1.0 - modulus * modulus
    gamma = jnp.exp(vectors[7:8, :states]) * jnp.sqrt(rest)
    params_ref[...] = jnp.concatenate(
        [
            jnp.concatenate(rate, axis=1),
            jnp.concatenate([gamma, speed], axis=1),
            jnp.concatenate([modulus, rest], axis=1),
            jnp.concatenate([rotation, rotation], axis=1),
            jnp.zeros((4, 2 * states), F32),
        ],
        axis=0,
    )
    gamma_pair = jnp.concatenate([gamma, gamma], axis=1)
    turn = turn_matrix().astype(BF16)

    def rows_step(index, _):
        at = plan.block_rows(index)
        standard, _ = standard_rows(plan, x_ref, stats_ref, at)
        normed = (standard * gain + shift).astype(BF16)
        normed_ref[at, :] = normed
        turned = turn_rows(turn, normed)
        drive = dot(turned, input_map_ref[...])
        source_ref[at, :] = drive * gamma_pair * wide(masks_ref[2, at, :], 2 * states)
        return 0

    lax.fori_loop(0, plan.blocks, rows_step, 0)
    ends_re, ends_im, hold = local_ends(plan, source_ref, masks_ref.at[0], rate, False)
    ends_ref[...] = jnp.concatenate([ends_re, ends_im], axis=1)
    hold_ref[...] = hold
    _, leaving = chunk_entries(plan, ends_re, ends_im, hold, rate, None, False)
    carry_ref[...] = jnp.broadcast_to(leaving, carry_ref.shape)


def middle_kernel(
    plan, me_ref, x_ref, grad_ref, normed_ref, source_ref, ends_ref, hold_ref, carry_ref,
    g0_ref, g1_ref, vec_ref, params_ref, masks_ref,
    mixed_ref, hidden_ref, lru_grad_ref, state_grad_ref, act_ref, unit_grad_ref, low_ref, sums_ref,
    pack_ref, wpack_ref, out_map_ref,
):
    states, features, units = plan.states, plan.features, plan.units
    pair = 2 * plan.own_states
    targets = [
        (0, pair, pack_ref, 0),
        (pair, units, wpack_ref, 0),
        (pair + units, units, wpack_ref, features),
    ]
    for order, base, rows, first in half_blocks(plan, plan.up_crossed):
        collect(plan, me_ref[0], order[::-1], (g0_ref, g1_ref), base, rows, first, targets)
    sign = jnp.where(grid_index((1, 2 * states), 1) < states, 1.0, -1.0)
    regroup = regroup_matrix(states, plan.tensor)
    out_map_ref[...] = (dot(pack_ref[...].astype(BF16), regroup) * sign).astype(BF16)
    rate = (params_ref[0:1, :states], params_ref[0:1, states:])
    start = (carry_ref[0:1, :states], carry_ref[0:1, states:])
    entries, _ = chunk_entries(
        plan, ends_ref[:, :states], ends_ref[:, states:], hold_ref[...], rate, start, False
    )
    rate_re = jnp.broadcast_to(rate[0], (SIDE, states))
    rate_im = jnp.broadcast_to(rate[1], (SIDE, states))

    def visit(tile, at, keep, state, extra):
        now_re, now_im = state
        held = wide(keep, states)
        pass_re, pass_im = held * rate_re, held * rate_im
        source = source_ref[at, :]
        next_re = (source[:, :states] + pass_re * now_re) - pass_im * now_im
        next_im = (source[:, states:] + pass_re * now_im) + pass_im * now_re
        hidden_ref[at, :states] = next_re
        hidden_ref[at, states:] = next_im
        return (next_re, next_im), extra

    scan_pass(plan, masks_ref.at[0], entries, 0, False, visit)
    vectors = read_vectors(vec_ref)
    skip = vectors[2:3]
    biases = jnp.concatenate([vectors[3:4], vectors[4:5]], axis=1)
    sums_ref[...] = jnp.zeros_like(sums_ref)
    turn = turn_matrix().astype(BF16)

    def rows_step(index, _):
        at = plan.block_rows(index)
        low = turn_rows(turn, hidden_ref[at, :].astype(BF16))
        low_ref[at, :] = low
        normed = normed_ref[at, :].astype(F32)
        lru = dot(low, out_map_ref[...], 1, 1) + skip * normed
        square = lru * lru
        bent = jnp.tanh(lru * (GELU_SCALE + (GELU_SCALE * GELU_CUBE) * square))
        half = 0.5 + 0.5 * bent
        act_wide = lru * half
        slope = half + act_wide * (1.0 - half) * (
            2.0 * GELU_SCALE + (6.0 * GELU_SCALE * GELU_CUBE) * square
        )
        act = act_wide.astype(BF16)
        act_ref[at, :] = act
        mapped = dot(act, wpack_ref[...].astype(BF16)) + biases
        value = mapped[:, :features]
        live_half = wide(0.5 * masks_ref[3, at, :], features)
        opening = live_half + live_half * jnp.tanh(0.5 * mapped[:, features:])
        gated = value * opening
        mixed_ref[at, :] = (x_ref[at, :].astype(F32) + gated).astype(BF16)
        value_grad = grad_ref[at, :].astype(F32) * opening
        gate_grad = value_grad * (value - gated)
        sums_ref[8:16, :] += fold_rows(value_grad)
        sums_ref[16:24, :] += fold_rows(gate_grad)
        unit_grad = jnp.concatenate([value_grad, gate_grad], axis=1).astype(BF16)
        unit_grad_ref[at, :] = unit_grad
        act_grad = dot(unit_grad, wpack_ref[...].astype(BF16), 1, 1)
        lru_grad = act_grad * slope
        sums_ref[0:8, :] += fold_rows(lru_grad * normed)
        lru_grad = lru_grad.astype(BF16)
        lru_grad_ref[at, :] = lru_grad
        turned = turn_rows(turn, lru_grad)
        state_grad_ref[at, :] = dot(turned, out_map_ref[...])
        return 0

    lax.fori_loop(0, plan.blocks, rows_step, 0)


def back_kernel(
    plan, me_ref, state_grad_ref, params_ref, masks_ref, back_ends_ref, back_hold_ref, back_ref
):
    states = plan.states
    back_rate = (params_ref[0:1, :states], -params_ref[0:1, states:])
    ends_re, ends_im, hold = local_ends(plan, state_grad_ref, masks_ref.at[1], back_rate, True)
    back_ends_ref[...] = jnp.concatenate([ends_re, ends_im], axis=1)
    back_hold_ref[...] = hold
    _, leaving = chunk_entries(plan, ends_re, ends_im, hold, back_rate, None, True)
    back_ref[...] = jnp.broadcast_to(leaving, back_ref.shape)


def weight_kernel(
    plan, me_ref, act_ref, unit_grad_ref, lru_grad_ref, low_ref, keep_ref, send_ref, full_ref, out_ref
):
    states, features, units = plan.states, plan.features, plan.units
    pair = 2 * plan.own_states
    sign = jnp.where(grid_index((1, 2 * states), 1) < states, 1.0, -1.0)
    full_ref[...] = dot(act_ref[...], unit_grad_ref[...], 0, 0)
    out_grad = dot(lru_grad_ref[...], low_ref[...], 0, 0) * sign
    out_ref[...] = dot(out_grad.astype(BF16), regroup_matrix(states, plan.tensor), 1, 1)
    targets = [
        (0, pair, out_ref, 0),
        (pair, units, full_ref, 0),
        (pair + units, units, full_ref, features),
    ]
    for order, base, rows, first in half_blocks(plan, plan.down_crossed):
        distribute(plan, me_ref[0], order, (keep_ref, send_ref), base, rows, first, targets)


def leave_kernel(
    plan, me_ref, x_ref, stats_ref, normed_ref, source_ref, ends_ref, hold_ref, carry_ref, hidden_ref,
    state_grad_ref, lru_grad_ref, input_map_ref, vec_ref, params_ref, masks_ref, sums_ref,
    keep_ref, send_ref, normed_grad_ref,
    drive_grad_ref, low_ref, full_ref,
):
    states, features = plan.states, plan.features
    params = params_ref[...]
    rate = (params[0:1, :states], params[0:1, states:])
    gamma, speed = params[1:2, :states], params[1:2, states:]
    modulus, rest = params[2:3, :states], params[2:3, states:]
    rotation = params[3:4, :states]
    back_rate = (rate[0], -rate[1])
    start = (carry_ref[0:1, :states], carry_ref[0:1, states:])
    entries, _ = chunk_entries(
        plan, ends_ref[:, :states], ends_ref[:, states:], hold_ref[...], back_rate, start, True
    )
    zero = jnp.zeros((SIDE, states), F32)
    rate_re = jnp.broadcast_to(back_rate[0], zero.shape)
    rate_im = jnp.broadcast_to(back_rate[1], zero.shape)
    gamma_wide = jnp.broadcast_to(gamma, zero.shape)

    def visit(tile, at, keep, state, sums):
        now_re, now_im = state
        held = wide(keep, states)
        next_re, next_im = held * now_re, held * now_im
        hidden_re, hidden_im = hidden_ref[at, :states], hidden_ref[at, states:]
        now_re = (state_grad_ref[at, :states] + rate_re * next_re) - rate_im * next_im
        now_im = (state_grad_ref[at, states:] + rate_re * next_im) + rate_im * next_re
        sums = (
            sums[0] + (hidden_re * next_re + hidden_im * next_im),
            sums[1] + (hidden_re * next_im - hidden_im * next_re),
            sums[2] + (source_ref[at, :states] * now_re + source_ref[at, states:] * now_im),
        )
        scale = gamma_wide * wide(masks_ref[2, at, :], states)
        drive_grad_ref[at, :states] = scale * now_re
        drive_grad_ref[at, states:] = scale * now_im
        return (now_re, now_im), sums

    _, sums = scan_pass(plan, masks_ref.at[1], entries, (zero, zero, zero), True, visit)
    rate_sum_re, rate_sum_im, gamma_sum = (jnp.sum(part, axis=0, keepdims=True) for part in sums)
    nu_grad = speed * (
        gamma_sum * modulus * modulus / rest - (rate_sum_re * rate[0] + rate_sum_im * rate[1])
    )
    theta_grad = rotation * (rate_sum_im * rate[0] - rate_sum_re * rate[1])
    vectors = read_vectors(vec_ref)
    skip = vectors[2:3]
    gain_sum = jnp.zeros((8, features), F32)
    turn = turn_matrix().astype(BF16)

    def rows_step(index, sums):
        gain_sum, shift_sum = sums
        at = plan.block_rows(index)
        low = turn_rows(turn, drive_grad_ref[at, :].astype(BF16))
        low_ref[at, :] = low
        normed_grad = dot(low, input_map_ref[...], 1, 1) + skip * lru_grad_ref[at, :].astype(F32)
        normed_grad_ref[at, :] = normed_grad
        standard, _ = standard_rows(plan, x_ref, stats_ref, at)
        return gain_sum + fold_rows(normed_grad * standard), shift_sum + fold_rows(normed_grad)

    gain_sum, shift_sum = lax.fori_loop(0, plan.blocks, rows_step, (gain_sum, gain_sum))
    into = dot(normed_ref[...], low_ref[...], 0, 0)
    full_ref[...] = dot(into.astype(BF16), regroup_matrix(states, plan.tensor), 1, 1)
    distribute(
        plan, me_ref[0], plan.down, (keep_ref, send_ref), 0, plan.own_rows, 0,
        [(0, 2 * plan.own_states, full_ref, 0)],
    )
    empty = jnp.zeros((1, features - states), F32)
    vector_sums = jnp.concatenate(
        [jnp.sum(part, axis=0, keepdims=True) for part in (gain_sum, shift_sum)]
        + [
            jnp.sum(sums_ref[8 * place : 8 * place + 8, :], axis=0, keepdims=True)
            for place in range(3)
        ]
        + [jnp.concatenate([part, empty], axis=1) for part in (nu_grad, theta_grad, gamma_sum)],
        axis=0,
    )
    base = plan.own_rows * plan.count // 2
    parts = features // LANES
    for part in range(parts):
        piece = vector_sums[:, part * LANES : (part + 1) * LANES]
        high = piece.astype(BF16)
        low = (piece - high.astype(F32)).astype(BF16)
        send_ref[base + 8 * part : base + 8 * part + 8, :] = high
        send_ref[base + 8 * (parts + part) : base + 8 * (parts + part) + 8, :] = low


def last_kernel(plan, me_ref, *refs):
    b_keep, b_other, w_mine_ref, tail_ref = refs[:4]
    outs, held, sems = refs[4:18], refs[18:32], refs[32]
    own, units = plan.own_states, plan.units
    b_mine = b_keep[...].astype(F32) + b_other[...].astype(F32)
    w_mine = w_mine_ref[...]
    half = tail_ref.shape[0] // 4
    tail = [tail_ref[part * half : part * half + half, :].astype(F32) for part in range(4)]
    vectors = (tail[0] + tail[1]) + (tail[2] + tail[3])
    count = half // 8
    vectors = jnp.concatenate([vectors[8 * part : 8 * part + 8] for part in range(count)], axis=1)
    band = me_ref[0] >> log2(plan.tensor)
    at = grid_index((plan.features, LANES), 0)
    lane = grid_index((plan.features, LANES), 1)

    def pick(length):
        chosen = jnp.where(at == band * length + lane, 1.0, 0.0)
        return lax.dot_general(
            vectors,
            chosen,
            (((1,), (0,)), ((), ())),
            precision=lax.Precision.HIGHEST,
            preferred_element_type=F32,
        )

    long, short = plan.own_rows, plan.states // plan.fsdp
    long_part, short_part = pick(long), pick(short)
    held[0][...] = b_mine[:, :own]
    held[1][...] = b_mine[:, own:]
    held[2][...] = w_mine[:, :own]
    held[3][...] = w_mine[:, own : 2 * own]
    held[4][...] = w_mine[:, 2 * own : 2 * own + units]
    held[5][...] = w_mine[:, 2 * own + units :]
    for place in range(8):
        part, length = (long_part, long) if place < 5 else (short_part, short)
        held[6 + place][...] = part[place : place + 1, :length]
    for copy in start_copies(list(zip(held, outs)), sems):
        copy.wait()


def input_kernel(plan, me_ref, x_ref, stats_ref, grad_ref, normed_grad_ref, vec_ref, input_grad_ref):
    gain = read_vectors(vec_ref)[0:1]

    def rows_step(index, _):
        at = plan.block_rows(index)
        standard, inverse = standard_rows(plan, x_ref, stats_ref, at)
        scaled = normed_grad_ref[at, :] * gain
        input_grad_ref[at, :] = grad_ref[at, :].astype(F32) + inverse * (
            scaled
            - jnp.mean(scaled, axis=1, keepdims=True)
            - standard * jnp.mean(scaled * standard, axis=1, keepdims=True)
        )
        return 0

    lax.fori_loop(0, plan.blocks, rows_step, 0)


def call(kernel, plan, outs, scratch, limit, time, *args, far_in=0, far_out=False):
    args = [*args[:1], *(pltpu.with_memory_space_constraint(a, pltpu.HBM) for a in args[1 : 1 + far_in]), *args[1 + far_in :]]
    whole = pl.BlockSpec(memory_space=pltpu.VMEM)
    far = pl.BlockSpec(memory_space=pltpu.HBM)
    return pl.pallas_call(
        functools.partial(kernel, plan),
        out_shape=outs,
        in_specs=[pl.BlockSpec(memory_space=pltpu.SMEM)]
        + [far] * far_in
        + [whole] * (len(args) - 1 - far_in),
        out_specs=[far if far_out else whole] * len(outs),
        scratch_shapes=scratch,
        compiler_params=pltpu.CompilerParams(vmem_limit_bytes=limit * MIB),
        cost_estimate=pl.CostEstimate(
            flops=int(time * 1e9), bytes_accessed=int(time * 3.5e6), transcendentals=0
        ),
    )(*args)


def shape(dims, dtype=F32):
    return jax.ShapeDtypeStruct(dims, dtype)


def after(value, *others):
    return lax.optimization_barrier((value, *others))[0]


def joined(*parts):
    return jnp.concatenate(parts, axis=0)


def gather_blocks(plan, first, summed, second, cover):
    count, width = plan.count, second.shape[1]
    tensor_bits = log2(plan.tensor)
    other = None

    def first_step(bit):
        rows = first.shape[0]
        if bit < tensor_bits:
            got = flip(first, bit, count)
            return got, joined(first, got), summed
        got = flip(joined(first, summed), bit, count)
        if other is None:
            got = after(got, cover, second_other)
        return got, joined(first, got[:rows]), summed + got[rows:]

    for bit in plan.far:
        second_other = flip(second if other is None else after(second, other), bit, count)
        other, first, summed = first_step(bit)
        second = joined(second, second_other)
    second = joined(second, flip(after(second, other), 1, count))
    other, first, summed = first_step(3)
    blocks = second.reshape(-1, plan.own_rows, width)
    size = plan.own_rows // plan.halves
    halves = [
        after(blocks[:, half * size : half * size + size].reshape(-1, width), other)
        for half in range(plan.halves)
    ]
    halves = [joined(part, flip(part, bit, count)) for part, bit in zip(halves, (3, 2))]
    other, first, summed = first_step(2)
    halves = [(part, flip(part, bit, count)) for part, bit in zip(halves, (2, 3))]
    other, first, summed = first_step(1)
    return first, flip(first, 0, count), summed, halves


def split_high_low(value):
    high = lax.reduce_precision(value, 8, 7)
    return jnp.concatenate([high, value - high], axis=0).astype(BF16)


def cut(value):
    count = value.shape[0] // 2
    return value[:count].astype(BF16), value[count:].astype(BF16)


def added(keep, other):
    return keep.astype(F32) + other.astype(F32)


def summed_step(keep, send, other):
    count = keep.shape[0]
    rows = (send.shape[0] - count) // 2
    pairs = [part[count:].astype(F32) for part in (send, other)]
    summed = sum(pair[:rows] + pair[rows:] for pair in pairs)
    keep, send = cut(added(keep, other[:count]))
    return keep, joined(send, split_high_low(summed))


def together(*values):
    return lax.optimization_barrier(values)


def shards(
    mesh,
    block_input,
    segments,
    ln_gain,
    ln_bias,
    b_real,
    b_imag,
    c_real,
    c_imag,
    nu_log,
    theta_log,
    gamma_log,
    d_skip,
    w_value,
    w_gate,
    b_value,
    b_gate,
    out_grad,
):
    band = lax.axis_index("fsdp")
    shard = lax.axis_index("tensor")
    rows, features = block_input.shape
    own = b_real.shape[1]
    plan = Plan(
        mesh, rows, segments.shape[0], features, own * mesh.shape["tensor"], w_value.shape[1]
    )
    states, units, chunks = plan.states, plan.units, plan.chunks
    me = (band * plan.tensor + shard).astype(jnp.int32).reshape(1)
    long, short = plan.own_rows, states // plan.fsdp
    vector_rows = 8 * features // LANES
    matrices = (b_real, b_imag, c_real, c_imag, w_value, w_gate)
    lines = [
        v.reshape(1, -1)
        for v in (ln_gain, ln_bias, d_skip, b_value, b_gate, nu_log, theta_log, gamma_log)
    ]
    block = 2 * own + 2 * units
    first, second = call(
        pack_kernel,
        plan,
        [shape((long + vector_rows, 2 * own), BF16), shape((long, block), BF16)],
        [pltpu.VMEM(v.shape, BF16) for v in (*matrices, *lines)] + [pltpu.SemaphoreType.DMA((14,))],
        4,
        1.5,
        me, *matrices, *lines,
        far_in=14,
    )
    stats, masks = call(
        token_kernel,
        plan,
        [shape((2, rows, LANES)), shape((4, rows, LANES))],
        [pltpu.VMEM((3, plan.group_rows // LANES, LANES), F32)],
        8,
        2,
        me, block_input, segments.reshape(-1, LANES),
    )
    b0, b1, vectors, halves = gather_blocks(plan, first[:long], first[long:], second, masks)

    pack_type = BF16 if long % 16 == 0 else F32
    full = (rows, 2 * states)
    normed, source, ends, hold, carry, input_map, params = call(
        enter_kernel,
        plan,
        [
            shape((rows, features), BF16),
            shape(full),
            shape((chunks, 2 * states)),
            shape((chunks, LANES)),
            shape((8, 2 * states)),
            shape((features, 2 * states), BF16),
            shape((8, 2 * states)),
        ],
        [pltpu.VMEM((features, 2 * states), pack_type)],
        8,
        0.3,
        me, block_input, stats, b0, b1, vectors, masks,
    )

    def pass_on(value, forward):
        pairs = []
        for one in range(0, plan.tensor, 2):
            pairs.append((one, one + 1) if forward else (one + 1, one))
        return lax.ppermute(value, "tensor", pairs)

    left = carry
    carry = pass_on(carry, True) if plan.pieces == 2 else jnp.zeros_like(carry)
    g0 = joined(*(joined(part, after(got, left)) for part, got in halves))
    g1 = flip(after(g0, carry), 0, plan.count)
    (
        mixed, hidden, lru_grad, state_grad, act, unit_grad, low, sums,
    ) = call(
        middle_kernel,
        plan,
        [
            shape((rows, features), BF16),
            shape(full),
            shape((rows, features), BF16),
            shape(full),
            shape((rows, features), BF16),
            shape((rows, 2 * features), BF16),
            shape(full, BF16),
            shape((24, features)),
        ],
        [
            pltpu.VMEM((features, 2 * states), pack_type),
            pltpu.VMEM((features, 2 * features), pack_type),
            pltpu.VMEM((features, 2 * states), BF16),
        ],
        24,
        10,
        me, block_input, out_grad, normed, source, ends, hold, carry, g0, g1, vectors, params, masks,
    )
    half_rows = plan.count // 2 * long
    w_keep, w_send = call(
        weight_kernel,
        plan,
        [shape((half_rows, block), BF16)] * 2,
        [
            pltpu.VMEM((features, 2 * features), F32),
            pltpu.VMEM((features, 2 * states), F32),
        ],
        10,
        2.5,
        me, act, unit_grad, lru_grad, low,
    )
    w_other = flip(w_send, 0, plan.count)
    back_ends, back_hold, back = call(
        back_kernel,
        plan,
        [shape((chunks, 2 * states)), shape((chunks, LANES)), shape((8, 2 * states))],
        [],
        8,
        1,
        me, after(state_grad, w_send), params, masks,
    )
    back = pass_on(back, False) if plan.pieces == 2 else jnp.zeros_like(back)
    pieces = plan.halves
    w_total = added(w_keep, after(w_other, back_ends))
    size = w_total.shape[0] // pieces
    halves = [cut(w_total[half * size : half * size + size]) for half in range(pieces)]
    w_others = [flip(half[1], bit, plan.count) for half, bit in zip(halves, (2, 3))]
    back_ends = after(back_ends, *(half[1] for half in halves))
    b_keep, b_send, normed_grad = call(
        leave_kernel,
        plan,
        [
            shape((half_rows, 2 * own), BF16),
            shape((half_rows + 2 * vector_rows, 2 * own), BF16),
            shape((rows, features)),
        ],
        [
            pltpu.VMEM(full, F32),
            pltpu.VMEM(full, BF16),
            pltpu.VMEM((features, 2 * states), F32),
        ],
        14,
        4.5,
        me, block_input, stats, normed, source, back_ends, back_hold, back, hidden,
        state_grad, lru_grad, input_map, vectors, params, masks, sums,
    )
    w_others = [after(other, b_keep) for other in w_others]
    halves = [cut(added(half[0], other)) for half, other in zip(halves, w_others)]
    b_other = after(flip(b_send, 0, plan.count), *(half[1] for half in halves))
    b_keep, b_send = summed_step(b_keep, b_send, b_other)
    b_other = flip(b_send, 1, plan.count)
    w_others = [flip(half[1], bit, plan.count) for half, bit in zip(halves, (3, 2))]
    (input_grad,) = call(
        input_kernel,
        plan,
        [shape((rows, features))],
        [],
        8,
        2.5,
        me, block_input, stats, out_grad, after(normed_grad, b_send), vectors,
    )
    b_other = after(b_other, input_grad)
    b_keep, b_send = summed_step(b_keep, b_send, b_other)
    halves = [cut(added(half[0], after(other, b_send))) for half, other in zip(halves, w_others)]
    w_keep = joined(*(half[0] for half in halves))
    w_send = joined(*(half[1] for half in halves))
    for bit in range(2, plan.bits - 1):
        w_bit = 1 if bit == 2 else bit + 1
        b_other = flip(b_send, bit, plan.count)
        w_other = flip(w_send, w_bit, plan.count)
        b_keep, b_send = summed_step(b_keep, b_send, b_other)
        if w_bit < plan.bits - 1:
            w_other = after(w_other, b_send)
            total = added(w_keep, w_other).reshape(pieces, -1, block)
            size = total.shape[1] // 2
            w_keep = total[:, :size].reshape(-1, block).astype(BF16)
            w_send = total[:, size:].reshape(-1, block).astype(BF16)
    w_mine = added(w_keep, w_other)
    b_other = after(flip(b_send, plan.bits - 1, plan.count), w_mine)
    b_other, tail = b_other[:long], joined(b_send[long:], b_other[long:])
    small = (
        [(long, own)] * 4 + [(long, units)] * 2 + [(1, long)] * 5 + [(1, short)] * 3
    )
    (
        b_real_grad, b_imag_grad, c_real_grad, c_imag_grad, value_grad, gate_grad, *lines
    ) = call(
        last_kernel,
        plan,
        [shape(dims) for dims in small],
        [pltpu.VMEM(dims, F32) for dims in small] + [pltpu.SemaphoreType.DMA((14,))],
        4,
        2,
        me, b_keep, b_other, w_mine, tail,
        far_out=True,
    )
    gain_grad, bias_grad, skip_grad, value_line, gate_line, nu_grad, theta_grad, gamma_grad = (
        line.reshape(-1) for line in lines
    )
    return (
        mixed,
        input_grad,
        gain_grad,
        bias_grad,
        b_real_grad,
        b_imag_grad,
        c_real_grad,
        c_imag_grad,
        nu_grad,
        theta_grad,
        gamma_grad,
        skip_grad,
        value_grad,
        gate_grad,
        value_line,
        gate_line,
    )


def solution(mesh):
    in_specs = (
        P(("fsdp", "tensor"), None),
        P("fsdp"),
        P("fsdp"),
        P("fsdp"),
        P("fsdp", "tensor"),
        P("fsdp", "tensor"),
        P("fsdp", "tensor"),
        P("fsdp", "tensor"),
        P("fsdp"),
        P("fsdp"),
        P("fsdp"),
        P("fsdp"),
        P("fsdp", "tensor"),
        P("fsdp", "tensor"),
        P("fsdp"),
        P("fsdp"),
        P(("fsdp", "tensor"), None),
    )
    out_specs = (
        P(("fsdp", "tensor"), None),
        P(("fsdp", "tensor"), None),
        P("fsdp"),
        P("fsdp"),
        P("fsdp", "tensor"),
        P("fsdp", "tensor"),
        P("fsdp", "tensor"),
        P("fsdp", "tensor"),
        P("fsdp"),
        P("fsdp"),
        P("fsdp"),
        P("fsdp"),
        P("fsdp", "tensor"),
        P("fsdp", "tensor"),
        P("fsdp"),
        P("fsdp"),
    )
    return jax.shard_map(
        functools.partial(shards, mesh),
        mesh=mesh,
        in_specs=in_specs,
        out_specs=out_specs,
        check_vma=False,
    )
```

```python
import functools
import math

import jax
import jax.numpy as jnp
from jax import lax
from jax.experimental import pallas as pl
from jax.experimental.pallas import tpu as pltpu
from jax.sharding import PartitionSpec as P

SEQ_LEN = 2048
LANES = 128
TILE = 256
SIDE = 16
BLOCK = 1024
AXES = ("fsdp", "tensor")
norm_epsilon = 1e-05
GELU_SCALE = math.sqrt(2.0 / math.pi)
GELU_CUBE = 0.044715
F32 = jnp.float32
BF16 = jnp.bfloat16
MIB = 1024 * 1024


def log2(value):
    return value.bit_length() - 1


def flip(value, bit, count):
    return lax.ppermute(value, AXES, [(i, i ^ (1 << bit)) for i in range(count)])


def dot(left, right, left_dim=1, right_dim=0):
    return lax.dot_general(
        left, right, (((left_dim,), (right_dim,)), ((), ())), preferred_element_type=F32
    )


def fold_rows(value):
    rows, width = value.shape
    return jnp.sum(value.reshape(rows // 8, 8, width), axis=0)


def wide(mask, width):
    return jnp.concatenate([mask] * (width // LANES), axis=1)


def grid_index(dims, axis):
    return lax.broadcasted_iota(jnp.int32, dims, axis)


def regroup_matrix(states, shards):
    own = log2(states // shards)
    width = 2 * states
    source = grid_index((width, width), 0)
    target = grid_index((width, width), 1)
    part = (source >> own) & 1
    place = part * states + ((source >> (own + 1)) << own) + (source & ((1 << own) - 1))
    return jnp.where(place == target, 1.0, 0.0).astype(BF16)


def turn_matrix():
    source = grid_index((TILE, TILE), 0)
    target = grid_index((TILE, TILE), 1)
    bits = log2(SIDE)
    place = ((source & (SIDE - 1)) << bits) + (source >> bits)
    return jnp.where(place == target, 1.0, 0.0)


def turn_rows(turn, value):
    parts = [dot(turn, value[at : at + TILE]) for at in range(0, value.shape[0], TILE)]
    return jnp.concatenate(parts, axis=0).astype(BF16)


class Plan:
    def __init__(self, mesh, rows, group_rows, features, states, units):
        self.fsdp = mesh.shape["fsdp"]
        self.tensor = mesh.shape["tensor"]
        self.count = self.fsdp * self.tensor
        self.bits = log2(self.count)
        far = list(range(self.bits - 1, 3, -1))
        self.far = far
        self.up = [*far, 3, 2, 1, 0]
        self.up_crossed = ([*far, 1, 3, 2, 0], [*far, 1, 2, 3, 0])
        self.down = [0, 1, 2, 3, *far[::-1]]
        self.down_crossed = ([0, 2, 3, 1, *far[::-1]], [0, 3, 2, 1, *far[::-1]])
        self.halves = 2 if features // self.fsdp >= 32 else 1
        self.rows = rows
        self.group_rows = group_rows
        self.features = features
        self.states = states
        self.units = units
        self.own_states = states // self.tensor
        self.own_rows = features // self.fsdp
        self.pieces = SEQ_LEN // rows
        self.tiles = rows // TILE
        self.chunks = self.tiles * SIDE
        self.block = BLOCK if rows % BLOCK == 0 else TILE
        self.blocks = rows // self.block

    def slot_owner(self, slot, me, order):
        owner = me
        for place, bit in enumerate(order):
            owner = owner ^ (((slot >> (self.bits - 1 - place)) & 1) << bit)
        shift = log2(self.tensor)
        return owner >> shift, owner & (self.tensor - 1)

    def block_rows(self, index):
        return pl.ds(pl.multiple_of(index * self.block, self.block), self.block)


def step_rows(tile, place):
    return pl.ds(pl.multiple_of(tile * TILE + place * SIDE, SIDE), SIDE)


def scan_pass(plan, keep_ref, start, extra, reverse, visit):
    def step(index, carried):
        now, extra = carried
        place = SIDE - 1 - index if reverse else index
        after = []
        for tile in range(plan.tiles):
            at = step_rows(tile, place)
            state, extra = visit(tile, at, keep_ref[at, :], now[tile], extra)
            after.append(state)
        return after, extra

    return lax.fori_loop(0, SIDE, step, (start, extra), unroll=2)


def local_ends(plan, source_ref, keep_ref, rate, reverse):
    states = plan.states
    zero = jnp.zeros((SIDE, states), F32)
    rate_re = jnp.broadcast_to(rate[0], zero.shape)
    rate_im = jnp.broadcast_to(rate[1], zero.shape)
    one = jnp.ones((SIDE, LANES), F32)

    def visit(tile, at, keep, state, extra):
        now_re, now_im, hold = state
        held = wide(keep, states)
        pass_re, pass_im = held * rate_re, held * rate_im
        source = source_ref[at, :]
        next_re = (source[:, :states] + pass_re * now_re) - pass_im * now_im
        next_im = (source[:, states:] + pass_re * now_im) + pass_im * now_re
        return (next_re, next_im, hold * keep), extra

    ends, _ = scan_pass(plan, keep_ref, [(zero, zero, one)] * plan.tiles, 0, reverse, visit)
    return tuple(jnp.concatenate([end[part] for end in ends], axis=0) for part in range(3))


def shifted(value, distance, reverse):
    count = value.shape[0]
    row = grid_index(value.shape, 0)
    if reverse:
        moved = pltpu.roll(value, count - distance, 0)
        return jnp.where(row < count - distance, moved, 0.0)
    moved = pltpu.roll(value, distance, 0)
    return jnp.where(row >= distance, moved, 0.0)


def chunk_entries(plan, ends_re, ends_im, hold, rate, start, reverse):
    states, count = plan.states, plan.chunks
    power_re, power_im = rate
    for _ in range(log2(SIDE)):
        power_re, power_im = power_re * power_re - power_im * power_im, 2.0 * power_re * power_im
    first = count - 1 if reverse else 0
    if start is not None:
        at_first = grid_index((count, states), 0) == first
        held = jnp.where(at_first, wide(hold, states), 0.0)
        pass_re, pass_im = held * power_re, held * power_im
        ends_re = ends_re + (pass_re * start[0] - pass_im * start[1])
        ends_im = ends_im + (pass_re * start[1] + pass_im * start[0])
    distance = 1
    while distance < count:
        earlier_re = shifted(ends_re, distance, reverse)
        earlier_im = shifted(ends_im, distance, reverse)
        held = wide(hold, states)
        pass_re, pass_im = held * power_re, held * power_im
        ends_re = ends_re + (pass_re * earlier_re - pass_im * earlier_im)
        ends_im = ends_im + (pass_re * earlier_im + pass_im * earlier_re)
        hold = hold * shifted(hold, distance, reverse)
        power_re, power_im = power_re * power_re - power_im * power_im, 2.0 * power_re * power_im
        distance *= 2
    last = slice(0, 1) if reverse else slice(count - 1, count)
    leaving = jnp.concatenate([ends_re[last], ends_im[last]], axis=1)
    if start is None:
        return None, leaving
    entry_re = shifted(ends_re, 1, reverse) + jnp.where(at_first, start[0], 0.0)
    entry_im = shifted(ends_im, 1, reverse) + jnp.where(at_first, start[1], 0.0)
    entries = []
    for tile in range(plan.tiles):
        at = slice(tile * SIDE, (tile + 1) * SIDE)
        entries.append((entry_re[at], entry_im[at]))
    return entries, leaving


def block_places(plan, me, order, refs, base, rows, start):
    slot = 0
    for ref in refs:
        for place in range(plan.count // 2):
            band, shard = plan.slot_owner(slot, me, order)
            slot += 1
            first = pl.multiple_of(band * plan.own_rows + start, rows)
            yield ref, base + place * rows, pl.ds(first, rows), shard


def collect(plan, me, order, refs, base, rows, start, targets):
    for ref, row, at, shard in block_places(plan, me, order, refs, base, rows, start):
        for first, width, out_ref, lanes in targets:
            column = pl.multiple_of(lanes + shard * width, LANES)
            out_ref[at, pl.ds(column, width)] = ref[row : row + rows, first : first + width].astype(
                out_ref.dtype
            )


def distribute(plan, me, order, refs, base, rows, start, targets):
    for ref, row, at, shard in block_places(plan, me, order, refs, base, rows, start):
        for first, width, full_ref, lanes in targets:
            column = pl.multiple_of(lanes + shard * width, LANES)
            ref[row : row + rows, first : first + width] = full_ref[at, pl.ds(column, width)].astype(
                ref.dtype
            )


def half_blocks(plan, orders):
    rows = plan.own_rows // plan.halves
    for half in range(plan.halves):
        yield orders[half], half * plan.count // 2 * rows, rows, half * rows


def start_copies(pairs, sems):
    copies = [
        pltpu.make_async_copy(source, target, sems.at[place])
        for place, (source, target) in enumerate(pairs)
    ]
    for copy in copies:
        copy.start()
    return copies


def pack_kernel(plan, me_ref, *refs):
    sources, outs, held, sems = refs[:14], refs[14:16], refs[16:30], refs[30]
    copies = start_copies(list(zip(sources, held)), sems)
    first_ref, second_ref = outs
    band = me_ref[0] >> log2(plan.tensor)
    rows, features = plan.own_rows, plan.features
    for copy in copies:
        copy.wait()
    first_ref[:rows, :] = jnp.concatenate([held[0][...], held[1][...]], axis=1)
    second_ref[...] = jnp.concatenate([ref[...] for ref in held[2:6]], axis=1)
    placed = []
    lane = grid_index((1, features), 1)
    for ref in held[6:]:
        length = ref.shape[1]
        value = ref[...].astype(F32)
        value = jnp.concatenate([value] * (features // length), axis=1)
        placed.append(jnp.where((lane >> log2(length)) == band, value, 0.0))
    placed = jnp.concatenate(placed, axis=0).astype(BF16)
    for part in range(features // LANES):
        first_ref[rows + 8 * part : rows + 8 * part + 8, :] = placed[
            :, part * LANES : (part + 1) * LANES
        ]


def token_kernel(plan, me_ref, x_ref, segments_ref, stats_ref, masks_ref, flags_ref):
    shard = me_ref[0] & (plan.tensor - 1)
    ids = segments_ref[...]
    count = ids.shape[0]
    lane = grid_index(ids.shape, 1)
    position = (grid_index(ids.shape, 0) * LANES + lane) & (SEQ_LEN - 1)
    turned = pltpu.roll(ids, 1, 1)
    before = jnp.where(lane == 0, pltpu.roll(turned, 1, 0), turned)
    turned = pltpu.roll(ids, LANES - 1, 1)
    after = jnp.where(lane == LANES - 1, pltpu.roll(turned, count - 1, 0), turned)
    flags_ref[0] = jnp.where((position > 0) & (ids == before), 1.0, 0.0)
    flags_ref[1] = jnp.where((position < SEQ_LEN - 1) & (ids == after), 1.0, 0.0)
    flags_ref[2] = jnp.where(ids > 0, 1.0, 0.0)
    turn = turn_matrix()
    plain = jnp.where(grid_index((TILE, TILE), 0) == grid_index((TILE, TILE), 1), 1.0, 0.0)
    ones = jnp.ones((TILE, LANES), BF16)
    per_tile = TILE // LANES
    own = plan.rows // LANES
    flags = [flags_ref[kind, pl.ds(pl.multiple_of(shard * own, own), own), :] for kind in range(3)]
    for tile in range(plan.tiles):
        at = slice(tile * TILE, (tile + 1) * TILE)
        for kind in range(4):
            rows = flags[min(kind, 2)][tile * per_tile : (tile + 1) * per_tile, :]
            line = jnp.concatenate([rows[part : part + 1, :] for part in range(per_tile)], axis=1)
            spread = (plain if kind == 3 else turn) * line
            masks_ref[kind, at, :] = dot(spread.astype(BF16), ones)

    def rows_step(index, _):
        at = plan.block_rows(index)
        values = x_ref[at, :].astype(F32)
        mean = jnp.mean(values, axis=1, keepdims=True)
        centred = values - mean
        inverse = lax.rsqrt(jnp.mean(centred * centred, axis=1, keepdims=True) + norm_epsilon)
        stats_ref[0, at, :] = jnp.broadcast_to(mean, (plan.block, LANES))
        stats_ref[1, at, :] = jnp.broadcast_to(inverse, (plan.block, LANES))
        return 0

    lax.fori_loop(0, plan.blocks, rows_step, 0)


def standard_rows(plan, x_ref, stats_ref, at):
    mean = wide(stats_ref[0, at, :], plan.features)
    inverse = wide(stats_ref[1, at, :], plan.features)
    return (x_ref[at, :].astype(F32) - mean) * inverse, inverse


def read_vectors(vec_ref):
    count = vec_ref.shape[0] // 8
    parts = [vec_ref[8 * part : 8 * part + 8, :].astype(F32) for part in range(count)]
    return jnp.concatenate(parts, axis=1)


def received(carry_ref, wanted, states):
    value = jnp.where(wanted, carry_ref[0:1, :], 0.0)
    return value[:, :states], value[:, states:]


def enter_kernel(
    plan, me_ref, x_ref, stats_ref, b0_ref, b1_ref, vec_ref, masks_ref,
    normed_ref, source_ref, ends_ref, hold_ref, carry_ref, input_map_ref, params_ref,
    pack_ref,
):
    states = plan.states
    collect(
        plan, me_ref[0], plan.up[::-1], (b0_ref, b1_ref), 0, plan.own_rows, 0,
        [(0, 2 * plan.own_states, pack_ref, 0)],
    )
    input_map_ref[...] = dot(
        pack_ref[...].astype(BF16), regroup_matrix(states, plan.tensor)
    ).astype(BF16)
    vectors = read_vectors(vec_ref)
    gain, shift = vectors[0:1], vectors[1:2]
    speed = jnp.exp(vectors[5:6, :states])
    modulus = jnp.exp(-speed)
    rotation = jnp.exp(vectors[6:7, :states])
    rate = (modulus * jnp.cos(rotation), modulus * jnp.sin(rotation))
    rest = 1.0 - modulus * modulus
    gamma = jnp.exp(vectors[7:8, :states]) * jnp.sqrt(rest)
    params_ref[...] = jnp.concatenate(
        [
            jnp.concatenate(rate, axis=1),
            jnp.concatenate([gamma, speed], axis=1),
            jnp.concatenate([modulus, rest], axis=1),
            jnp.concatenate([rotation, rotation], axis=1),
            jnp.zeros((4, 2 * states), F32),
        ],
        axis=0,
    )
    gamma_pair = jnp.concatenate([gamma, gamma], axis=1)
    turn = turn_matrix().astype(BF16)

    def rows_step(index, _):
        at = plan.block_rows(index)
        standard, _ = standard_rows(plan, x_ref, stats_ref, at)
        normed = (standard * gain + shift).astype(BF16)
        normed_ref[at, :] = normed
        turned = turn_rows(turn, normed)
        drive = dot(turned, input_map_ref[...])
        source_ref[at, :] = drive * gamma_pair * wide(masks_ref[2, at, :], 2 * states)
        return 0

    lax.fori_loop(0, plan.blocks, rows_step, 0)
    ends_re, ends_im, hold = local_ends(plan, source_ref, masks_ref.at[0], rate, False)
    ends_ref[...] = jnp.concatenate([ends_re, ends_im], axis=1)
    hold_ref[...] = hold
    _, leaving = chunk_entries(plan, ends_re, ends_im, hold, rate, None, False)
    carry_ref[...] = jnp.broadcast_to(leaving, carry_ref.shape)


def middle_kernel(
    plan, me_ref, x_ref, grad_ref, normed_ref, source_ref, ends_ref, hold_ref, carry_ref,
    g0_ref, g1_ref, vec_ref, params_ref, masks_ref,
    mixed_ref, hidden_ref, lru_grad_ref, state_grad_ref, act_ref, unit_grad_ref, low_ref, sums_ref,
    pack_ref, wpack_ref, out_map_ref,
):
    states, features, units = plan.states, plan.features, plan.units
    pair = 2 * plan.own_states
    targets = [
        (0, pair, pack_ref, 0),
        (pair, units, wpack_ref, 0),
        (pair + units, units, wpack_ref, features),
    ]
    for order, base, rows, first in half_blocks(plan, plan.up_crossed):
        collect(plan, me_ref[0], order[::-1], (g0_ref, g1_ref), base, rows, first, targets)
    sign = jnp.where(grid_index((1, 2 * states), 1) < states, 1.0, -1.0)
    regroup = regroup_matrix(states, plan.tensor)
    out_map_ref[...] = (dot(pack_ref[...].astype(BF16), regroup) * sign).astype(BF16)
    rate = (params_ref[0:1, :states], params_ref[0:1, states:])
    start = received(carry_ref, me_ref[0] & 1 == 1, states)
    entries, _ = chunk_entries(
        plan, ends_ref[:, :states], ends_ref[:, states:], hold_ref[...], rate, start, False
    )
    rate_re = jnp.broadcast_to(rate[0], (SIDE, states))
    rate_im = jnp.broadcast_to(rate[1], (SIDE, states))

    def visit(tile, at, keep, state, extra):
        now_re, now_im = state
        held = wide(keep, states)
        pass_re, pass_im = held * rate_re, held * rate_im
        source = source_ref[at, :]
        next_re = (source[:, :states] + pass_re * now_re) - pass_im * now_im
        next_im = (source[:, states:] + pass_re * now_im) + pass_im * now_re
        hidden_ref[at, :states] = next_re
        hidden_ref[at, states:] = next_im
        return (next_re, next_im), extra

    scan_pass(plan, masks_ref.at[0], entries, 0, False, visit)
    vectors = read_vectors(vec_ref)
    skip = vectors[2:3]
    biases = jnp.concatenate([vectors[3:4], vectors[4:5]], axis=1)
    sums_ref[...] = jnp.zeros_like(sums_ref)
    turn = turn_matrix().astype(BF16)

    def rows_step(index, _):
        at = plan.block_rows(index)
        low = turn_rows(turn, hidden_ref[at, :].astype(BF16))
        low_ref[at, :] = low
        normed = normed_ref[at, :].astype(F32)
        lru = dot(low, out_map_ref[...], 1, 1) + skip * normed
        square = lru * lru
        bent = jnp.tanh(lru * (GELU_SCALE + (GELU_SCALE * GELU_CUBE) * square))
        half = 0.5 + 0.5 * bent
        act_wide = lru * half
        slope = half + act_wide * (1.0 - half) * (
            2.0 * GELU_SCALE + (6.0 * GELU_SCALE * GELU_CUBE) * square
        )
        act = act_wide.astype(BF16)
        act_ref[at, :] = act
        mapped = dot(act, wpack_ref[...].astype(BF16)) + biases
        value = mapped[:, :features]
        live_half = wide(0.5 * masks_ref[3, at, :], features)
        opening = live_half + live_half * jnp.tanh(0.5 * mapped[:, features:])
        gated = value * opening
        mixed_ref[at, :] = (x_ref[at, :].astype(F32) + gated).astype(BF16)
        value_grad = grad_ref[at, :].astype(F32) * opening
        gate_grad = value_grad * (value - gated)
        sums_ref[8:16, :] += fold_rows(value_grad)
        sums_ref[16:24, :] += fold_rows(gate_grad)
        unit_grad = jnp.concatenate([value_grad, gate_grad], axis=1).astype(BF16)
        unit_grad_ref[at, :] = unit_grad
        act_grad = dot(unit_grad, wpack_ref[...].astype(BF16), 1, 1)
        lru_grad = act_grad * slope
        sums_ref[0:8, :] += fold_rows(lru_grad * normed)
        lru_grad = lru_grad.astype(BF16)
        lru_grad_ref[at, :] = lru_grad
        turned = turn_rows(turn, lru_grad)
        state_grad_ref[at, :] = dot(turned, out_map_ref[...])
        return 0

    lax.fori_loop(0, plan.blocks, rows_step, 0)


def back_kernel(
    plan, me_ref, state_grad_ref, params_ref, masks_ref, back_ends_ref, back_hold_ref, back_ref
):
    states = plan.states
    back_rate = (params_ref[0:1, :states], -params_ref[0:1, states:])
    ends_re, ends_im, hold = local_ends(plan, state_grad_ref, masks_ref.at[1], back_rate, True)
    back_ends_ref[...] = jnp.concatenate([ends_re, ends_im], axis=1)
    back_hold_ref[...] = hold
    _, leaving = chunk_entries(plan, ends_re, ends_im, hold, back_rate, None, True)
    back_ref[...] = jnp.broadcast_to(leaving, back_ref.shape)


def weight_kernel(
    plan, me_ref, act_ref, unit_grad_ref, lru_grad_ref, low_ref, keep_ref, send_ref, full_ref, out_ref
):
    states, features, units = plan.states, plan.features, plan.units
    pair = 2 * plan.own_states
    sign = jnp.where(grid_index((1, 2 * states), 1) < states, 1.0, -1.0)
    full_ref[...] = dot(act_ref[...], unit_grad_ref[...], 0, 0)
    out_grad = dot(lru_grad_ref[...], low_ref[...], 0, 0) * sign
    out_ref[...] = dot(out_grad.astype(BF16), regroup_matrix(states, plan.tensor), 1, 1)
    targets = [
        (0, pair, out_ref, 0),
        (pair, units, full_ref, 0),
        (pair + units, units, full_ref, features),
    ]
    for order, base, rows, first in half_blocks(plan, plan.down_crossed):
        distribute(plan, me_ref[0], order, (keep_ref, send_ref), base, rows, first, targets)


def leave_kernel(
    plan, me_ref, x_ref, stats_ref, normed_ref, source_ref, ends_ref, hold_ref, carry_ref, hidden_ref,
    state_grad_ref, lru_grad_ref, input_map_ref, vec_ref, params_ref, masks_ref, sums_ref,
    keep_ref, send_ref, normed_grad_ref,
    drive_grad_ref, low_ref, full_ref,
):
    states, features = plan.states, plan.features
    params = params_ref[...]
    rate = (params[0:1, :states], params[0:1, states:])
    gamma, speed = params[1:2, :states], params[1:2, states:]
    modulus, rest = params[2:3, :states], params[2:3, states:]
    rotation = params[3:4, :states]
    back_rate = (rate[0], -rate[1])
    start = received(carry_ref, me_ref[0] & 1 == 0, states)
    entries, _ = chunk_entries(
        plan, ends_ref[:, :states], ends_ref[:, states:], hold_ref[...], back_rate, start, True
    )
    zero = jnp.zeros((SIDE, states), F32)
    rate_re = jnp.broadcast_to(back_rate[0], zero.shape)
    rate_im = jnp.broadcast_to(back_rate[1], zero.shape)
    gamma_wide = jnp.broadcast_to(gamma, zero.shape)

    def visit(tile, at, keep, state, sums):
        now_re, now_im = state
        held = wide(keep, states)
        next_re, next_im = held * now_re, held * now_im
        hidden_re, hidden_im = hidden_ref[at, :states], hidden_ref[at, states:]
        now_re = (state_grad_ref[at, :states] + rate_re * next_re) - rate_im * next_im
        now_im = (state_grad_ref[at, states:] + rate_re * next_im) + rate_im * next_re
        sums = (
            sums[0] + (hidden_re * next_re + hidden_im * next_im),
            sums[1] + (hidden_re * next_im - hidden_im * next_re),
            sums[2] + (source_ref[at, :states] * now_re + source_ref[at, states:] * now_im),
        )
        scale = gamma_wide * wide(masks_ref[2, at, :], states)
        drive_grad_ref[at, :states] = scale * now_re
        drive_grad_ref[at, states:] = scale * now_im
        return (now_re, now_im), sums

    _, sums = scan_pass(plan, masks_ref.at[1], entries, (zero, zero, zero), True, visit)
    rate_sum_re, rate_sum_im, gamma_sum = (jnp.sum(part, axis=0, keepdims=True) for part in sums)
    nu_grad = speed * (
        gamma_sum * modulus * modulus / rest - (rate_sum_re * rate[0] + rate_sum_im * rate[1])
    )
    theta_grad = rotation * (rate_sum_im * rate[0] - rate_sum_re * rate[1])
    vectors = read_vectors(vec_ref)
    skip = vectors[2:3]
    gain_sum = jnp.zeros((8, features), F32)
    turn = turn_matrix().astype(BF16)

    def rows_step(index, sums):
        gain_sum, shift_sum = sums
        at = plan.block_rows(index)
        low = turn_rows(turn, drive_grad_ref[at, :].astype(BF16))
        low_ref[at, :] = low
        normed_grad = dot(low, input_map_ref[...], 1, 1) + skip * lru_grad_ref[at, :].astype(F32)
        normed_grad_ref[at, :] = normed_grad
        standard, _ = standard_rows(plan, x_ref, stats_ref, at)
        return gain_sum + fold_rows(normed_grad * standard), shift_sum + fold_rows(normed_grad)

    gain_sum, shift_sum = lax.fori_loop(0, plan.blocks, rows_step, (gain_sum, gain_sum))
    into = dot(normed_ref[...], low_ref[...], 0, 0)
    full_ref[...] = dot(into.astype(BF16), regroup_matrix(states, plan.tensor), 1, 1)
    distribute(
        plan, me_ref[0], plan.down, (keep_ref, send_ref), 0, plan.own_rows, 0,
        [(0, 2 * plan.own_states, full_ref, 0)],
    )
    empty = jnp.zeros((1, features - states), F32)
    vector_sums = jnp.concatenate(
        [jnp.sum(part, axis=0, keepdims=True) for part in (gain_sum, shift_sum)]
        + [
            jnp.sum(sums_ref[8 * place : 8 * place + 8, :], axis=0, keepdims=True)
            for place in range(3)
        ]
        + [jnp.concatenate([part, empty], axis=1) for part in (nu_grad, theta_grad, gamma_sum)],
        axis=0,
    )
    base = plan.own_rows * plan.count // 2
    parts = features // LANES
    for part in range(parts):
        piece = vector_sums[:, part * LANES : (part + 1) * LANES]
        high = piece.astype(BF16)
        low = (piece - high.astype(F32)).astype(BF16)
        send_ref[base + 8 * part : base + 8 * part + 8, :] = high
        send_ref[base + 8 * (parts + part) : base + 8 * (parts + part) + 8, :] = low


def last_kernel(plan, me_ref, *refs):
    b_keep, b_other, w_mine_ref, tail_ref = refs[:4]
    outs, held, sems = refs[4:18], refs[18:32], refs[32]
    own, units = plan.own_states, plan.units
    b_mine = b_keep[...].astype(F32) + b_other[...].astype(F32)
    w_mine = w_mine_ref[...]
    half = tail_ref.shape[0] // 4
    tail = [tail_ref[part * half : part * half + half, :].astype(F32) for part in range(4)]
    vectors = (tail[0] + tail[1]) + (tail[2] + tail[3])
    count = half // 8
    vectors = jnp.concatenate([vectors[8 * part : 8 * part + 8] for part in range(count)], axis=1)
    band = me_ref[0] >> log2(plan.tensor)
    at = grid_index((plan.features, LANES), 0)
    lane = grid_index((plan.features, LANES), 1)

    def pick(length):
        chosen = jnp.where(at == band * length + lane, 1.0, 0.0)
        return lax.dot_general(
            vectors,
            chosen,
            (((1,), (0,)), ((), ())),
            precision=lax.Precision.HIGHEST,
            preferred_element_type=F32,
        )

    long, short = plan.own_rows, plan.states // plan.fsdp
    long_part, short_part = pick(long), pick(short)
    held[0][...] = b_mine[:, :own]
    held[1][...] = b_mine[:, own:]
    held[2][...] = w_mine[:, :own]
    held[3][...] = w_mine[:, own : 2 * own]
    held[4][...] = w_mine[:, 2 * own : 2 * own + units]
    held[5][...] = w_mine[:, 2 * own + units :]
    for place in range(8):
        part, length = (long_part, long) if place < 5 else (short_part, short)
        held[6 + place][...] = part[place : place + 1, :length]
    for copy in start_copies(list(zip(held, outs)), sems):
        copy.wait()


def input_kernel(plan, me_ref, x_ref, stats_ref, grad_ref, normed_grad_ref, vec_ref, input_grad_ref):
    gain = read_vectors(vec_ref)[0:1]

    def rows_step(index, _):
        at = plan.block_rows(index)
        standard, inverse = standard_rows(plan, x_ref, stats_ref, at)
        scaled = normed_grad_ref[at, :] * gain
        input_grad_ref[at, :] = grad_ref[at, :].astype(F32) + inverse * (
            scaled
            - jnp.mean(scaled, axis=1, keepdims=True)
            - standard * jnp.mean(scaled * standard, axis=1, keepdims=True)
        )
        return 0

    lax.fori_loop(0, plan.blocks, rows_step, 0)


def call(kernel, plan, outs, scratch, limit, time, *args, far_in=0, far_out=False):
    args = [*args[:1], *(pltpu.with_memory_space_constraint(a, pltpu.HBM) for a in args[1 : 1 + far_in]), *args[1 + far_in :]]
    whole = pl.BlockSpec(memory_space=pltpu.VMEM)
    far = pl.BlockSpec(memory_space=pltpu.HBM)
    return pl.pallas_call(
        functools.partial(kernel, plan),
        out_shape=outs,
        in_specs=[pl.BlockSpec(memory_space=pltpu.SMEM)]
        + [far] * far_in
        + [whole] * (len(args) - 1 - far_in),
        out_specs=[far if far_out else whole] * len(outs),
        scratch_shapes=scratch,
        compiler_params=pltpu.CompilerParams(vmem_limit_bytes=limit * MIB),
        cost_estimate=pl.CostEstimate(
            flops=int(time * 1e9), bytes_accessed=int(time * 3.5e6), transcendentals=0
        ),
    )(*args)


def shape(dims, dtype=F32):
    return jax.ShapeDtypeStruct(dims, dtype)


def after(value, *others):
    return lax.optimization_barrier((value, *others))[0]


def joined(*parts):
    return jnp.concatenate(parts, axis=0)


def gather_blocks(plan, first, summed, second, cover):
    count, width = plan.count, second.shape[1]
    tensor_bits = log2(plan.tensor)
    other = None

    def first_step(bit):
        rows = first.shape[0]
        if bit < tensor_bits:
            got = flip(first, bit, count)
            return got, joined(first, got), summed
        got = flip(joined(first, summed), bit, count)
        if other is None:
            got = after(got, cover, second_other)
        return got, joined(first, got[:rows]), summed + got[rows:]

    for bit in plan.far:
        second_other = flip(second if other is None else after(second, other), bit, count)
        other, first, summed = first_step(bit)
        second = joined(second, second_other)
    second = joined(second, flip(after(second, other), 1, count))
    other, first, summed = first_step(3)
    blocks = second.reshape(-1, plan.own_rows, width)
    size = plan.own_rows // plan.halves
    halves = [
        after(blocks[:, half * size : half * size + size].reshape(-1, width), other)
        for half in range(plan.halves)
    ]
    halves = [joined(part, flip(part, bit, count)) for part, bit in zip(halves, (3, 2))]
    other, first, summed = first_step(2)
    halves = [(part, flip(part, bit, count)) for part, bit in zip(halves, (2, 3))]
    other, first, summed = first_step(1)
    return first, flip(first, 0, count), summed, halves


def split_high_low(value):
    high = lax.reduce_precision(value, 8, 7)
    return jnp.concatenate([high, value - high], axis=0).astype(BF16)


def cut(value):
    count = value.shape[0] // 2
    return value[:count].astype(BF16), value[count:].astype(BF16)


def added(keep, other):
    return keep.astype(F32) + other.astype(F32)


def summed_step(keep, send, other):
    count = keep.shape[0]
    rows = (send.shape[0] - count) // 2
    pairs = [part[count:].astype(F32) for part in (send, other)]
    summed = sum(pair[:rows] + pair[rows:] for pair in pairs)
    keep, send = cut(added(keep, other[:count]))
    return keep, joined(send, split_high_low(summed))


def together(*values):
    return lax.optimization_barrier(values)


def shards(
    mesh,
    block_input,
    segments,
    ln_gain,
    ln_bias,
    b_real,
    b_imag,
    c_real,
    c_imag,
    nu_log,
    theta_log,
    gamma_log,
    d_skip,
    w_value,
    w_gate,
    b_value,
    b_gate,
    out_grad,
):
    band = lax.axis_index("fsdp")
    shard = lax.axis_index("tensor")
    rows, features = block_input.shape
    own = b_real.shape[1]
    plan = Plan(
        mesh, rows, segments.shape[0], features, own * mesh.shape["tensor"], w_value.shape[1]
    )
    states, units, chunks = plan.states, plan.units, plan.chunks
    me = (band * plan.tensor + shard).astype(jnp.int32).reshape(1)
    long, short = plan.own_rows, states // plan.fsdp
    vector_rows = 8 * features // LANES
    matrices = (b_real, b_imag, c_real, c_imag, w_value, w_gate)
    lines = [
        v.reshape(1, -1)
        for v in (ln_gain, ln_bias, d_skip, b_value, b_gate, nu_log, theta_log, gamma_log)
    ]
    block = 2 * own + 2 * units
    first, second = call(
        pack_kernel,
        plan,
        [shape((long + vector_rows, 2 * own), BF16), shape((long, block), BF16)],
        [pltpu.VMEM(v.shape, BF16) for v in (*matrices, *lines)] + [pltpu.SemaphoreType.DMA((14,))],
        4,
        1.5,
        me, *matrices, *lines,
        far_in=14,
    )
    stats, masks = call(
        token_kernel,
        plan,
        [shape((2, rows, LANES)), shape((4, rows, LANES))],
        [pltpu.VMEM((3, plan.group_rows // LANES, LANES), F32)],
        8,
        2,
        me, block_input, segments.reshape(-1, LANES),
    )
    b0, b1, vectors, halves = gather_blocks(plan, first[:long], first[long:], second, masks)

    pack_type = BF16 if long % 16 == 0 else F32
    full = (rows, 2 * states)
    normed, source, ends, hold, carry, input_map, params = call(
        enter_kernel,
        plan,
        [
            shape((rows, features), BF16),
            shape(full),
            shape((chunks, 2 * states)),
            shape((chunks, LANES)),
            shape((8, 2 * states)),
            shape((features, 2 * states), BF16),
            shape((8, 2 * states)),
        ],
        [pltpu.VMEM((features, 2 * states), pack_type)],
        8,
        0.3,
        me, block_input, stats, b0, b1, vectors, masks,
    )

    left = carry
    carry = flip(carry, 0, plan.count) if plan.pieces == 2 else jnp.zeros_like(carry)
    g0 = joined(*(joined(part, after(got, left)) for part, got in halves))
    g1 = flip(g0, 0, plan.count)
    (
        mixed, hidden, lru_grad, state_grad, act, unit_grad, low, sums,
    ) = call(
        middle_kernel,
        plan,
        [
            shape((rows, features), BF16),
            shape(full),
            shape((rows, features), BF16),
            shape(full),
            shape((rows, features), BF16),
            shape((rows, 2 * features), BF16),
            shape(full, BF16),
            shape((24, features)),
        ],
        [
            pltpu.VMEM((features, 2 * states), pack_type),
            pltpu.VMEM((features, 2 * features), pack_type),
            pltpu.VMEM((features, 2 * states), BF16),
        ],
        24,
        10,
        me, block_input, out_grad, normed, source, ends, hold, carry, g0, g1, vectors, params, masks,
    )
    half_rows = plan.count // 2 * long
    w_keep, w_send = call(
        weight_kernel,
        plan,
        [shape((half_rows, block), BF16)] * 2,
        [
            pltpu.VMEM((features, 2 * features), F32),
            pltpu.VMEM((features, 2 * states), F32),
        ],
        10,
        2.5,
        me, act, unit_grad, lru_grad, low,
    )
    w_other = flip(w_send, 0, plan.count)
    back_ends, back_hold, back = call(
        back_kernel,
        plan,
        [shape((chunks, 2 * states)), shape((chunks, LANES)), shape((8, 2 * states))],
        [],
        8,
        1,
        me, after(state_grad, w_send), params, masks,
    )
    back = flip(back, 0, plan.count) if plan.pieces == 2 else jnp.zeros_like(back)
    pieces = plan.halves
    w_total = added(w_keep, after(w_other, back_ends))
    size = w_total.shape[0] // pieces
    halves = [cut(w_total[half * size : half * size + size]) for half in range(pieces)]
    w_others = [flip(half[1], bit, plan.count) for half, bit in zip(halves, (2, 3))]
    back_ends = after(back_ends, *(half[1] for half in halves))
    b_keep, b_send, normed_grad = call(
        leave_kernel,
        plan,
        [
            shape((half_rows, 2 * own), BF16),
            shape((half_rows + 2 * vector_rows, 2 * own), BF16),
            shape((rows, features)),
        ],
        [
            pltpu.VMEM(full, F32),
            pltpu.VMEM(full, BF16),
            pltpu.VMEM((features, 2 * states), F32),
        ],
        14,
        4.5,
        me, block_input, stats, normed, source, back_ends, back_hold, back, hidden,
        state_grad, lru_grad, input_map, vectors, params, masks, sums,
    )
    w_others = [after(other, b_keep) for other in w_others]
    halves = [cut(added(half[0], other)) for half, other in zip(halves, w_others)]
    b_other = after(flip(b_send, 0, plan.count), *(half[1] for half in halves))
    b_keep, b_send = summed_step(b_keep, b_send, b_other)
    b_other = flip(b_send, 1, plan.count)
    w_others = [flip(half[1], bit, plan.count) for half, bit in zip(halves, (3, 2))]
    (input_grad,) = call(
        input_kernel,
        plan,
        [shape((rows, features))],
        [],
        8,
        2.5,
        me, block_input, stats, out_grad, after(normed_grad, b_send), vectors,
    )
    b_other = after(b_other, input_grad)
    b_keep, b_send = summed_step(b_keep, b_send, b_other)
    halves = [cut(added(half[0], after(other, b_send))) for half, other in zip(halves, w_others)]
    w_keep = joined(*(half[0] for half in halves))
    w_send = joined(*(half[1] for half in halves))
    for bit in range(2, plan.bits - 1):
        w_bit = 1 if bit == 2 else bit + 1
        b_other = flip(b_send, bit, plan.count)
        w_other = flip(w_send, w_bit, plan.count)
        b_keep, b_send = summed_step(b_keep, b_send, b_other)
        if w_bit < plan.bits - 1:
            w_other = after(w_other, b_send)
            total = added(w_keep, w_other).reshape(pieces, -1, block)
            size = total.shape[1] // 2
            w_keep = total[:, :size].reshape(-1, block).astype(BF16)
            w_send = total[:, size:].reshape(-1, block).astype(BF16)
    w_mine = added(w_keep, w_other)
    b_other = after(flip(b_send, plan.bits - 1, plan.count), w_mine)
    b_other, tail = b_other[:long], joined(b_send[long:], b_other[long:])
    small = (
        [(long, own)] * 4 + [(long, units)] * 2 + [(1, long)] * 5 + [(1, short)] * 3
    )
    (
        b_real_grad, b_imag_grad, c_real_grad, c_imag_grad, value_grad, gate_grad, *lines
    ) = call(
        last_kernel,
        plan,
        [shape(dims) for dims in small],
        [pltpu.VMEM(dims, F32) for dims in small] + [pltpu.SemaphoreType.DMA((14,))],
        4,
        2,
        me, b_keep, b_other, w_mine, tail,
        far_out=True,
    )
    gain_grad, bias_grad, skip_grad, value_line, gate_line, nu_grad, theta_grad, gamma_grad = (
        line.reshape(-1) for line in lines
    )
    return (
        mixed,
        input_grad,
        gain_grad,
        bias_grad,
        b_real_grad,
        b_imag_grad,
        c_real_grad,
        c_imag_grad,
        nu_grad,
        theta_grad,
        gamma_grad,
        skip_grad,
        value_grad,
        gate_grad,
        value_line,
        gate_line,
    )


def solution(mesh):
    in_specs = (
        P(("fsdp", "tensor"), None),
        P("fsdp"),
        P("fsdp"),
        P("fsdp"),
        P("fsdp", "tensor"),
        P("fsdp", "tensor"),
        P("fsdp", "tensor"),
        P("fsdp", "tensor"),
        P("fsdp"),
        P("fsdp"),
        P("fsdp"),
        P("fsdp"),
        P("fsdp", "tensor"),
        P("fsdp", "tensor"),
        P("fsdp"),
        P("fsdp"),
        P(("fsdp", "tensor"), None),
    )
    out_specs = (
        P(("fsdp", "tensor"), None),
        P(("fsdp", "tensor"), None),
        P("fsdp"),
        P("fsdp"),
        P("fsdp", "tensor"),
        P("fsdp", "tensor"),
        P("fsdp", "tensor"),
        P("fsdp", "tensor"),
        P("fsdp"),
        P("fsdp"),
        P("fsdp"),
        P("fsdp"),
        P("fsdp", "tensor"),
        P("fsdp", "tensor"),
        P("fsdp"),
        P("fsdp"),
    )
    return jax.shard_map(
        functools.partial(shards, mesh),
        mesh=mesh,
        in_specs=in_specs,
        out_specs=out_specs,
        check_vma=False,
    )
```

```python
import functools
import math

import jax
import jax.numpy as jnp
from jax import lax
from jax.experimental import pallas as pl
from jax.experimental.pallas import tpu as pltpu
from jax.sharding import PartitionSpec as P

SEQ_LEN = 2048
LANES = 128
TILE = 256
SIDE = 16
BLOCK = 1024
AXES = ("fsdp", "tensor")
norm_epsilon = 1e-05
GELU_SCALE = math.sqrt(2.0 / math.pi)
GELU_CUBE = 0.044715
F32 = jnp.float32
BF16 = jnp.bfloat16
MIB = 1024 * 1024


def log2(value):
    return value.bit_length() - 1


def flip(value, bit, count):
    return lax.ppermute(value, AXES, [(i, i ^ (1 << bit)) for i in range(count)])


def dot(left, right, left_dim=1, right_dim=0):
    return lax.dot_general(
        left, right, (((left_dim,), (right_dim,)), ((), ())), preferred_element_type=F32
    )


def fold_rows(value):
    rows, width = value.shape
    return jnp.sum(value.reshape(rows // 8, 8, width), axis=0)


def wide(mask, width):
    return jnp.concatenate([mask] * (width // LANES), axis=1)


def grid_index(dims, axis):
    return lax.broadcasted_iota(jnp.int32, dims, axis)


def regroup_matrix(states, shards):
    own = log2(states // shards)
    width = 2 * states
    source = grid_index((width, width), 0)
    target = grid_index((width, width), 1)
    part = (source >> own) & 1
    place = part * states + ((source >> (own + 1)) << own) + (source & ((1 << own) - 1))
    return jnp.where(place == target, 1.0, 0.0).astype(BF16)


def turn_matrix():
    source = grid_index((TILE, TILE), 0)
    target = grid_index((TILE, TILE), 1)
    bits = log2(SIDE)
    place = ((source & (SIDE - 1)) << bits) + (source >> bits)
    return jnp.where(place == target, 1.0, 0.0)


def turn_rows(turn, value):
    parts = [dot(turn, value[at : at + TILE]) for at in range(0, value.shape[0], TILE)]
    return jnp.concatenate(parts, axis=0).astype(BF16)


class Plan:
    def __init__(self, mesh, rows, group_rows, features, states, units):
        self.fsdp = mesh.shape["fsdp"]
        self.tensor = mesh.shape["tensor"]
        self.count = self.fsdp * self.tensor
        self.bits = log2(self.count)
        far = list(range(self.bits - 1, 3, -1))
        self.far = far
        self.up = [*far, 3, 2, 1, 0]
        self.up_crossed = ([*far, 1, 3, 2, 0], [*far, 1, 2, 3, 0])
        self.down = [0, 1, 2, 3, *far[::-1]]
        self.down_crossed = ([0, 2, 3, 1, *far[::-1]], [0, 3, 2, 1, *far[::-1]])
        self.halves = 2 if features // self.fsdp >= 32 else 1
        self.rows = rows
        self.group_rows = group_rows
        self.features = features
        self.states = states
        self.units = units
        self.own_states = states // self.tensor
        self.own_rows = features // self.fsdp
        self.pieces = SEQ_LEN // rows
        self.tiles = rows // TILE
        self.chunks = self.tiles * SIDE
        self.block = BLOCK if rows % BLOCK == 0 else TILE
        self.blocks = rows // self.block

    def slot_owner(self, slot, me, order):
        owner = me
        for place, bit in enumerate(order):
            owner = owner ^ (((slot >> (self.bits - 1 - place)) & 1) << bit)
        shift = log2(self.tensor)
        return owner >> shift, owner & (self.tensor - 1)

    def block_rows(self, index):
        return pl.ds(pl.multiple_of(index * self.block, self.block), self.block)


def step_rows(tile, place):
    return pl.ds(pl.multiple_of(tile * TILE + place * SIDE, SIDE), SIDE)


def scan_pass(plan, keep_ref, start, extra, reverse, visit):
    def step(index, carried):
        now, extra = carried
        place = SIDE - 1 - index if reverse else index
        after = []
        for tile in range(plan.tiles):
            at = step_rows(tile, place)
            state, extra = visit(tile, at, keep_ref[at, :], now[tile], extra)
            after.append(state)
        return after, extra

    return lax.fori_loop(0, SIDE, step, (start, extra), unroll=True)


def local_ends(plan, source_ref, keep_ref, rate, reverse):
    states = plan.states
    zero = jnp.zeros((SIDE, states), F32)
    rate_re = jnp.broadcast_to(rate[0], zero.shape)
    rate_im = jnp.broadcast_to(rate[1], zero.shape)
    one = jnp.ones((SIDE, LANES), F32)

    def visit(tile, at, keep, state, extra):
        now_re, now_im, hold = state
        held = wide(keep, states)
        pass_re, pass_im = held * rate_re, held * rate_im
        source = source_ref[at, :]
        next_re = (source[:, :states] + pass_re * now_re) - pass_im * now_im
        next_im = (source[:, states:] + pass_re * now_im) + pass_im * now_re
        return (next_re, next_im, hold * keep), extra

    ends, _ = scan_pass(plan, keep_ref, [(zero, zero, one)] * plan.tiles, 0, reverse, visit)
    return tuple(jnp.concatenate([end[part] for end in ends], axis=0) for part in range(3))


def shifted(value, distance, reverse):
    count = value.shape[0]
    row = grid_index(value.shape, 0)
    if reverse:
        moved = pltpu.roll(value, count - distance, 0)
        return jnp.where(row < count - distance, moved, 0.0)
    moved = pltpu.roll(value, distance, 0)
    return jnp.where(row >= distance, moved, 0.0)


def chunk_entries(plan, ends_re, ends_im, hold, rate, start, reverse):
    states, count = plan.states, plan.chunks
    power_re, power_im = rate
    for _ in range(log2(SIDE)):
        power_re, power_im = power_re * power_re - power_im * power_im, 2.0 * power_re * power_im
    first = count - 1 if reverse else 0
    if start is not None:
        at_first = grid_index((count, states), 0) == first
        held = jnp.where(at_first, wide(hold, states), 0.0)
        pass_re, pass_im = held * power_re, held * power_im
        ends_re = ends_re + (pass_re * start[0] - pass_im * start[1])
        ends_im = ends_im + (pass_re * start[1] + pass_im * start[0])
    distance = 1
    while distance < count:
        earlier_re = shifted(ends_re, distance, reverse)
        earlier_im = shifted(ends_im, distance, reverse)
        held = wide(hold, states)
        pass_re, pass_im = held * power_re, held * power_im
        ends_re = ends_re + (pass_re * earlier_re - pass_im * earlier_im)
        ends_im = ends_im + (pass_re * earlier_im + pass_im * earlier_re)
        hold = hold * shifted(hold, distance, reverse)
        power_re, power_im = power_re * power_re - power_im * power_im, 2.0 * power_re * power_im
        distance *= 2
    last = slice(0, 1) if reverse else slice(count - 1, count)
    leaving = jnp.concatenate([ends_re[last], ends_im[last]], axis=1)
    if start is None:
        return None, leaving
    entry_re = shifted(ends_re, 1, reverse) + jnp.where(at_first, start[0], 0.0)
    entry_im = shifted(ends_im, 1, reverse) + jnp.where(at_first, start[1], 0.0)
    entries = []
    for tile in range(plan.tiles):
        at = slice(tile * SIDE, (tile + 1) * SIDE)
        entries.append((entry_re[at], entry_im[at]))
    return entries, leaving


def block_places(plan, me, order, refs, base, rows, start):
    slot = 0
    for ref in refs:
        for place in range(plan.count // 2):
            band, shard = plan.slot_owner(slot, me, order)
            slot += 1
            first = pl.multiple_of(band * plan.own_rows + start, rows)
            yield ref, base + place * rows, pl.ds(first, rows), shard


def collect(plan, me, order, refs, base, rows, start, targets):
    for ref, row, at, shard in block_places(plan, me, order, refs, base, rows, start):
        for first, width, out_ref, lanes in targets:
            column = pl.multiple_of(lanes + shard * width, LANES)
            out_ref[at, pl.ds(column, width)] = ref[row : row + rows, first : first + width].astype(
                out_ref.dtype
            )


def distribute(plan, me, order, refs, base, rows, start, targets):
    for ref, row, at, shard in block_places(plan, me, order, refs, base, rows, start):
        for first, width, full_ref, lanes in targets:
            column = pl.multiple_of(lanes + shard * width, LANES)
            ref[row : row + rows, first : first + width] = full_ref[at, pl.ds(column, width)].astype(
                ref.dtype
            )


def half_blocks(plan, orders):
    rows = plan.own_rows // plan.halves
    for half in range(plan.halves):
        yield orders[half], half * plan.count // 2 * rows, rows, half * rows


def start_copies(pairs, sems):
    copies = [
        pltpu.make_async_copy(source, target, sems.at[place])
        for place, (source, target) in enumerate(pairs)
    ]
    for copy in copies:
        copy.start()
    return copies


def pack_kernel(plan, me_ref, *refs):
    sources, outs, held, sems = refs[:14], refs[14:16], refs[16:30], refs[30]
    copies = start_copies(list(zip(sources, held)), sems)
    first_ref, second_ref = outs
    band = me_ref[0] >> log2(plan.tensor)
    rows, features = plan.own_rows, plan.features
    for copy in copies:
        copy.wait()
    first_ref[:rows, :] = jnp.concatenate([held[0][...], held[1][...]], axis=1)
    second_ref[...] = jnp.concatenate([ref[...] for ref in held[2:6]], axis=1)
    placed = []
    lane = grid_index((1, features), 1)
    for ref in held[6:]:
        length = ref.shape[1]
        value = ref[...].astype(F32)
        value = jnp.concatenate([value] * (features // length), axis=1)
        placed.append(jnp.where((lane >> log2(length)) == band, value, 0.0))
    placed = jnp.concatenate(placed, axis=0).astype(BF16)
    for part in range(features // LANES):
        first_ref[rows + 8 * part : rows + 8 * part + 8, :] = placed[
            :, part * LANES : (part + 1) * LANES
        ]


def token_kernel(plan, me_ref, x_ref, segments_ref, stats_ref, masks_ref, flags_ref):
    shard = me_ref[0] & (plan.tensor - 1)
    ids = segments_ref[...]
    count = ids.shape[0]
    lane = grid_index(ids.shape, 1)
    position = (grid_index(ids.shape, 0) * LANES + lane) & (SEQ_LEN - 1)
    turned = pltpu.roll(ids, 1, 1)
    before = jnp.where(lane == 0, pltpu.roll(turned, 1, 0), turned)
    turned = pltpu.roll(ids, LANES - 1, 1)
    after = jnp.where(lane == LANES - 1, pltpu.roll(turned, count - 1, 0), turned)
    flags_ref[0] = jnp.where((position > 0) & (ids == before), 1.0, 0.0)
    flags_ref[1] = jnp.where((position < SEQ_LEN - 1) & (ids == after), 1.0, 0.0)
    flags_ref[2] = jnp.where(ids > 0, 1.0, 0.0)
    turn = turn_matrix()
    plain = jnp.where(grid_index((TILE, TILE), 0) == grid_index((TILE, TILE), 1), 1.0, 0.0)
    ones = jnp.ones((TILE, LANES), BF16)
    per_tile = TILE // LANES
    own = plan.rows // LANES
    flags = [flags_ref[kind, pl.ds(pl.multiple_of(shard * own, own), own), :] for kind in range(3)]
    for tile in range(plan.tiles):
        at = slice(tile * TILE, (tile + 1) * TILE)
        for kind in range(4):
            rows = flags[min(kind, 2)][tile * per_tile : (tile + 1) * per_tile, :]
            line = jnp.concatenate([rows[part : part + 1, :] for part in range(per_tile)], axis=1)
            spread = (plain if kind == 3 else turn) * line
            masks_ref[kind, at, :] = dot(spread.astype(BF16), ones)

    def rows_step(index, _):
        at = plan.block_rows(index)
        values = x_ref[at, :].astype(F32)
        mean = jnp.mean(values, axis=1, keepdims=True)
        centred = values - mean
        inverse = lax.rsqrt(jnp.mean(centred * centred, axis=1, keepdims=True) + norm_epsilon)
        stats_ref[0, at, :] = jnp.broadcast_to(mean, (plan.block, LANES))
        stats_ref[1, at, :] = jnp.broadcast_to(inverse, (plan.block, LANES))
        return 0

    lax.fori_loop(0, plan.blocks, rows_step, 0)


def standard_rows(plan, x_ref, stats_ref, at):
    mean = wide(stats_ref[0, at, :], plan.features)
    inverse = wide(stats_ref[1, at, :], plan.features)
    return (x_ref[at, :].astype(F32) - mean) * inverse, inverse


def read_vectors(vec_ref):
    count = vec_ref.shape[0] // 8
    parts = [vec_ref[8 * part : 8 * part + 8, :].astype(F32) for part in range(count)]
    return jnp.concatenate(parts, axis=1)


def received(carry_ref, wanted, states):
    value = jnp.where(wanted, carry_ref[0:1, :], 0.0)
    return value[:, :states], value[:, states:]


def enter_kernel(
    plan, me_ref, x_ref, stats_ref, b0_ref, b1_ref, vec_ref, masks_ref,
    normed_ref, source_ref, ends_ref, hold_ref, carry_ref, input_map_ref, params_ref,
    pack_ref,
):
    states = plan.states
    collect(
        plan, me_ref[0], plan.up[::-1], (b0_ref, b1_ref), 0, plan.own_rows, 0,
        [(0, 2 * plan.own_states, pack_ref, 0)],
    )
    input_map_ref[...] = dot(
        pack_ref[...].astype(BF16), regroup_matrix(states, plan.tensor)
    ).astype(BF16)
    vectors = read_vectors(vec_ref)
    gain, shift = vectors[0:1], vectors[1:2]
    speed = jnp.exp(vectors[5:6, :states])
    modulus = jnp.exp(-speed)
    rotation = jnp.exp(vectors[6:7, :states])
    rate = (modulus * jnp.cos(rotation), modulus * jnp.sin(rotation))
    rest = 1.0 - modulus * modulus
    gamma = jnp.exp(vectors[7:8, :states]) * jnp.sqrt(rest)
    params_ref[...] = jnp.concatenate(
        [
            jnp.concatenate(rate, axis=1),
            jnp.concatenate([gamma, speed], axis=1),
            jnp.concatenate([modulus, rest], axis=1),
            jnp.concatenate([rotation, rotation], axis=1),
            jnp.zeros((4, 2 * states), F32),
        ],
        axis=0,
    )
    gamma_pair = jnp.concatenate([gamma, gamma], axis=1)
    turn = turn_matrix().astype(BF16)

    def rows_step(index, _):
        at = plan.block_rows(index)
        standard, _ = standard_rows(plan, x_ref, stats_ref, at)
        normed = (standard * gain + shift).astype(BF16)
        normed_ref[at, :] = normed
        turned = turn_rows(turn, normed)
        drive = dot(turned, input_map_ref[...])
        source_ref[at, :] = drive * gamma_pair * wide(masks_ref[2, at, :], 2 * states)
        return 0

    lax.fori_loop(0, plan.blocks, rows_step, 0)
    ends_re, ends_im, hold = local_ends(plan, source_ref, masks_ref.at[0], rate, False)
    ends_ref[...] = jnp.concatenate([ends_re, ends_im], axis=1)
    hold_ref[...] = hold
    _, leaving = chunk_entries(plan, ends_re, ends_im, hold, rate, None, False)
    carry_ref[...] = jnp.broadcast_to(leaving, carry_ref.shape)


def middle_kernel(
    plan, me_ref, x_ref, grad_ref, normed_ref, source_ref, ends_ref, hold_ref, carry_ref,
    g0_ref, g1_ref, vec_ref, params_ref, masks_ref,
    mixed_ref, hidden_ref, lru_grad_ref, state_grad_ref, act_ref, unit_grad_ref, low_ref, sums_ref,
    pack_ref, wpack_ref, out_map_ref,
):
    states, features, units = plan.states, plan.features, plan.units
    pair = 2 * plan.own_states
    targets = [
        (0, pair, pack_ref, 0),
        (pair, units, wpack_ref, 0),
        (pair + units, units, wpack_ref, features),
    ]
    for order, base, rows, first in half_blocks(plan, plan.up_crossed):
        collect(plan, me_ref[0], order[::-1], (g0_ref, g1_ref), base, rows, first, targets)
    sign = jnp.where(grid_index((1, 2 * states), 1) < states, 1.0, -1.0)
    regroup = regroup_matrix(states, plan.tensor)
    out_map_ref[...] = (dot(pack_ref[...].astype(BF16), regroup) * sign).astype(BF16)
    rate = (params_ref[0:1, :states], params_ref[0:1, states:])
    start = received(carry_ref, me_ref[0] & 1 == 1, states)
    entries, _ = chunk_entries(
        plan, ends_ref[:, :states], ends_ref[:, states:], hold_ref[...], rate, start, False
    )
    rate_re = jnp.broadcast_to(rate[0], (SIDE, states))
    rate_im = jnp.broadcast_to(rate[1], (SIDE, states))

    def visit(tile, at, keep, state, extra):
        now_re, now_im = state
        held = wide(keep, states)
        pass_re, pass_im = held * rate_re, held * rate_im
        source = source_ref[at, :]
        next_re = (source[:, :states] + pass_re * now_re) - pass_im * now_im
        next_im = (source[:, states:] + pass_re * now_im) + pass_im * now_re
        hidden_ref[at, :states] = next_re
        hidden_ref[at, states:] = next_im
        return (next_re, next_im), extra

    scan_pass(plan, masks_ref.at[0], entries, 0, False, visit)
    vectors = read_vectors(vec_ref)
    skip = vectors[2:3]
    biases = jnp.concatenate([vectors[3:4], vectors[4:5]], axis=1)
    sums_ref[...] = jnp.zeros_like(sums_ref)
    turn = turn_matrix().astype(BF16)

    def rows_step(index, _):
        at = plan.block_rows(index)
        low = turn_rows(turn, hidden_ref[at, :].astype(BF16))
        low_ref[at, :] = low
        normed = normed_ref[at, :].astype(F32)
        lru = dot(low, out_map_ref[...], 1, 1) + skip * normed
        square = lru * lru
        bent = jnp.tanh(lru * (GELU_SCALE + (GELU_SCALE * GELU_CUBE) * square))
        half = 0.5 + 0.5 * bent
        act_wide = lru * half
        slope = half + act_wide * (1.0 - half) * (
            2.0 * GELU_SCALE + (6.0 * GELU_SCALE * GELU_CUBE) * square
        )
        act = act_wide.astype(BF16)
        act_ref[at, :] = act
        mapped = dot(act, wpack_ref[...].astype(BF16)) + biases
        value = mapped[:, :features]
        live_half = wide(0.5 * masks_ref[3, at, :], features)
        opening = live_half + live_half * jnp.tanh(0.5 * mapped[:, features:])
        gated = value * opening
        mixed_ref[at, :] = (x_ref[at, :].astype(F32) + gated).astype(BF16)
        value_grad = grad_ref[at, :].astype(F32) * opening
        gate_grad = value_grad * (value - gated)
        sums_ref[8:16, :] += fold_rows(value_grad)
        sums_ref[16:24, :] += fold_rows(gate_grad)
        unit_grad = jnp.concatenate([value_grad, gate_grad], axis=1).astype(BF16)
        unit_grad_ref[at, :] = unit_grad
        act_grad = dot(unit_grad, wpack_ref[...].astype(BF16), 1, 1)
        lru_grad = act_grad * slope
        sums_ref[0:8, :] += fold_rows(lru_grad * normed)
        lru_grad = lru_grad.astype(BF16)
        lru_grad_ref[at, :] = lru_grad
        turned = turn_rows(turn, lru_grad)
        state_grad_ref[at, :] = dot(turned, out_map_ref[...])
        return 0

    lax.fori_loop(0, plan.blocks, rows_step, 0)


def back_kernel(
    plan, me_ref, state_grad_ref, params_ref, masks_ref, back_ends_ref, back_hold_ref, back_ref
):
    states = plan.states
    back_rate = (params_ref[0:1, :states], -params_ref[0:1, states:])
    ends_re, ends_im, hold = local_ends(plan, state_grad_ref, masks_ref.at[1], back_rate, True)
    back_ends_ref[...] = jnp.concatenate([ends_re, ends_im], axis=1)
    back_hold_ref[...] = hold
    _, leaving = chunk_entries(plan, ends_re, ends_im, hold, back_rate, None, True)
    back_ref[...] = jnp.broadcast_to(leaving, back_ref.shape)


def weight_kernel(
    plan, me_ref, act_ref, unit_grad_ref, lru_grad_ref, low_ref, keep_ref, send_ref, full_ref, out_ref
):
    states, features, units = plan.states, plan.features, plan.units
    pair = 2 * plan.own_states
    sign = jnp.where(grid_index((1, 2 * states), 1) < states, 1.0, -1.0)
    full_ref[...] = dot(act_ref[...], unit_grad_ref[...], 0, 0)
    out_grad = dot(lru_grad_ref[...], low_ref[...], 0, 0) * sign
    out_ref[...] = dot(out_grad.astype(BF16), regroup_matrix(states, plan.tensor), 1, 1)
    targets = [
        (0, pair, out_ref, 0),
        (pair, units, full_ref, 0),
        (pair + units, units, full_ref, features),
    ]
    for order, base, rows, first in half_blocks(plan, plan.down_crossed):
        distribute(plan, me_ref[0], order, (keep_ref, send_ref), base, rows, first, targets)


def leave_kernel(
    plan, me_ref, x_ref, stats_ref, normed_ref, source_ref, ends_ref, hold_ref, carry_ref, hidden_ref,
    state_grad_ref, lru_grad_ref, input_map_ref, vec_ref, params_ref, masks_ref, sums_ref,
    keep_ref, send_ref, normed_grad_ref,
    drive_grad_ref, low_ref, full_ref,
):
    states, features = plan.states, plan.features
    params = params_ref[...]
    rate = (params[0:1, :states], params[0:1, states:])
    gamma, speed = params[1:2, :states], params[1:2, states:]
    modulus, rest = params[2:3, :states], params[2:3, states:]
    rotation = params[3:4, :states]
    back_rate = (rate[0], -rate[1])
    start = received(carry_ref, me_ref[0] & 1 == 0, states)
    entries, _ = chunk_entries(
        plan, ends_ref[:, :states], ends_ref[:, states:], hold_ref[...], back_rate, start, True
    )
    zero = jnp.zeros((SIDE, states), F32)
    rate_re = jnp.broadcast_to(back_rate[0], zero.shape)
    rate_im = jnp.broadcast_to(back_rate[1], zero.shape)
    gamma_wide = jnp.broadcast_to(gamma, zero.shape)

    def visit(tile, at, keep, state, sums):
        now_re, now_im = state
        held = wide(keep, states)
        next_re, next_im = held * now_re, held * now_im
        hidden_re, hidden_im = hidden_ref[at, :states], hidden_ref[at, states:]
        now_re = (state_grad_ref[at, :states] + rate_re * next_re) - rate_im * next_im
        now_im = (state_grad_ref[at, states:] + rate_re * next_im) + rate_im * next_re
        sums = (
            sums[0] + (hidden_re * next_re + hidden_im * next_im),
            sums[1] + (hidden_re * next_im - hidden_im * next_re),
            sums[2] + (source_ref[at, :states] * now_re + source_ref[at, states:] * now_im),
        )
        scale = gamma_wide * wide(masks_ref[2, at, :], states)
        drive_grad_ref[at, :states] = scale * now_re
        drive_grad_ref[at, states:] = scale * now_im
        return (now_re, now_im), sums

    _, sums = scan_pass(plan, masks_ref.at[1], entries, (zero, zero, zero), True, visit)
    rate_sum_re, rate_sum_im, gamma_sum = (jnp.sum(part, axis=0, keepdims=True) for part in sums)
    nu_grad = speed * (
        gamma_sum * modulus * modulus / rest - (rate_sum_re * rate[0] + rate_sum_im * rate[1])
    )
    theta_grad = rotation * (rate_sum_im * rate[0] - rate_sum_re * rate[1])
    vectors = read_vectors(vec_ref)
    skip = vectors[2:3]
    gain_sum = jnp.zeros((8, features), F32)
    turn = turn_matrix().astype(BF16)

    def rows_step(index, sums):
        gain_sum, shift_sum = sums
        at = plan.block_rows(index)
        low = turn_rows(turn, drive_grad_ref[at, :].astype(BF16))
        low_ref[at, :] = low
        normed_grad = dot(low, input_map_ref[...], 1, 1) + skip * lru_grad_ref[at, :].astype(F32)
        normed_grad_ref[at, :] = normed_grad
        standard, _ = standard_rows(plan, x_ref, stats_ref, at)
        return gain_sum + fold_rows(normed_grad * standard), shift_sum + fold_rows(normed_grad)

    gain_sum, shift_sum = lax.fori_loop(0, plan.blocks, rows_step, (gain_sum, gain_sum))
    into = dot(normed_ref[...], low_ref[...], 0, 0)
    full_ref[...] = dot(into.astype(BF16), regroup_matrix(states, plan.tensor), 1, 1)
    distribute(
        plan, me_ref[0], plan.down, (keep_ref, send_ref), 0, plan.own_rows, 0,
        [(0, 2 * plan.own_states, full_ref, 0)],
    )
    empty = jnp.zeros((1, features - states), F32)
    vector_sums = jnp.concatenate(
        [jnp.sum(part, axis=0, keepdims=True) for part in (gain_sum, shift_sum)]
        + [
            jnp.sum(sums_ref[8 * place : 8 * place + 8, :], axis=0, keepdims=True)
            for place in range(3)
        ]
        + [jnp.concatenate([part, empty], axis=1) for part in (nu_grad, theta_grad, gamma_sum)],
        axis=0,
    )
    base = plan.own_rows * plan.count // 2
    for part in range(features // LANES):
        piece = vector_sums[:, part * LANES : (part + 1) * LANES]
        send_ref[base + 8 * part : base + 8 * part + 8, :] = piece.astype(BF16)


def last_kernel(plan, me_ref, *refs):
    b_keep, b_other, w_mine_ref, tail_ref = refs[:4]
    outs, held, sems = refs[4:18], refs[18:32], refs[32]
    own, units = plan.own_states, plan.units
    b_mine = b_keep[...].astype(F32) + b_other[...].astype(F32)
    w_mine = w_mine_ref[...]
    half = tail_ref.shape[0] // 2
    vectors = tail_ref[:half, :].astype(F32) + tail_ref[half:, :].astype(F32)
    count = half // 8
    vectors = jnp.concatenate([vectors[8 * part : 8 * part + 8] for part in range(count)], axis=1)
    band = me_ref[0] >> log2(plan.tensor)
    at = grid_index((plan.features, LANES), 0)
    lane = grid_index((plan.features, LANES), 1)

    def pick(length):
        chosen = jnp.where(at == band * length + lane, 1.0, 0.0)
        return lax.dot_general(
            vectors,
            chosen,
            (((1,), (0,)), ((), ())),
            precision=lax.Precision.HIGHEST,
            preferred_element_type=F32,
        )

    long, short = plan.own_rows, plan.states // plan.fsdp
    long_part, short_part = pick(long), pick(short)
    held[0][...] = b_mine[:, :own]
    held[1][...] = b_mine[:, own:]
    held[2][...] = w_mine[:, :own]
    held[3][...] = w_mine[:, own : 2 * own]
    held[4][...] = w_mine[:, 2 * own : 2 * own + units]
    held[5][...] = w_mine[:, 2 * own + units :]
    for place in range(8):
        part, length = (long_part, long) if place < 5 else (short_part, short)
        held[6 + place][...] = part[place : place + 1, :length]
    for copy in start_copies(list(zip(held, outs)), sems):
        copy.wait()


def input_kernel(plan, me_ref, x_ref, stats_ref, grad_ref, normed_grad_ref, vec_ref, input_grad_ref):
    gain = read_vectors(vec_ref)[0:1]

    def rows_step(index, _):
        at = plan.block_rows(index)
        standard, inverse = standard_rows(plan, x_ref, stats_ref, at)
        scaled = normed_grad_ref[at, :] * gain
        input_grad_ref[at, :] = grad_ref[at, :].astype(F32) + inverse * (
            scaled
            - jnp.mean(scaled, axis=1, keepdims=True)
            - standard * jnp.mean(scaled * standard, axis=1, keepdims=True)
        )
        return 0

    lax.fori_loop(0, plan.blocks, rows_step, 0)


def call(kernel, plan, outs, scratch, limit, time, *args, far_in=0, far_out=False):
    args = [*args[:1], *(pltpu.with_memory_space_constraint(a, pltpu.HBM) for a in args[1 : 1 + far_in]), *args[1 + far_in :]]
    whole = pl.BlockSpec(memory_space=pltpu.VMEM)
    far = pl.BlockSpec(memory_space=pltpu.HBM)
    return pl.pallas_call(
        functools.partial(kernel, plan),
        out_shape=outs,
        in_specs=[pl.BlockSpec(memory_space=pltpu.SMEM)]
        + [far] * far_in
        + [whole] * (len(args) - 1 - far_in),
        out_specs=[far if far_out else whole] * len(outs),
        scratch_shapes=scratch,
        compiler_params=pltpu.CompilerParams(vmem_limit_bytes=limit * MIB),
        cost_estimate=pl.CostEstimate(
            flops=int(time * 1e9), bytes_accessed=int(time * 3.5e6), transcendentals=0
        ),
    )(*args)


def shape(dims, dtype=F32):
    return jax.ShapeDtypeStruct(dims, dtype)


def after(value, *others):
    return lax.optimization_barrier((value, *others))[0]


def joined(*parts):
    return jnp.concatenate(parts, axis=0)


def gather_blocks(plan, first, summed, second, cover):
    count, width = plan.count, second.shape[1]
    tensor_bits = log2(plan.tensor)
    other = None

    def first_step(bit):
        rows = first.shape[0]
        if bit < tensor_bits:
            got = flip(first, bit, count)
            return got, joined(first, got), summed
        got = flip(joined(first, summed), bit, count)
        if other is None:
            got = after(got, cover, second_other)
        return got, joined(first, got[:rows]), summed + got[rows:]

    for bit in plan.far:
        second_other = flip(second if other is None else after(second, other), bit, count)
        other, first, summed = first_step(bit)
        second = joined(second, second_other)
    second = joined(second, flip(after(second, other), 1, count))
    other, first, summed = first_step(3)
    blocks = second.reshape(-1, plan.own_rows, width)
    size = plan.own_rows // plan.halves
    halves = [
        after(blocks[:, half * size : half * size + size].reshape(-1, width), other)
        for half in range(plan.halves)
    ]
    halves = [joined(part, flip(part, bit, count)) for part, bit in zip(halves, (3, 2))]
    other, first, summed = first_step(2)
    halves = [(part, flip(part, bit, count)) for part, bit in zip(halves, (2, 3))]
    other, first, summed = first_step(1)
    return first, flip(first, 0, count), summed, halves


def cut(value):
    count = value.shape[0] // 2
    return value[:count].astype(BF16), value[count:].astype(BF16)


def added(keep, other):
    return keep.astype(F32) + other.astype(F32)


def summed_step(keep, send, other):
    count = keep.shape[0]
    summed = added(send[count:], other[count:]).astype(BF16)
    keep, send = cut(added(keep, other[:count]))
    return keep, joined(send, summed)


def together(*values):
    return lax.optimization_barrier(values)


def shards(
    mesh,
    block_input,
    segments,
    ln_gain,
    ln_bias,
    b_real,
    b_imag,
    c_real,
    c_imag,
    nu_log,
    theta_log,
    gamma_log,
    d_skip,
    w_value,
    w_gate,
    b_value,
    b_gate,
    out_grad,
):
    band = lax.axis_index("fsdp")
    shard = lax.axis_index("tensor")
    rows, features = block_input.shape
    own = b_real.shape[1]
    plan = Plan(
        mesh, rows, segments.shape[0], features, own * mesh.shape["tensor"], w_value.shape[1]
    )
    states, units, chunks = plan.states, plan.units, plan.chunks
    me = (band * plan.tensor + shard).astype(jnp.int32).reshape(1)
    long, short = plan.own_rows, states // plan.fsdp
    vector_rows = 8 * features // LANES
    matrices = (b_real, b_imag, c_real, c_imag, w_value, w_gate)
    lines = [
        v.reshape(1, -1)
        for v in (ln_gain, ln_bias, d_skip, b_value, b_gate, nu_log, theta_log, gamma_log)
    ]
    block = 2 * own + 2 * units
    first, second = call(
        pack_kernel,
        plan,
        [shape((long + vector_rows, 2 * own), BF16), shape((long, block), BF16)],
        [pltpu.VMEM(v.shape, BF16) for v in (*matrices, *lines)] + [pltpu.SemaphoreType.DMA((14,))],
        4,
        1.5,
        me, *matrices, *lines,
        far_in=14,
    )
    stats, masks = call(
        token_kernel,
        plan,
        [shape((2, rows, LANES)), shape((4, rows, LANES))],
        [pltpu.VMEM((3, plan.group_rows // LANES, LANES), F32)],
        8,
        2,
        me, block_input, segments.reshape(-1, LANES),
    )
    b0, b1, vectors, halves = gather_blocks(plan, first[:long], first[long:], second, masks)

    pack_type = BF16 if long % 16 == 0 else F32
    full = (rows, 2 * states)
    normed, source, ends, hold, carry, input_map, params = call(
        enter_kernel,
        plan,
        [
            shape((rows, features), BF16),
            shape(full),
            shape((chunks, 2 * states)),
            shape((chunks, LANES)),
            shape((8, 2 * states)),
            shape((features, 2 * states), BF16),
            shape((8, 2 * states)),
        ],
        [pltpu.VMEM((features, 2 * states), pack_type)],
        8,
        0.3,
        me, block_input, stats, b0, b1, vectors, masks,
    )

    left = carry
    carry = flip(carry, 0, plan.count) if plan.pieces == 2 else jnp.zeros_like(carry)
    g0 = joined(*(joined(part, after(got, left)) for part, got in halves))
    g1 = flip(g0, 0, plan.count)
    (
        mixed, hidden, lru_grad, state_grad, act, unit_grad, low, sums,
    ) = call(
        middle_kernel,
        plan,
        [
            shape((rows, features), BF16),
            shape(full),
            shape((rows, features), BF16),
            shape(full),
            shape((rows, features), BF16),
            shape((rows, 2 * features), BF16),
            shape(full, BF16),
            shape((24, features)),
        ],
        [
            pltpu.VMEM((features, 2 * states), pack_type),
            pltpu.VMEM((features, 2 * features), pack_type),
            pltpu.VMEM((features, 2 * states), BF16),
        ],
        24,
        10,
        me, block_input, out_grad, normed, source, ends, hold, carry, g0, g1, vectors, params, masks,
    )
    half_rows = plan.count // 2 * long
    w_keep, w_send = call(
        weight_kernel,
        plan,
        [shape((half_rows, block), BF16)] * 2,
        [
            pltpu.VMEM((features, 2 * features), F32),
            pltpu.VMEM((features, 2 * states), F32),
        ],
        10,
        2.5,
        me, act, unit_grad, lru_grad, low,
    )
    w_other = flip(w_send, 0, plan.count)
    back_ends, back_hold, back = call(
        back_kernel,
        plan,
        [shape((chunks, 2 * states)), shape((chunks, LANES)), shape((8, 2 * states))],
        [],
        8,
        1,
        me, after(state_grad, w_send), params, masks,
    )
    back = flip(back, 0, plan.count) if plan.pieces == 2 else jnp.zeros_like(back)
    pieces = plan.halves
    w_total = added(w_keep, after(w_other, back_ends))
    size = w_total.shape[0] // pieces
    halves = [cut(w_total[half * size : half * size + size]) for half in range(pieces)]
    w_others = [flip(half[1], bit, plan.count) for half, bit in zip(halves, (2, 3))]
    back_ends = after(back_ends, *(half[1] for half in halves))
    b_keep, b_send, normed_grad = call(
        leave_kernel,
        plan,
        [
            shape((half_rows, 2 * own), BF16),
            shape((half_rows + vector_rows, 2 * own), BF16),
            shape((rows, features)),
        ],
        [
            pltpu.VMEM(full, F32),
            pltpu.VMEM(full, BF16),
            pltpu.VMEM((features, 2 * states), F32),
        ],
        14,
        4.5,
        me, block_input, stats, normed, source, back_ends, back_hold, back, hidden,
        state_grad, lru_grad, input_map, vectors, params, masks, sums,
    )
    w_others = [after(other, b_keep) for other in w_others]
    halves = [cut(added(half[0], other)) for half, other in zip(halves, w_others)]
    b_other = after(flip(b_send, 0, plan.count), *(half[1] for half in halves))
    b_keep, b_send = summed_step(b_keep, b_send, b_other)
    b_other = flip(b_send, 1, plan.count)
    w_others = [flip(half[1], bit, plan.count) for half, bit in zip(halves, (3, 2))]
    b_keep, b_send = summed_step(b_keep, b_send, b_other)
    halves = [cut(added(half[0], after(other, b_send))) for half, other in zip(halves, w_others)]
    w_keep = joined(*(half[0] for half in halves))
    w_send = joined(*(half[1] for half in halves))
    for bit in range(2, plan.bits - 1):
        w_bit = 1 if bit == 2 else bit + 1
        b_other = flip(b_send, bit, plan.count)
        w_other = flip(w_send, w_bit, plan.count)
        b_keep, b_send = summed_step(b_keep, b_send, b_other)
        if w_bit < plan.bits - 1:
            w_other = after(w_other, b_send)
            total = added(w_keep, w_other).reshape(pieces, -1, block)
            size = total.shape[1] // 2
            w_keep = total[:, :size].reshape(-1, block).astype(BF16)
            w_send = total[:, size:].reshape(-1, block).astype(BF16)
    (input_grad,) = call(
        input_kernel,
        plan,
        [shape((rows, features))],
        [],
        8,
        2.5,
        me, block_input, stats, out_grad, after(normed_grad, b_send), vectors,
    )
    w_mine = added(w_keep, w_other)
    b_other = after(flip(b_send, plan.bits - 1, plan.count), w_mine, input_grad)
    b_other, tail = b_other[:long], joined(b_send[long:], b_other[long:])
    small = (
        [(long, own)] * 4 + [(long, units)] * 2 + [(1, long)] * 5 + [(1, short)] * 3
    )
    (
        b_real_grad, b_imag_grad, c_real_grad, c_imag_grad, value_grad, gate_grad, *lines
    ) = call(
        last_kernel,
        plan,
        [shape(dims) for dims in small],
        [pltpu.VMEM(dims, F32) for dims in small] + [pltpu.SemaphoreType.DMA((14,))],
        4,
        2,
        me, b_keep, b_other, w_mine, tail,
        far_out=True,
    )
    gain_grad, bias_grad, skip_grad, value_line, gate_line, nu_grad, theta_grad, gamma_grad = (
        line.reshape(-1) for line in lines
    )
    return (
        mixed,
        input_grad,
        gain_grad,
        bias_grad,
        b_real_grad,
        b_imag_grad,
        c_real_grad,
        c_imag_grad,
        nu_grad,
        theta_grad,
        gamma_grad,
        skip_grad,
        value_grad,
        gate_grad,
        value_line,
        gate_line,
    )


def solution(mesh):
    in_specs = (
        P(("fsdp", "tensor"), None),
        P("fsdp"),
        P("fsdp"),
        P("fsdp"),
        P("fsdp", "tensor"),
        P("fsdp", "tensor"),
        P("fsdp", "tensor"),
        P("fsdp", "tensor"),
        P("fsdp"),
        P("fsdp"),
        P("fsdp"),
        P("fsdp"),
        P("fsdp", "tensor"),
        P("fsdp", "tensor"),
        P("fsdp"),
        P("fsdp"),
        P(("fsdp", "tensor"), None),
    )
    out_specs = (
        P(("fsdp", "tensor"), None),
        P(("fsdp", "tensor"), None),
        P("fsdp"),
        P("fsdp"),
        P("fsdp", "tensor"),
        P("fsdp", "tensor"),
        P("fsdp", "tensor"),
        P("fsdp", "tensor"),
        P("fsdp"),
        P("fsdp"),
        P("fsdp"),
        P("fsdp"),
        P("fsdp", "tensor"),
        P("fsdp", "tensor"),
        P("fsdp"),
        P("fsdp"),
    )
    return jax.shard_map(
        functools.partial(shards, mesh),
        mesh=mesh,
        in_specs=in_specs,
        out_specs=out_specs,
        check_vma=False,
    )
```

```python
import functools
import math

import jax
import jax.numpy as jnp
from jax import lax
from jax.experimental import pallas as pl
from jax.experimental.pallas import tpu as pltpu
from jax.sharding import PartitionSpec as P

SEQ_LEN = 2048
LANES = 128
TILE = 256
SIDE = 16
BLOCK = 1024
AXES = ("fsdp", "tensor")
norm_epsilon = 1e-05
GELU_SCALE = math.sqrt(2.0 / math.pi)
GELU_CUBE = 0.044715
F32 = jnp.float32
BF16 = jnp.bfloat16
MIB = 1024 * 1024


def log2(value):
    return value.bit_length() - 1


def flip(value, bit, count):
    return lax.ppermute(value, AXES, [(i, i ^ (1 << bit)) for i in range(count)])


def dot(left, right, left_dim=1, right_dim=0):
    return lax.dot_general(
        left, right, (((left_dim,), (right_dim,)), ((), ())), preferred_element_type=F32
    )


def fold_rows(value):
    rows, width = value.shape
    return jnp.sum(value.reshape(rows // 8, 8, width), axis=0)


def wide(mask, width):
    return jnp.concatenate([mask] * (width // LANES), axis=1)


def grid_index(dims, axis):
    return lax.broadcasted_iota(jnp.int32, dims, axis)


def regroup_matrix(states, shards):
    own = log2(states // shards)
    width = 2 * states
    source = grid_index((width, width), 0)
    target = grid_index((width, width), 1)
    part = (source >> own) & 1
    place = part * states + ((source >> (own + 1)) << own) + (source & ((1 << own) - 1))
    return jnp.where(place == target, 1.0, 0.0).astype(BF16)


def turn_matrix():
    source = grid_index((TILE, TILE), 0)
    target = grid_index((TILE, TILE), 1)
    bits = log2(SIDE)
    place = ((source & (SIDE - 1)) << bits) + (source >> bits)
    return jnp.where(place == target, 1.0, 0.0)


def turn_rows(turn, value):
    parts = [dot(turn, value[at : at + TILE]) for at in range(0, value.shape[0], TILE)]
    return jnp.concatenate(parts, axis=0).astype(BF16)


class Plan:
    def __init__(self, mesh, rows, group_rows, features, states, units):
        self.fsdp = mesh.shape["fsdp"]
        self.tensor = mesh.shape["tensor"]
        self.count = self.fsdp * self.tensor
        self.bits = log2(self.count)
        far = list(range(self.bits - 1, 3, -1))
        self.far = far
        self.up = [*far, 3, 2, 1, 0]
        self.up_crossed = ([*far, 1, 3, 2, 0], [*far, 1, 2, 3, 0])
        self.down = [0, 1, 2, 3, *far[::-1]]
        self.down_crossed = ([0, 2, 3, 1, *far[::-1]], [0, 3, 2, 1, *far[::-1]])
        self.halves = 2 if features // self.fsdp >= 32 else 1
        self.rows = rows
        self.group_rows = group_rows
        self.features = features
        self.states = states
        self.units = units
        self.own_states = states // self.tensor
        self.own_rows = features // self.fsdp
        self.pieces = SEQ_LEN // rows
        self.tiles = rows // TILE
        self.chunks = self.tiles * SIDE
        self.block = BLOCK if rows % BLOCK == 0 else TILE
        self.blocks = rows // self.block

    def slot_owner(self, slot, me, order):
        owner = me
        for place, bit in enumerate(order):
            owner = owner ^ (((slot >> (self.bits - 1 - place)) & 1) << bit)
        shift = log2(self.tensor)
        return owner >> shift, owner & (self.tensor - 1)

    def block_rows(self, index):
        return pl.ds(pl.multiple_of(index * self.block, self.block), self.block)


def step_rows(tile, place):
    return pl.ds(pl.multiple_of(tile * TILE + place * SIDE, SIDE), SIDE)


def scan_pass(plan, keep_ref, start, extra, reverse, visit):
    def step(index, carried):
        now, extra = carried
        place = SIDE - 1 - index if reverse else index
        after = []
        for tile in range(plan.tiles):
            at = step_rows(tile, place)
            state, extra = visit(tile, at, keep_ref[at, :], now[tile], extra)
            after.append(state)
        return after, extra

    return lax.fori_loop(0, SIDE, step, (start, extra), unroll=True)


def local_ends(plan, source_ref, keep_ref, rate, reverse):
    states = plan.states
    zero = jnp.zeros((SIDE, states), F32)
    rate_re = jnp.broadcast_to(rate[0], zero.shape)
    rate_im = jnp.broadcast_to(rate[1], zero.shape)
    one = jnp.ones((SIDE, LANES), F32)

    def visit(tile, at, keep, state, extra):
        now_re, now_im, hold = state
        held = wide(keep, states)
        pass_re, pass_im = held * rate_re, held * rate_im
        source = source_ref[at, :]
        next_re = (source[:, :states] + pass_re * now_re) - pass_im * now_im
        next_im = (source[:, states:] + pass_re * now_im) + pass_im * now_re
        return (next_re, next_im, hold * keep), extra

    ends, _ = scan_pass(plan, keep_ref, [(zero, zero, one)] * plan.tiles, 0, reverse, visit)
    return tuple(jnp.concatenate([end[part] for end in ends], axis=0) for part in range(3))


def shifted(value, distance, reverse):
    count = value.shape[0]
    row = grid_index(value.shape, 0)
    if reverse:
        moved = pltpu.roll(value, count - distance, 0)
        return jnp.where(row < count - distance, moved, 0.0)
    moved = pltpu.roll(value, distance, 0)
    return jnp.where(row >= distance, moved, 0.0)


def chunk_entries(plan, ends_re, ends_im, hold, rate, start, reverse):
    states, count = plan.states, plan.chunks
    power_re, power_im = rate
    for _ in range(log2(SIDE)):
        power_re, power_im = power_re * power_re - power_im * power_im, 2.0 * power_re * power_im
    first = count - 1 if reverse else 0
    if start is not None:
        at_first = grid_index((count, states), 0) == first
        held = jnp.where(at_first, wide(hold, states), 0.0)
        pass_re, pass_im = held * power_re, held * power_im
        ends_re = ends_re + (pass_re * start[0] - pass_im * start[1])
        ends_im = ends_im + (pass_re * start[1] + pass_im * start[0])
    distance = 1
    while distance < count:
        earlier_re = shifted(ends_re, distance, reverse)
        earlier_im = shifted(ends_im, distance, reverse)
        held = wide(hold, states)
        pass_re, pass_im = held * power_re, held * power_im
        ends_re = ends_re + (pass_re * earlier_re - pass_im * earlier_im)
        ends_im = ends_im + (pass_re * earlier_im + pass_im * earlier_re)
        hold = hold * shifted(hold, distance, reverse)
        power_re, power_im = power_re * power_re - power_im * power_im, 2.0 * power_re * power_im
        distance *= 2
    last = slice(0, 1) if reverse else slice(count - 1, count)
    leaving = jnp.concatenate([ends_re[last], ends_im[last]], axis=1)
    if start is None:
        return None, leaving
    entry_re = shifted(ends_re, 1, reverse) + jnp.where(at_first, start[0], 0.0)
    entry_im = shifted(ends_im, 1, reverse) + jnp.where(at_first, start[1], 0.0)
    entries = []
    for tile in range(plan.tiles):
        at = slice(tile * SIDE, (tile + 1) * SIDE)
        entries.append((entry_re[at], entry_im[at]))
    return entries, leaving


def block_places(plan, me, order, refs, base, rows, start):
    slot = 0
    for ref in refs:
        for place in range(plan.count // len(refs)):
            band, shard = plan.slot_owner(slot, me, order)
            slot += 1
            first = pl.multiple_of(band * plan.own_rows + start, rows)
            yield ref, base + place * rows, pl.ds(first, rows), shard


def collect(plan, me, order, refs, base, rows, start, targets):
    for ref, row, at, shard in block_places(plan, me, order, refs, base, rows, start):
        for first, width, out_ref, lanes in targets:
            column = pl.multiple_of(lanes + shard * width, LANES)
            out_ref[at, pl.ds(column, width)] = ref[row : row + rows, first : first + width].astype(
                out_ref.dtype
            )


def distribute(plan, me, order, refs, base, rows, start, targets):
    for ref, row, at, shard in block_places(plan, me, order, refs, base, rows, start):
        for first, width, full_ref, lanes in targets:
            column = pl.multiple_of(lanes + shard * width, LANES)
            ref[row : row + rows, first : first + width] = full_ref[at, pl.ds(column, width)].astype(
                ref.dtype
            )


def half_blocks(plan, orders, arrays):
    rows = plan.own_rows // plan.halves
    for half in range(plan.halves):
        yield orders[half], half * plan.count // arrays * rows, rows, half * rows


def start_copies(pairs, sems):
    copies = [
        pltpu.make_async_copy(source, target, sems.at[place])
        for place, (source, target) in enumerate(pairs)
    ]
    for copy in copies:
        copy.start()
    return copies


def pack_kernel(plan, me_ref, *refs):
    sources, outs, held, sems = refs[:14], refs[14:16], refs[16:30], refs[30]
    copies = start_copies(list(zip(sources, held)), sems)
    first_ref, second_ref = outs
    band = me_ref[0] >> log2(plan.tensor)
    rows, features = plan.own_rows, plan.features
    for copy in copies:
        copy.wait()
    first_ref[:rows, :] = jnp.concatenate([held[0][...], held[1][...]], axis=1)
    second_ref[...] = jnp.concatenate([ref[...] for ref in held[2:6]], axis=1)
    placed = []
    lane = grid_index((1, features), 1)
    for ref in held[6:]:
        length = ref.shape[1]
        value = ref[...].astype(F32)
        value = jnp.concatenate([value] * (features // length), axis=1)
        placed.append(jnp.where((lane >> log2(length)) == band, value, 0.0))
    placed = jnp.concatenate(placed, axis=0).astype(BF16)
    for part in range(features // LANES):
        first_ref[rows + 8 * part : rows + 8 * part + 8, :] = placed[
            :, part * LANES : (part + 1) * LANES
        ]


def token_kernel(plan, me_ref, x_ref, segments_ref, stats_ref, masks_ref, flags_ref):
    shard = me_ref[0] & (plan.tensor - 1)
    ids = segments_ref[...]
    count = ids.shape[0]
    lane = grid_index(ids.shape, 1)
    position = (grid_index(ids.shape, 0) * LANES + lane) & (SEQ_LEN - 1)
    turned = pltpu.roll(ids, 1, 1)
    before = jnp.where(lane == 0, pltpu.roll(turned, 1, 0), turned)
    turned = pltpu.roll(ids, LANES - 1, 1)
    after = jnp.where(lane == LANES - 1, pltpu.roll(turned, count - 1, 0), turned)
    flags_ref[0] = jnp.where((position > 0) & (ids == before), 1.0, 0.0)
    flags_ref[1] = jnp.where((position < SEQ_LEN - 1) & (ids == after), 1.0, 0.0)
    flags_ref[2] = jnp.where(ids > 0, 1.0, 0.0)
    turn = turn_matrix()
    plain = jnp.where(grid_index((TILE, TILE), 0) == grid_index((TILE, TILE), 1), 1.0, 0.0)
    ones = jnp.ones((TILE, LANES), BF16)
    per_tile = TILE // LANES
    own = plan.rows // LANES
    flags = [flags_ref[kind, pl.ds(pl.multiple_of(shard * own, own), own), :] for kind in range(3)]
    for tile in range(plan.tiles):
        at = slice(tile * TILE, (tile + 1) * TILE)
        for kind in range(4):
            rows = flags[min(kind, 2)][tile * per_tile : (tile + 1) * per_tile, :]
            line = jnp.concatenate([rows[part : part + 1, :] for part in range(per_tile)], axis=1)
            spread = (plain if kind == 3 else turn) * line
            masks_ref[kind, at, :] = dot(spread.astype(BF16), ones)

    def rows_step(index, _):
        at = plan.block_rows(index)
        values = x_ref[at, :].astype(F32)
        mean = jnp.mean(values, axis=1, keepdims=True)
        centred = values - mean
        inverse = lax.rsqrt(jnp.mean(centred * centred, axis=1, keepdims=True) + norm_epsilon)
        stats_ref[0, at, :] = jnp.broadcast_to(mean, (plan.block, LANES))
        stats_ref[1, at, :] = jnp.broadcast_to(inverse, (plan.block, LANES))
        return 0

    lax.fori_loop(0, plan.blocks, rows_step, 0)


def standard_rows(plan, x_ref, stats_ref, at):
    mean = wide(stats_ref[0, at, :], plan.features)
    inverse = wide(stats_ref[1, at, :], plan.features)
    return (x_ref[at, :].astype(F32) - mean) * inverse, inverse


def read_vectors(vec_ref):
    count = vec_ref.shape[0] // 8
    parts = [vec_ref[8 * part : 8 * part + 8, :].astype(F32) for part in range(count)]
    return jnp.concatenate(parts, axis=1)


def received(carry_ref, wanted, states):
    value = jnp.where(wanted, carry_ref[0:1, :], 0.0)
    return value[:, :states], value[:, states:]


def enter_kernel(
    plan, me_ref, x_ref, stats_ref, b0_ref, b1_ref, vec_ref, masks_ref,
    normed_ref, source_ref, ends_ref, hold_ref, carry_ref, input_map_ref, params_ref,
    pack_ref,
):
    states = plan.states
    collect(
        plan, me_ref[0], plan.up[::-1], (b0_ref, b1_ref), 0, plan.own_rows, 0,
        [(0, 2 * plan.own_states, pack_ref, 0)],
    )
    input_map_ref[...] = dot(
        pack_ref[...].astype(BF16), regroup_matrix(states, plan.tensor)
    ).astype(BF16)
    vectors = read_vectors(vec_ref)
    gain, shift = vectors[0:1], vectors[1:2]
    speed = jnp.exp(vectors[5:6, :states])
    modulus = jnp.exp(-speed)
    rotation = jnp.exp(vectors[6:7, :states])
    rate = (modulus * jnp.cos(rotation), modulus * jnp.sin(rotation))
    rest = 1.0 - modulus * modulus
    gamma = jnp.exp(vectors[7:8, :states]) * jnp.sqrt(rest)
    params_ref[...] = jnp.concatenate(
        [
            jnp.concatenate(rate, axis=1),
            jnp.concatenate([gamma, speed], axis=1),
            jnp.concatenate([modulus, rest], axis=1),
            jnp.concatenate([rotation, rotation], axis=1),
            jnp.zeros((4, 2 * states), F32),
        ],
        axis=0,
    )
    gamma_pair = jnp.concatenate([gamma, gamma], axis=1)
    turn = turn_matrix().astype(BF16)

    def rows_step(index, _):
        at = plan.block_rows(index)
        standard, _ = standard_rows(plan, x_ref, stats_ref, at)
        normed = (standard * gain + shift).astype(BF16)
        normed_ref[at, :] = normed
        turned = turn_rows(turn, normed)
        drive = dot(turned, input_map_ref[...])
        source_ref[at, :] = drive * gamma_pair * wide(masks_ref[2, at, :], 2 * states)
        return 0

    lax.fori_loop(0, plan.blocks, rows_step, 0)
    ends_re, ends_im, hold = local_ends(plan, source_ref, masks_ref.at[0], rate, False)
    ends_ref[...] = jnp.concatenate([ends_re, ends_im], axis=1)
    hold_ref[...] = hold
    _, leaving = chunk_entries(plan, ends_re, ends_im, hold, rate, None, False)
    carry_ref[...] = jnp.broadcast_to(leaving, carry_ref.shape)


def middle_kernel(
    plan, me_ref, x_ref, grad_ref, normed_ref, source_ref, ends_ref, hold_ref, carry_ref,
    g0_ref, g1_ref, g2_ref, g3_ref, vec_ref, params_ref, masks_ref,
    mixed_ref, hidden_ref, lru_grad_ref, state_grad_ref, act_ref, unit_grad_ref, low_ref, sums_ref,
    pack_ref, wpack_ref, out_map_ref,
):
    states, features, units = plan.states, plan.features, plan.units
    pair = 2 * plan.own_states
    targets = [
        (0, pair, pack_ref, 0),
        (pair, units, wpack_ref, 0),
        (pair + units, units, wpack_ref, features),
    ]
    block_refs = (g0_ref, g1_ref, g2_ref, g3_ref)
    for order, base, rows, first in half_blocks(plan, plan.up_crossed, len(block_refs)):
        collect(plan, me_ref[0], order[::-1], block_refs, base, rows, first, targets)
    sign = jnp.where(grid_index((1, 2 * states), 1) < states, 1.0, -1.0)
    regroup = regroup_matrix(states, plan.tensor)
    out_map_ref[...] = (dot(pack_ref[...].astype(BF16), regroup) * sign).astype(BF16)
    rate = (params_ref[0:1, :states], params_ref[0:1, states:])
    start = received(carry_ref, me_ref[0] & 1 == 1, states)
    entries, _ = chunk_entries(
        plan, ends_ref[:, :states], ends_ref[:, states:], hold_ref[...], rate, start, False
    )
    rate_re = jnp.broadcast_to(rate[0], (SIDE, states))
    rate_im = jnp.broadcast_to(rate[1], (SIDE, states))

    def visit(tile, at, keep, state, extra):
        now_re, now_im = state
        held = wide(keep, states)
        pass_re, pass_im = held * rate_re, held * rate_im
        source = source_ref[at, :]
        next_re = (source[:, :states] + pass_re * now_re) - pass_im * now_im
        next_im = (source[:, states:] + pass_re * now_im) + pass_im * now_re
        hidden_ref[at, :states] = next_re
        hidden_ref[at, states:] = next_im
        return (next_re, next_im), extra

    scan_pass(plan, masks_ref.at[0], entries, 0, False, visit)
    vectors = read_vectors(vec_ref)
    skip = vectors[2:3]
    biases = jnp.concatenate([vectors[3:4], vectors[4:5]], axis=1)
    sums_ref[...] = jnp.zeros_like(sums_ref)
    turn = turn_matrix().astype(BF16)

    def rows_step(index, _):
        at = plan.block_rows(index)
        low = turn_rows(turn, hidden_ref[at, :].astype(BF16))
        low_ref[at, :] = low
        normed = normed_ref[at, :].astype(F32)
        lru = dot(low, out_map_ref[...], 1, 1) + skip * normed
        square = lru * lru
        bent = jnp.tanh(lru * (GELU_SCALE + (GELU_SCALE * GELU_CUBE) * square))
        half = 0.5 + 0.5 * bent
        act_wide = lru * half
        slope = half + act_wide * (1.0 - half) * (
            2.0 * GELU_SCALE + (6.0 * GELU_SCALE * GELU_CUBE) * square
        )
        act = act_wide.astype(BF16)
        act_ref[at, :] = act
        mapped = dot(act, wpack_ref[...].astype(BF16)) + biases
        value = mapped[:, :features]
        live_half = wide(0.5 * masks_ref[3, at, :], features)
        opening = live_half + live_half * jnp.tanh(0.5 * mapped[:, features:])
        gated = value * opening
        mixed_ref[at, :] = (x_ref[at, :].astype(F32) + gated).astype(BF16)
        value_grad = grad_ref[at, :].astype(F32) * opening
        gate_grad = value_grad * (value - gated)
        sums_ref[8:16, :] += fold_rows(value_grad)
        sums_ref[16:24, :] += fold_rows(gate_grad)
        unit_grad = jnp.concatenate([value_grad, gate_grad], axis=1).astype(BF16)
        unit_grad_ref[at, :] = unit_grad
        act_grad = dot(unit_grad, wpack_ref[...].astype(BF16), 1, 1)
        lru_grad = act_grad * slope
        sums_ref[0:8, :] += fold_rows(lru_grad * normed)
        lru_grad = lru_grad.astype(BF16)
        lru_grad_ref[at, :] = lru_grad
        turned = turn_rows(turn, lru_grad)
        state_grad_ref[at, :] = dot(turned, out_map_ref[...])
        return 0

    lax.fori_loop(0, plan.blocks, rows_step, 0)


def back_kernel(
    plan, me_ref, state_grad_ref, params_ref, masks_ref, back_ends_ref, back_hold_ref, back_ref
):
    states = plan.states
    back_rate = (params_ref[0:1, :states], -params_ref[0:1, states:])
    ends_re, ends_im, hold = local_ends(plan, state_grad_ref, masks_ref.at[1], back_rate, True)
    back_ends_ref[...] = jnp.concatenate([ends_re, ends_im], axis=1)
    back_hold_ref[...] = hold
    _, leaving = chunk_entries(plan, ends_re, ends_im, hold, back_rate, None, True)
    back_ref[...] = jnp.broadcast_to(leaving, back_ref.shape)


def weight_kernel(
    plan, me_ref, act_ref, unit_grad_ref, lru_grad_ref, low_ref, *refs
):
    outs, (full_ref, out_ref) = refs[:-2], refs[-2:]
    states, features, units = plan.states, plan.features, plan.units
    pair = 2 * plan.own_states
    sign = jnp.where(grid_index((1, 2 * states), 1) < states, 1.0, -1.0)
    full_ref[...] = dot(act_ref[...], unit_grad_ref[...], 0, 0)
    out_grad = dot(lru_grad_ref[...], low_ref[...], 0, 0) * sign
    out_ref[...] = dot(out_grad.astype(BF16), regroup_matrix(states, plan.tensor), 1, 1)
    targets = [
        (0, pair, out_ref, 0),
        (pair, units, full_ref, 0),
        (pair + units, units, full_ref, features),
    ]
    for half, (order, _, rows, first) in enumerate(half_blocks(plan, plan.down_crossed, 2)):
        pair_refs = outs[2 * half : 2 * half + 2]
        distribute(plan, me_ref[0], order, pair_refs, 0, rows, first, targets)


def leave_kernel(
    plan, me_ref, x_ref, stats_ref, normed_ref, source_ref, ends_ref, hold_ref, carry_ref, hidden_ref,
    state_grad_ref, lru_grad_ref, input_map_ref, vec_ref, params_ref, masks_ref, sums_ref,
    keep_ref, send_ref, normed_grad_ref,
    drive_grad_ref, low_ref, full_ref,
):
    states, features = plan.states, plan.features
    params = params_ref[...]
    rate = (params[0:1, :states], params[0:1, states:])
    gamma, speed = params[1:2, :states], params[1:2, states:]
    modulus, rest = params[2:3, :states], params[2:3, states:]
    rotation = params[3:4, :states]
    back_rate = (rate[0], -rate[1])
    start = received(carry_ref, me_ref[0] & 1 == 0, states)
    entries, _ = chunk_entries(
        plan, ends_ref[:, :states], ends_ref[:, states:], hold_ref[...], back_rate, start, True
    )
    zero = jnp.zeros((SIDE, states), F32)
    rate_re = jnp.broadcast_to(back_rate[0], zero.shape)
    rate_im = jnp.broadcast_to(back_rate[1], zero.shape)
    gamma_wide = jnp.broadcast_to(gamma, zero.shape)

    def visit(tile, at, keep, state, sums):
        now_re, now_im = state
        held = wide(keep, states)
        next_re, next_im = held * now_re, held * now_im
        hidden_re, hidden_im = hidden_ref[at, :states], hidden_ref[at, states:]
        now_re = (state_grad_ref[at, :states] + rate_re * next_re) - rate_im * next_im
        now_im = (state_grad_ref[at, states:] + rate_re * next_im) + rate_im * next_re
        sums = (
            sums[0] + (hidden_re * next_re + hidden_im * next_im),
            sums[1] + (hidden_re * next_im - hidden_im * next_re),
            sums[2] + (source_ref[at, :states] * now_re + source_ref[at, states:] * now_im),
        )
        scale = gamma_wide * wide(masks_ref[2, at, :], states)
        drive_grad_ref[at, :states] = scale * now_re
        drive_grad_ref[at, states:] = scale * now_im
        return (now_re, now_im), sums

    _, sums = scan_pass(plan, masks_ref.at[1], entries, (zero, zero, zero), True, visit)
    rate_sum_re, rate_sum_im, gamma_sum = (jnp.sum(part, axis=0, keepdims=True) for part in sums)
    nu_grad = speed * (
        gamma_sum * modulus * modulus / rest - (rate_sum_re * rate[0] + rate_sum_im * rate[1])
    )
    theta_grad = rotation * (rate_sum_im * rate[0] - rate_sum_re * rate[1])
    vectors = read_vectors(vec_ref)
    skip = vectors[2:3]
    gain_sum = jnp.zeros((8, features), F32)
    turn = turn_matrix().astype(BF16)

    def rows_step(index, sums):
        gain_sum, shift_sum = sums
        at = plan.block_rows(index)
        low = turn_rows(turn, drive_grad_ref[at, :].astype(BF16))
        low_ref[at, :] = low
        normed_grad = dot(low, input_map_ref[...], 1, 1) + skip * lru_grad_ref[at, :].astype(F32)
        normed_grad_ref[at, :] = normed_grad
        standard, _ = standard_rows(plan, x_ref, stats_ref, at)
        return gain_sum + fold_rows(normed_grad * standard), shift_sum + fold_rows(normed_grad)

    gain_sum, shift_sum = lax.fori_loop(0, plan.blocks, rows_step, (gain_sum, gain_sum))
    into = dot(normed_ref[...], low_ref[...], 0, 0)
    full_ref[...] = dot(into.astype(BF16), regroup_matrix(states, plan.tensor), 1, 1)
    distribute(
        plan, me_ref[0], plan.down, (keep_ref, send_ref), 0, plan.own_rows, 0,
        [(0, 2 * plan.own_states, full_ref, 0)],
    )
    empty = jnp.zeros((1, features - states), F32)
    vector_sums = jnp.concatenate(
        [jnp.sum(part, axis=0, keepdims=True) for part in (gain_sum, shift_sum)]
        + [
            jnp.sum(sums_ref[8 * place : 8 * place + 8, :], axis=0, keepdims=True)
            for place in range(3)
        ]
        + [jnp.concatenate([part, empty], axis=1) for part in (nu_grad, theta_grad, gamma_sum)],
        axis=0,
    )
    base = plan.own_rows * plan.count // 2
    for part in range(features // LANES):
        piece = vector_sums[:, part * LANES : (part + 1) * LANES]
        send_ref[base + 8 * part : base + 8 * part + 8, :] = piece.astype(BF16)


def last_kernel(plan, me_ref, *refs):
    b_keep, b_other, w_mine_ref, tail_ref = refs[:4]
    outs, held, sems = refs[4:18], refs[18:32], refs[32]
    own, units = plan.own_states, plan.units
    b_mine = b_keep[...].astype(F32) + b_other[...].astype(F32)
    w_mine = w_mine_ref[...]
    half = tail_ref.shape[0] // 2
    vectors = tail_ref[:half, :].astype(F32) + tail_ref[half:, :].astype(F32)
    count = half // 8
    vectors = jnp.concatenate([vectors[8 * part : 8 * part + 8] for part in range(count)], axis=1)
    band = me_ref[0] >> log2(plan.tensor)
    at = grid_index((plan.features, LANES), 0)
    lane = grid_index((plan.features, LANES), 1)

    def pick(length):
        chosen = jnp.where(at == band * length + lane, 1.0, 0.0)
        return lax.dot_general(
            vectors,
            chosen,
            (((1,), (0,)), ((), ())),
            precision=lax.Precision.HIGHEST,
            preferred_element_type=F32,
        )

    long, short = plan.own_rows, plan.states // plan.fsdp
    long_part, short_part = pick(long), pick(short)
    held[0][...] = b_mine[:, :own]
    held[1][...] = b_mine[:, own:]
    held[2][...] = w_mine[:, :own]
    held[3][...] = w_mine[:, own : 2 * own]
    held[4][...] = w_mine[:, 2 * own : 2 * own + units]
    held[5][...] = w_mine[:, 2 * own + units :]
    for place in range(8):
        part, length = (long_part, long) if place < 5 else (short_part, short)
        held[6 + place][...] = part[place : place + 1, :length]
    for copy in start_copies(list(zip(held, outs)), sems):
        copy.wait()


def input_kernel(plan, me_ref, x_ref, stats_ref, grad_ref, normed_grad_ref, vec_ref, input_grad_ref):
    gain = read_vectors(vec_ref)[0:1]

    def rows_step(index, _):
        at = plan.block_rows(index)
        standard, inverse = standard_rows(plan, x_ref, stats_ref, at)
        scaled = normed_grad_ref[at, :] * gain
        input_grad_ref[at, :] = grad_ref[at, :].astype(F32) + inverse * (
            scaled
            - jnp.mean(scaled, axis=1, keepdims=True)
            - standard * jnp.mean(scaled * standard, axis=1, keepdims=True)
        )
        return 0

    lax.fori_loop(0, plan.blocks, rows_step, 0)


def call(kernel, plan, outs, scratch, limit, time, *args, far_in=0, far_out=False):
    args = [*args[:1], *(pltpu.with_memory_space_constraint(a, pltpu.HBM) for a in args[1 : 1 + far_in]), *args[1 + far_in :]]
    whole = pl.BlockSpec(memory_space=pltpu.VMEM)
    far = pl.BlockSpec(memory_space=pltpu.HBM)
    return pl.pallas_call(
        functools.partial(kernel, plan),
        out_shape=outs,
        in_specs=[pl.BlockSpec(memory_space=pltpu.SMEM)]
        + [far] * far_in
        + [whole] * (len(args) - 1 - far_in),
        out_specs=[far if far_out else whole] * len(outs),
        scratch_shapes=scratch,
        compiler_params=pltpu.CompilerParams(vmem_limit_bytes=limit * MIB),
        cost_estimate=pl.CostEstimate(
            flops=int(time * 1e9), bytes_accessed=int(time * 3.5e6), transcendentals=0
        ),
    )(*args)


def shape(dims, dtype=F32):
    return jax.ShapeDtypeStruct(dims, dtype)


def after(value, *others):
    return lax.optimization_barrier((value, *others))[0]


def joined(*parts):
    return jnp.concatenate(parts, axis=0)


def gather_blocks(plan, first, summed, second, cover):
    count, width = plan.count, second.shape[1]
    tensor_bits = log2(plan.tensor)
    other = None

    def first_step(bit):
        rows = first.shape[0]
        if bit < tensor_bits:
            got = flip(first, bit, count)
            return got, joined(first, got), summed
        got = flip(joined(first, summed), bit, count)
        if other is None:
            got = after(got, cover, second_other)
        return got, joined(first, got[:rows]), summed + got[rows:]

    for bit in plan.far:
        second_other = flip(second if other is None else after(second, other), bit, count)
        other, first, summed = first_step(bit)
        second = joined(second, second_other)
    second = joined(second, flip(after(second, other), 1, count))
    other, first, summed = first_step(3)
    blocks = second.reshape(-1, plan.own_rows, width)
    size = plan.own_rows // plan.halves
    halves = [
        after(blocks[:, half * size : half * size + size].reshape(-1, width), other)
        for half in range(plan.halves)
    ]
    halves = [joined(part, flip(part, bit, count)) for part, bit in zip(halves, (3, 2))]
    other, first, summed = first_step(2)
    halves = [(part, flip(part, bit, count)) for part, bit in zip(halves, (2, 3))]
    other, first, summed = first_step(1)
    return first, flip(first, 0, count), summed, halves


def cut(value):
    count = value.shape[0] // 2
    return value[:count].astype(BF16), value[count:].astype(BF16)


def added(keep, other):
    return keep.astype(F32) + other.astype(F32)


def summed_step(keep, send, other):
    count = keep.shape[0]
    summed = added(send[count:], other[count:]).astype(BF16)
    keep, send = cut(added(keep, other[:count]))
    return keep, joined(send, summed)


def together(*values):
    return lax.optimization_barrier(values)


def shards(
    mesh,
    block_input,
    segments,
    ln_gain,
    ln_bias,
    b_real,
    b_imag,
    c_real,
    c_imag,
    nu_log,
    theta_log,
    gamma_log,
    d_skip,
    w_value,
    w_gate,
    b_value,
    b_gate,
    out_grad,
):
    band = lax.axis_index("fsdp")
    shard = lax.axis_index("tensor")
    rows, features = block_input.shape
    own = b_real.shape[1]
    plan = Plan(
        mesh, rows, segments.shape[0], features, own * mesh.shape["tensor"], w_value.shape[1]
    )
    states, units, chunks = plan.states, plan.units, plan.chunks
    me = (band * plan.tensor + shard).astype(jnp.int32).reshape(1)
    long, short = plan.own_rows, states // plan.fsdp
    vector_rows = 8 * features // LANES
    matrices = (b_real, b_imag, c_real, c_imag, w_value, w_gate)
    lines = [
        v.reshape(1, -1)
        for v in (ln_gain, ln_bias, d_skip, b_value, b_gate, nu_log, theta_log, gamma_log)
    ]
    block = 2 * own + 2 * units
    first, second = call(
        pack_kernel,
        plan,
        [shape((long + vector_rows, 2 * own), BF16), shape((long, block), BF16)],
        [pltpu.VMEM(v.shape, BF16) for v in (*matrices, *lines)] + [pltpu.SemaphoreType.DMA((14,))],
        4,
        1.5,
        me, *matrices, *lines,
        far_in=14,
    )
    stats, masks = call(
        token_kernel,
        plan,
        [shape((2, rows, LANES)), shape((4, rows, LANES))],
        [pltpu.VMEM((3, plan.group_rows // LANES, LANES), F32)],
        8,
        2,
        me, block_input, segments.reshape(-1, LANES),
    )
    b0, b1, vectors, halves = gather_blocks(plan, first[:long], first[long:], second, masks)

    pack_type = BF16 if long % 16 == 0 else F32
    full = (rows, 2 * states)
    normed, source, ends, hold, carry, input_map, params = call(
        enter_kernel,
        plan,
        [
            shape((rows, features), BF16),
            shape(full),
            shape((chunks, 2 * states)),
            shape((chunks, LANES)),
            shape((8, 2 * states)),
            shape((features, 2 * states), BF16),
            shape((8, 2 * states)),
        ],
        [pltpu.VMEM((features, 2 * states), pack_type)],
        8,
        0.3,
        me, block_input, stats, b0, b1, vectors, masks,
    )

    left = carry
    carry = flip(carry, 0, plan.count) if plan.pieces == 2 else jnp.zeros_like(carry)
    held = joined(*(part for part, _ in halves))
    held_other = flip(held, 0, plan.count)
    came = joined(*(after(got, left) for _, got in halves))
    came_other = flip(came, 0, plan.count)
    (
        mixed, hidden, lru_grad, state_grad, act, unit_grad, low, sums,
    ) = call(
        middle_kernel,
        plan,
        [
            shape((rows, features), BF16),
            shape(full),
            shape((rows, features), BF16),
            shape(full),
            shape((rows, features), BF16),
            shape((rows, 2 * features), BF16),
            shape(full, BF16),
            shape((24, features)),
        ],
        [
            pltpu.VMEM((features, 2 * states), pack_type),
            pltpu.VMEM((features, 2 * features), pack_type),
            pltpu.VMEM((features, 2 * states), BF16),
        ],
        24,
        10,
        me, block_input, out_grad, normed, source, ends, hold, carry,
        held, came, held_other, came_other, vectors, params, masks,
    )
    half_rows = plan.count // 2 * long
    pieces = plan.halves
    outs = call(
        weight_kernel,
        plan,
        [shape((half_rows // pieces, block), BF16)] * (2 * pieces),
        [
            pltpu.VMEM((features, 2 * features), F32),
            pltpu.VMEM((features, 2 * states), F32),
        ],
        10,
        2.5,
        me, act, unit_grad, lru_grad, low,
    )
    w_keeps, w_sends = outs[::2], outs[1::2]
    w_others = [flip(send, 0, plan.count) for send in w_sends]
    back_ends, back_hold, back = call(
        back_kernel,
        plan,
        [shape((chunks, 2 * states)), shape((chunks, LANES)), shape((8, 2 * states))],
        [],
        8,
        1,
        me, after(state_grad, *w_sends), params, masks,
    )
    back = flip(back, 0, plan.count) if plan.pieces == 2 else jnp.zeros_like(back)
    halves = [
        cut(added(keep, after(other, back_ends))) for keep, other in zip(w_keeps, w_others)
    ]
    w_others = [flip(half[1], bit, plan.count) for half, bit in zip(halves, (2, 3))]
    back_ends = after(back_ends, *(half[1] for half in halves))
    b_keep, b_send, normed_grad = call(
        leave_kernel,
        plan,
        [
            shape((half_rows, 2 * own), BF16),
            shape((half_rows + vector_rows, 2 * own), BF16),
            shape((rows, features)),
        ],
        [
            pltpu.VMEM(full, F32),
            pltpu.VMEM(full, BF16),
            pltpu.VMEM((features, 2 * states), F32),
        ],
        14,
        4.5,
        me, block_input, stats, normed, source, back_ends, back_hold, back, hidden,
        state_grad, lru_grad, input_map, vectors, params, masks, sums,
    )
    w_others = [after(other, b_keep) for other in w_others]
    halves = [cut(added(half[0], other)) for half, other in zip(halves, w_others)]
    b_other = after(flip(b_send, 0, plan.count), *(half[1] for half in halves))
    b_keep, b_send = summed_step(b_keep, b_send, b_other)
    b_other = flip(b_send, 1, plan.count)
    w_others = [flip(half[1], bit, plan.count) for half, bit in zip(halves, (3, 2))]
    b_keep, b_send = summed_step(b_keep, b_send, b_other)
    halves = [cut(added(half[0], after(other, b_send))) for half, other in zip(halves, w_others)]
    w_keep = joined(*(half[0] for half in halves))
    w_send = joined(*(half[1] for half in halves))
    for bit in range(2, plan.bits - 1):
        w_bit = 1 if bit == 2 else bit + 1
        b_other = flip(b_send, bit, plan.count)
        w_other = flip(w_send, w_bit, plan.count)
        b_keep, b_send = summed_step(b_keep, b_send, b_other)
        if w_bit < plan.bits - 1:
            w_other = after(w_other, b_send)
            total = added(w_keep, w_other).reshape(pieces, -1, block)
            size = total.shape[1] // 2
            w_keep = total[:, :size].reshape(-1, block).astype(BF16)
            w_send = total[:, size:].reshape(-1, block).astype(BF16)
    (input_grad,) = call(
        input_kernel,
        plan,
        [shape((rows, features))],
        [],
        8,
        2.5,
        me, block_input, stats, out_grad, after(normed_grad, b_send), vectors,
    )
    w_mine = added(w_keep, w_other)
    b_other = after(flip(b_send, plan.bits - 1, plan.count), w_mine, input_grad)
    b_other, tail = b_other[:long], joined(b_send[long:], b_other[long:])
    small = (
        [(long, own)] * 4 + [(long, units)] * 2 + [(1, long)] * 5 + [(1, short)] * 3
    )
    (
        b_real_grad, b_imag_grad, c_real_grad, c_imag_grad, value_grad, gate_grad, *lines
    ) = call(
        last_kernel,
        plan,
        [shape(dims) for dims in small],
        [pltpu.VMEM(dims, F32) for dims in small] + [pltpu.SemaphoreType.DMA((14,))],
        4,
        2,
        me, b_keep, b_other, w_mine, tail,
        far_out=True,
    )
    gain_grad, bias_grad, skip_grad, value_line, gate_line, nu_grad, theta_grad, gamma_grad = (
        line.reshape(-1) for line in lines
    )
    return (
        mixed,
        input_grad,
        gain_grad,
        bias_grad,
        b_real_grad,
        b_imag_grad,
        c_real_grad,
        c_imag_grad,
        nu_grad,
        theta_grad,
        gamma_grad,
        skip_grad,
        value_grad,
        gate_grad,
        value_line,
        gate_line,
    )


def solution(mesh):
    in_specs = (
        P(("fsdp", "tensor"), None),
        P("fsdp"),
        P("fsdp"),
        P("fsdp"),
        P("fsdp", "tensor"),
        P("fsdp", "tensor"),
        P("fsdp", "tensor"),
        P("fsdp", "tensor"),
        P("fsdp"),
        P("fsdp"),
        P("fsdp"),
        P("fsdp"),
        P("fsdp", "tensor"),
        P("fsdp", "tensor"),
        P("fsdp"),
        P("fsdp"),
        P(("fsdp", "tensor"), None),
    )
    out_specs = (
        P(("fsdp", "tensor"), None),
        P(("fsdp", "tensor"), None),
        P("fsdp"),
        P("fsdp"),
        P("fsdp", "tensor"),
        P("fsdp", "tensor"),
        P("fsdp", "tensor"),
        P("fsdp", "tensor"),
        P("fsdp"),
        P("fsdp"),
        P("fsdp"),
        P("fsdp"),
        P("fsdp", "tensor"),
        P("fsdp", "tensor"),
        P("fsdp"),
        P("fsdp"),
    )
    return jax.shard_map(
        functools.partial(shards, mesh),
        mesh=mesh,
        in_specs=in_specs,
        out_specs=out_specs,
        check_vma=False,
    )
```

```python
import functools
import math

import jax
import jax.numpy as jnp
from jax import lax
from jax.experimental import pallas as pl
from jax.experimental.pallas import tpu as pltpu
from jax.sharding import PartitionSpec as P

SEQ_LEN = 2048
LANES = 128
TILE = 256
SIDE = 16
BLOCK = 1024
AXES = ("fsdp", "tensor")
norm_epsilon = 1e-05
GELU_SCALE = math.sqrt(2.0 / math.pi)
GELU_CUBE = 0.044715
F32 = jnp.float32
BF16 = jnp.bfloat16
MIB = 1024 * 1024


def log2(value):
    return value.bit_length() - 1


def flip(value, bit, count):
    return lax.ppermute(value, AXES, [(i, i ^ (1 << bit)) for i in range(count)])


def dot(left, right, left_dim=1, right_dim=0):
    return lax.dot_general(
        left, right, (((left_dim,), (right_dim,)), ((), ())), preferred_element_type=F32
    )


def fold_rows(value):
    rows, width = value.shape
    return jnp.sum(value.reshape(rows // 8, 8, width), axis=0)


def wide(mask, width):
    return jnp.concatenate([mask] * (width // LANES), axis=1)


def grid_index(dims, axis):
    return lax.broadcasted_iota(jnp.int32, dims, axis)


def regroup_matrix(states, shards):
    own = log2(states // shards)
    width = 2 * states
    source = grid_index((width, width), 0)
    target = grid_index((width, width), 1)
    part = (source >> own) & 1
    place = part * states + ((source >> (own + 1)) << own) + (source & ((1 << own) - 1))
    return jnp.where(place == target, 1.0, 0.0).astype(BF16)


def turn_matrix():
    source = grid_index((TILE, TILE), 0)
    target = grid_index((TILE, TILE), 1)
    bits = log2(SIDE)
    place = ((source & (SIDE - 1)) << bits) + (source >> bits)
    return jnp.where(place == target, 1.0, 0.0)


def turn_rows(turn, value):
    parts = [dot(turn, value[at : at + TILE]) for at in range(0, value.shape[0], TILE)]
    return jnp.concatenate(parts, axis=0).astype(BF16)


class Plan:
    def __init__(self, mesh, rows, group_rows, features, states, units):
        self.fsdp = mesh.shape["fsdp"]
        self.tensor = mesh.shape["tensor"]
        self.count = self.fsdp * self.tensor
        self.bits = log2(self.count)
        far = list(range(self.bits - 1, 3, -1))
        self.far = far
        self.up = [*far, 3, 2, 1, 0]
        self.up_crossed = ([*far, 1, 3, 2, 0], [*far, 1, 2, 3, 0])
        self.down = [0, 1, 2, 3, *far[::-1]]
        self.down_crossed = ([0, 2, 3, 1, *far[::-1]], [0, 3, 2, 1, *far[::-1]])
        self.halves = 2 if features // self.fsdp >= 32 else 1
        self.rows = rows
        self.group_rows = group_rows
        self.features = features
        self.states = states
        self.units = units
        self.own_states = states // self.tensor
        self.own_rows = features // self.fsdp
        self.pieces = SEQ_LEN // rows
        self.tiles = rows // TILE
        self.chunks = self.tiles * SIDE
        self.block = BLOCK if rows % BLOCK == 0 else TILE
        self.blocks = rows // self.block

    def slot_owner(self, slot, me, order):
        owner = me
        for place, bit in enumerate(order):
            owner = owner ^ (((slot >> (self.bits - 1 - place)) & 1) << bit)
        shift = log2(self.tensor)
        return owner >> shift, owner & (self.tensor - 1)

    def block_rows(self, index):
        return pl.ds(pl.multiple_of(index * self.block, self.block), self.block)


def step_rows(tile, place):
    return pl.ds(pl.multiple_of(tile * TILE + place * SIDE, SIDE), SIDE)


def scan_pass(plan, keep_ref, start, extra, reverse, visit):
    def step(index, carried):
        now, extra = carried
        place = SIDE - 1 - index if reverse else index
        after = []
        for tile in range(plan.tiles):
            at = step_rows(tile, place)
            state, extra = visit(tile, at, keep_ref[at, :], now[tile], extra)
            after.append(state)
        return after, extra

    return lax.fori_loop(0, SIDE, step, (start, extra), unroll=True)


def local_ends(plan, source_ref, keep_ref, rate, reverse):
    states = plan.states
    zero = jnp.zeros((SIDE, states), F32)
    rate_re = jnp.broadcast_to(rate[0], zero.shape)
    rate_im = jnp.broadcast_to(rate[1], zero.shape)
    one = jnp.ones((SIDE, LANES), F32)

    def visit(tile, at, keep, state, extra):
        now_re, now_im, hold = state
        held = wide(keep, states)
        pass_re, pass_im = held * rate_re, held * rate_im
        source = source_ref[at, :]
        next_re = (source[:, :states] + pass_re * now_re) - pass_im * now_im
        next_im = (source[:, states:] + pass_re * now_im) + pass_im * now_re
        return (next_re, next_im, hold * keep), extra

    ends, _ = scan_pass(plan, keep_ref, [(zero, zero, one)] * plan.tiles, 0, reverse, visit)
    return tuple(jnp.concatenate([end[part] for end in ends], axis=0) for part in range(3))


def shifted(value, distance, reverse):
    count = value.shape[0]
    row = grid_index(value.shape, 0)
    if reverse:
        moved = pltpu.roll(value, count - distance, 0)
        return jnp.where(row < count - distance, moved, 0.0)
    moved = pltpu.roll(value, distance, 0)
    return jnp.where(row >= distance, moved, 0.0)


def chunk_entries(plan, ends_re, ends_im, hold, rate, start, reverse):
    states, count = plan.states, plan.chunks
    power_re, power_im = rate
    for _ in range(log2(SIDE)):
        power_re, power_im = power_re * power_re - power_im * power_im, 2.0 * power_re * power_im
    first = count - 1 if reverse else 0
    if start is not None:
        at_first = grid_index((count, states), 0) == first
        held = jnp.where(at_first, wide(hold, states), 0.0)
        pass_re, pass_im = held * power_re, held * power_im
        ends_re = ends_re + (pass_re * start[0] - pass_im * start[1])
        ends_im = ends_im + (pass_re * start[1] + pass_im * start[0])
    distance = 1
    while distance < count:
        earlier_re = shifted(ends_re, distance, reverse)
        earlier_im = shifted(ends_im, distance, reverse)
        held = wide(hold, states)
        pass_re, pass_im = held * power_re, held * power_im
        ends_re = ends_re + (pass_re * earlier_re - pass_im * earlier_im)
        ends_im = ends_im + (pass_re * earlier_im + pass_im * earlier_re)
        hold = hold * shifted(hold, distance, reverse)
        power_re, power_im = power_re * power_re - power_im * power_im, 2.0 * power_re * power_im
        distance *= 2
    last = slice(0, 1) if reverse else slice(count - 1, count)
    leaving = jnp.concatenate([ends_re[last], ends_im[last]], axis=1)
    if start is None:
        return None, leaving
    entry_re = shifted(ends_re, 1, reverse) + jnp.where(at_first, start[0], 0.0)
    entry_im = shifted(ends_im, 1, reverse) + jnp.where(at_first, start[1], 0.0)
    entries = []
    for tile in range(plan.tiles):
        at = slice(tile * SIDE, (tile + 1) * SIDE)
        entries.append((entry_re[at], entry_im[at]))
    return entries, leaving


def block_places(plan, me, order, refs, base, rows, start):
    slot = 0
    for ref in refs:
        for place in range(plan.count // len(refs)):
            band, shard = plan.slot_owner(slot, me, order)
            slot += 1
            first = pl.multiple_of(band * plan.own_rows + start, rows)
            yield ref, base + place * rows, pl.ds(first, rows), shard


def collect(plan, me, order, refs, base, rows, start, targets):
    for ref, row, at, shard in block_places(plan, me, order, refs, base, rows, start):
        for first, width, out_ref, lanes in targets:
            column = pl.multiple_of(lanes + shard * width, LANES)
            out_ref[at, pl.ds(column, width)] = ref[row : row + rows, first : first + width].astype(
                out_ref.dtype
            )


def distribute(plan, me, order, refs, base, rows, start, targets):
    for ref, row, at, shard in block_places(plan, me, order, refs, base, rows, start):
        for first, width, full_ref, lanes in targets:
            column = pl.multiple_of(lanes + shard * width, LANES)
            ref[row : row + rows, first : first + width] = full_ref[at, pl.ds(column, width)].astype(
                ref.dtype
            )


def half_blocks(plan, orders, arrays):
    rows = plan.own_rows // plan.halves
    for half in range(plan.halves):
        yield orders[half], half * plan.count // arrays * rows, rows, half * rows


def start_copies(pairs, sems):
    copies = [
        pltpu.make_async_copy(source, target, sems.at[place])
        for place, (source, target) in enumerate(pairs)
    ]
    for copy in copies:
        copy.start()
    return copies


def pack_kernel(plan, me_ref, *refs):
    sources, outs, held, sems = refs[:14], refs[14:16], refs[16:30], refs[30]
    copies = start_copies(list(zip(sources, held)), sems)
    first_ref, second_ref = outs
    band = me_ref[0] >> log2(plan.tensor)
    rows, features = plan.own_rows, plan.features
    for copy in copies:
        copy.wait()
    first_ref[:rows, :] = jnp.concatenate([held[0][...], held[1][...]], axis=1)
    second_ref[...] = jnp.concatenate([ref[...] for ref in held[2:6]], axis=1)
    placed = []
    lane = grid_index((1, features), 1)
    for ref in held[6:]:
        length = ref.shape[1]
        value = ref[...].astype(F32)
        value = jnp.concatenate([value] * (features // length), axis=1)
        placed.append(jnp.where((lane >> log2(length)) == band, value, 0.0))
    placed = jnp.concatenate(placed, axis=0).astype(BF16)
    for part in range(features // LANES):
        first_ref[rows + 8 * part : rows + 8 * part + 8, :] = placed[
            :, part * LANES : (part + 1) * LANES
        ]


def token_kernel(
    plan, me_ref, x_ref, segments_ref, stats_ref, masks_ref, turn_ref, regroup_ref, flags_ref
):
    shard = me_ref[0] & (plan.tensor - 1)
    ids = segments_ref[...]
    count = ids.shape[0]
    lane = grid_index(ids.shape, 1)
    position = (grid_index(ids.shape, 0) * LANES + lane) & (SEQ_LEN - 1)
    turned = pltpu.roll(ids, 1, 1)
    before = jnp.where(lane == 0, pltpu.roll(turned, 1, 0), turned)
    turned = pltpu.roll(ids, LANES - 1, 1)
    after = jnp.where(lane == LANES - 1, pltpu.roll(turned, count - 1, 0), turned)
    flags_ref[0] = jnp.where((position > 0) & (ids == before), 1.0, 0.0)
    flags_ref[1] = jnp.where((position < SEQ_LEN - 1) & (ids == after), 1.0, 0.0)
    flags_ref[2] = jnp.where(ids > 0, 1.0, 0.0)
    turn = turn_matrix()
    turn_ref[...] = turn.astype(BF16)
    regroup_ref[...] = regroup_matrix(plan.states, plan.tensor)
    plain = jnp.where(grid_index((TILE, TILE), 0) == grid_index((TILE, TILE), 1), 1.0, 0.0)
    ones = jnp.ones((TILE, LANES), BF16)
    per_tile = TILE // LANES
    own = plan.rows // LANES
    flags = [flags_ref[kind, pl.ds(pl.multiple_of(shard * own, own), own), :] for kind in range(3)]
    for tile in range(plan.tiles):
        at = slice(tile * TILE, (tile + 1) * TILE)
        for kind in range(4):
            rows = flags[min(kind, 2)][tile * per_tile : (tile + 1) * per_tile, :]
            line = jnp.concatenate([rows[part : part + 1, :] for part in range(per_tile)], axis=1)
            spread = (plain if kind == 3 else turn) * line
            masks_ref[kind, at, :] = dot(spread.astype(BF16), ones)

    def rows_step(index, _):
        at = plan.block_rows(index)
        values = x_ref[at, :].astype(F32)
        mean = jnp.mean(values, axis=1, keepdims=True)
        centred = values - mean
        inverse = lax.rsqrt(jnp.mean(centred * centred, axis=1, keepdims=True) + norm_epsilon)
        stats_ref[0, at, :] = jnp.broadcast_to(mean, (plan.block, LANES))
        stats_ref[1, at, :] = jnp.broadcast_to(inverse, (plan.block, LANES))
        return 0

    lax.fori_loop(0, plan.blocks, rows_step, 0)


def standard_rows(plan, x_ref, stats_ref, at):
    mean = wide(stats_ref[0, at, :], plan.features)
    inverse = wide(stats_ref[1, at, :], plan.features)
    return (x_ref[at, :].astype(F32) - mean) * inverse, inverse


def read_vectors(vec_ref):
    count = vec_ref.shape[0] // 8
    parts = [vec_ref[8 * part : 8 * part + 8, :].astype(F32) for part in range(count)]
    return jnp.concatenate(parts, axis=1)


def received(carry_ref, wanted, states):
    value = jnp.where(wanted, carry_ref[0:1, :], 0.0)
    return value[:, :states], value[:, states:]


def enter_kernel(
    plan, me_ref, x_ref, stats_ref, b0_ref, b1_ref, vec_ref, masks_ref, turn_ref, regroup_ref,
    normed_ref, source_ref, ends_ref, hold_ref, carry_ref, input_map_ref, params_ref,
    pack_ref,
):
    states = plan.states
    collect(
        plan, me_ref[0], plan.up[::-1], (b0_ref, b1_ref), 0, plan.own_rows, 0,
        [(0, 2 * plan.own_states, pack_ref, 0)],
    )
    input_map_ref[...] = dot(
        pack_ref[...].astype(BF16), regroup_ref[...]
    ).astype(BF16)
    vectors = read_vectors(vec_ref)
    gain, shift = vectors[0:1], vectors[1:2]
    speed = jnp.exp(vectors[5:6, :states])
    modulus = jnp.exp(-speed)
    rotation = jnp.exp(vectors[6:7, :states])
    rate = (modulus * jnp.cos(rotation), modulus * jnp.sin(rotation))
    rest = 1.0 - modulus * modulus
    gamma = jnp.exp(vectors[7:8, :states]) * jnp.sqrt(rest)
    params_ref[...] = jnp.concatenate(
        [
            jnp.concatenate(rate, axis=1),
            jnp.concatenate([gamma, speed], axis=1),
            jnp.concatenate([modulus, rest], axis=1),
            jnp.concatenate([rotation, rotation], axis=1),
            jnp.zeros((4, 2 * states), F32),
        ],
        axis=0,
    )
    gamma_pair = jnp.concatenate([gamma, gamma], axis=1)
    turn = turn_ref[...]

    def rows_step(index, _):
        at = plan.block_rows(index)
        standard, _ = standard_rows(plan, x_ref, stats_ref, at)
        normed = (standard * gain + shift).astype(BF16)
        normed_ref[at, :] = normed
        turned = turn_rows(turn, normed)
        drive = dot(turned, input_map_ref[...])
        source_ref[at, :] = drive * gamma_pair * wide(masks_ref[2, at, :], 2 * states)
        return 0

    lax.fori_loop(0, plan.blocks, rows_step, 0)
    ends_re, ends_im, hold = local_ends(plan, source_ref, masks_ref.at[0], rate, False)
    ends_ref[...] = jnp.concatenate([ends_re, ends_im], axis=1)
    hold_ref[...] = hold
    _, leaving = chunk_entries(plan, ends_re, ends_im, hold, rate, None, False)
    carry_ref[...] = jnp.broadcast_to(leaving, carry_ref.shape)


def middle_kernel(
    plan, me_ref, x_ref, grad_ref, normed_ref, source_ref, ends_ref, hold_ref, carry_ref,
    g0_ref, g1_ref, g2_ref, g3_ref, vec_ref, params_ref, masks_ref, turn_ref, regroup_ref,
    mixed_ref, hidden_ref, lru_grad_ref, state_grad_ref, act_ref, unit_grad_ref, low_ref, sums_ref,
    pack_ref, wpack_ref, out_map_ref,
):
    states, features, units = plan.states, plan.features, plan.units
    pair = 2 * plan.own_states
    targets = [
        (0, pair, pack_ref, 0),
        (pair, units, wpack_ref, 0),
        (pair + units, units, wpack_ref, features),
    ]
    block_refs = (g0_ref, g1_ref, g2_ref, g3_ref)
    for order, base, rows, first in half_blocks(plan, plan.up_crossed, len(block_refs)):
        collect(plan, me_ref[0], order[::-1], block_refs, base, rows, first, targets)
    sign = jnp.where(grid_index((1, 2 * states), 1) < states, 1.0, -1.0)
    regroup = regroup_ref[...]
    out_map_ref[...] = (dot(pack_ref[...].astype(BF16), regroup) * sign).astype(BF16)
    rate = (params_ref[0:1, :states], params_ref[0:1, states:])
    start = received(carry_ref, me_ref[0] & 1 == 1, states)
    entries, _ = chunk_entries(
        plan, ends_ref[:, :states], ends_ref[:, states:], hold_ref[...], rate, start, False
    )
    rate_re = jnp.broadcast_to(rate[0], (SIDE, states))
    rate_im = jnp.broadcast_to(rate[1], (SIDE, states))

    def visit(tile, at, keep, state, extra):
        now_re, now_im = state
        held = wide(keep, states)
        pass_re, pass_im = held * rate_re, held * rate_im
        source = source_ref[at, :]
        next_re = (source[:, :states] + pass_re * now_re) - pass_im * now_im
        next_im = (source[:, states:] + pass_re * now_im) + pass_im * now_re
        hidden_ref[at, :states] = next_re
        hidden_ref[at, states:] = next_im
        return (next_re, next_im), extra

    scan_pass(plan, masks_ref.at[0], entries, 0, False, visit)
    vectors = read_vectors(vec_ref)
    skip = vectors[2:3]
    biases = jnp.concatenate([vectors[3:4], vectors[4:5]], axis=1)
    sums_ref[...] = jnp.zeros_like(sums_ref)
    turn = turn_ref[...]

    def rows_step(index, _):
        at = plan.block_rows(index)
        low = turn_rows(turn, hidden_ref[at, :].astype(BF16))
        low_ref[at, :] = low
        normed = normed_ref[at, :].astype(F32)
        lru = dot(low, out_map_ref[...], 1, 1) + skip * normed
        square = lru * lru
        bent = jnp.tanh(lru * (GELU_SCALE + (GELU_SCALE * GELU_CUBE) * square))
        half = 0.5 + 0.5 * bent
        act_wide = lru * half
        slope = half + act_wide * (1.0 - half) * (
            2.0 * GELU_SCALE + (6.0 * GELU_SCALE * GELU_CUBE) * square
        )
        act = act_wide.astype(BF16)
        act_ref[at, :] = act
        mapped = dot(act, wpack_ref[...].astype(BF16)) + biases
        value = mapped[:, :features]
        live_half = wide(0.5 * masks_ref[3, at, :], features)
        opening = live_half + live_half * jnp.tanh(0.5 * mapped[:, features:])
        gated = value * opening
        mixed_ref[at, :] = (x_ref[at, :].astype(F32) + gated).astype(BF16)
        value_grad = grad_ref[at, :].astype(F32) * opening
        gate_grad = value_grad * (value - gated)
        sums_ref[8:16, :] += fold_rows(value_grad)
        sums_ref[16:24, :] += fold_rows(gate_grad)
        unit_grad = jnp.concatenate([value_grad, gate_grad], axis=1).astype(BF16)
        unit_grad_ref[at, :] = unit_grad
        act_grad = dot(unit_grad, wpack_ref[...].astype(BF16), 1, 1)
        lru_grad = act_grad * slope
        sums_ref[0:8, :] += fold_rows(lru_grad * normed)
        lru_grad = lru_grad.astype(BF16)
        lru_grad_ref[at, :] = lru_grad
        turned = turn_rows(turn, lru_grad)
        state_grad_ref[at, :] = dot(turned, out_map_ref[...])
        return 0

    lax.fori_loop(0, plan.blocks, rows_step, 0)


def back_kernel(
    plan, me_ref, state_grad_ref, params_ref, masks_ref, back_ends_ref, back_hold_ref, back_ref
):
    states = plan.states
    back_rate = (params_ref[0:1, :states], -params_ref[0:1, states:])
    ends_re, ends_im, hold = local_ends(plan, state_grad_ref, masks_ref.at[1], back_rate, True)
    back_ends_ref[...] = jnp.concatenate([ends_re, ends_im], axis=1)
    back_hold_ref[...] = hold
    _, leaving = chunk_entries(plan, ends_re, ends_im, hold, back_rate, None, True)
    back_ref[...] = jnp.broadcast_to(leaving, back_ref.shape)


def weight_kernel(
    plan, me_ref, act_ref, unit_grad_ref, lru_grad_ref, low_ref, regroup_ref, *refs
):
    outs, (full_ref, out_ref) = refs[:-2], refs[-2:]
    states, features, units = plan.states, plan.features, plan.units
    pair = 2 * plan.own_states
    sign = jnp.where(grid_index((1, 2 * states), 1) < states, 1.0, -1.0)
    full_ref[...] = dot(act_ref[...], unit_grad_ref[...], 0, 0)
    out_grad = dot(lru_grad_ref[...], low_ref[...], 0, 0) * sign
    out_ref[...] = dot(out_grad.astype(BF16), regroup_ref[...], 1, 1)
    targets = [
        (0, pair, out_ref, 0),
        (pair, units, full_ref, 0),
        (pair + units, units, full_ref, features),
    ]
    for half, (order, _, rows, first) in enumerate(half_blocks(plan, plan.down_crossed, 2)):
        pair_refs = outs[2 * half : 2 * half + 2]
        distribute(plan, me_ref[0], order, pair_refs, 0, rows, first, targets)


def leave_kernel(
    plan, me_ref, x_ref, stats_ref, normed_ref, source_ref, ends_ref, hold_ref, carry_ref, hidden_ref,
    state_grad_ref, lru_grad_ref, input_map_ref, vec_ref, params_ref, masks_ref, sums_ref,
    turn_ref, regroup_ref,
    keep_ref, send_ref, normed_grad_ref,
    drive_grad_ref, low_ref, full_ref,
):
    states, features = plan.states, plan.features
    params = params_ref[...]
    rate = (params[0:1, :states], params[0:1, states:])
    gamma, speed = params[1:2, :states], params[1:2, states:]
    modulus, rest = params[2:3, :states], params[2:3, states:]
    rotation = params[3:4, :states]
    back_rate = (rate[0], -rate[1])
    start = received(carry_ref, me_ref[0] & 1 == 0, states)
    entries, _ = chunk_entries(
        plan, ends_ref[:, :states], ends_ref[:, states:], hold_ref[...], back_rate, start, True
    )
    zero = jnp.zeros((SIDE, states), F32)
    rate_re = jnp.broadcast_to(back_rate[0], zero.shape)
    rate_im = jnp.broadcast_to(back_rate[1], zero.shape)
    gamma_wide = jnp.broadcast_to(gamma, zero.shape)

    def visit(tile, at, keep, state, sums):
        now_re, now_im = state
        held = wide(keep, states)
        next_re, next_im = held * now_re, held * now_im
        hidden_re, hidden_im = hidden_ref[at, :states], hidden_ref[at, states:]
        now_re = (state_grad_ref[at, :states] + rate_re * next_re) - rate_im * next_im
        now_im = (state_grad_ref[at, states:] + rate_re * next_im) + rate_im * next_re
        sums = (
            sums[0] + (hidden_re * next_re + hidden_im * next_im),
            sums[1] + (hidden_re * next_im - hidden_im * next_re),
            sums[2] + (source_ref[at, :states] * now_re + source_ref[at, states:] * now_im),
        )
        scale = gamma_wide * wide(masks_ref[2, at, :], states)
        drive_grad_ref[at, :states] = scale * now_re
        drive_grad_ref[at, states:] = scale * now_im
        return (now_re, now_im), sums

    _, sums = scan_pass(plan, masks_ref.at[1], entries, (zero, zero, zero), True, visit)
    rate_sum_re, rate_sum_im, gamma_sum = (jnp.sum(part, axis=0, keepdims=True) for part in sums)
    nu_grad = speed * (
        gamma_sum * modulus * modulus / rest - (rate_sum_re * rate[0] + rate_sum_im * rate[1])
    )
    theta_grad = rotation * (rate_sum_im * rate[0] - rate_sum_re * rate[1])
    vectors = read_vectors(vec_ref)
    skip = vectors[2:3]
    gain_sum = jnp.zeros((8, features), F32)
    turn = turn_ref[...]

    def rows_step(index, sums):
        gain_sum, shift_sum = sums
        at = plan.block_rows(index)
        low = turn_rows(turn, drive_grad_ref[at, :].astype(BF16))
        low_ref[at, :] = low
        normed_grad = dot(low, input_map_ref[...], 1, 1) + skip * lru_grad_ref[at, :].astype(F32)
        normed_grad_ref[at, :] = normed_grad
        standard, _ = standard_rows(plan, x_ref, stats_ref, at)
        return gain_sum + fold_rows(normed_grad * standard), shift_sum + fold_rows(normed_grad)

    gain_sum, shift_sum = lax.fori_loop(0, plan.blocks, rows_step, (gain_sum, gain_sum))
    into = dot(normed_ref[...], low_ref[...], 0, 0)
    full_ref[...] = dot(into.astype(BF16), regroup_ref[...], 1, 1)
    distribute(
        plan, me_ref[0], plan.down, (keep_ref, send_ref), 0, plan.own_rows, 0,
        [(0, 2 * plan.own_states, full_ref, 0)],
    )
    empty = jnp.zeros((1, features - states), F32)
    vector_sums = jnp.concatenate(
        [jnp.sum(part, axis=0, keepdims=True) for part in (gain_sum, shift_sum)]
        + [
            jnp.sum(sums_ref[8 * place : 8 * place + 8, :], axis=0, keepdims=True)
            for place in range(3)
        ]
        + [jnp.concatenate([part, empty], axis=1) for part in (nu_grad, theta_grad, gamma_sum)],
        axis=0,
    )
    base = plan.own_rows * plan.count // 2
    for part in range(features // LANES):
        piece = vector_sums[:, part * LANES : (part + 1) * LANES]
        send_ref[base + 8 * part : base + 8 * part + 8, :] = piece.astype(BF16)


def last_kernel(plan, me_ref, *refs):
    b_keep, b_other, w_mine_ref, tail_ref = refs[:4]
    outs, held, sems = refs[4:18], refs[18:32], refs[32]
    own, units = plan.own_states, plan.units
    b_mine = b_keep[...].astype(F32) + b_other[...].astype(F32)
    w_mine = w_mine_ref[...]
    half = tail_ref.shape[0] // 2
    vectors = tail_ref[:half, :].astype(F32) + tail_ref[half:, :].astype(F32)
    count = half // 8
    vectors = jnp.concatenate([vectors[8 * part : 8 * part + 8] for part in range(count)], axis=1)
    band = me_ref[0] >> log2(plan.tensor)
    at = grid_index((plan.features, LANES), 0)
    lane = grid_index((plan.features, LANES), 1)

    def pick(length):
        chosen = jnp.where(at == band * length + lane, 1.0, 0.0)
        return lax.dot_general(
            vectors,
            chosen,
            (((1,), (0,)), ((), ())),
            precision=lax.Precision.HIGHEST,
            preferred_element_type=F32,
        )

    long, short = plan.own_rows, plan.states // plan.fsdp
    long_part, short_part = pick(long), pick(short)
    held[0][...] = b_mine[:, :own]
    held[1][...] = b_mine[:, own:]
    held[2][...] = w_mine[:, :own]
    held[3][...] = w_mine[:, own : 2 * own]
    held[4][...] = w_mine[:, 2 * own : 2 * own + units]
    held[5][...] = w_mine[:, 2 * own + units :]
    for place in range(8):
        part, length = (long_part, long) if place < 5 else (short_part, short)
        held[6 + place][...] = part[place : place + 1, :length]
    for copy in start_copies(list(zip(held, outs)), sems):
        copy.wait()


def input_kernel(plan, me_ref, x_ref, stats_ref, grad_ref, normed_grad_ref, vec_ref, input_grad_ref):
    gain = read_vectors(vec_ref)[0:1]

    def rows_step(index, _):
        at = plan.block_rows(index)
        standard, inverse = standard_rows(plan, x_ref, stats_ref, at)
        scaled = normed_grad_ref[at, :] * gain
        input_grad_ref[at, :] = grad_ref[at, :].astype(F32) + inverse * (
            scaled
            - jnp.mean(scaled, axis=1, keepdims=True)
            - standard * jnp.mean(scaled * standard, axis=1, keepdims=True)
        )
        return 0

    lax.fori_loop(0, plan.blocks, rows_step, 0)


def call(kernel, plan, outs, scratch, limit, time, *args, far_in=0, far_out=False):
    args = [*args[:1], *(pltpu.with_memory_space_constraint(a, pltpu.HBM) for a in args[1 : 1 + far_in]), *args[1 + far_in :]]
    whole = pl.BlockSpec(memory_space=pltpu.VMEM)
    far = pl.BlockSpec(memory_space=pltpu.HBM)
    return pl.pallas_call(
        functools.partial(kernel, plan),
        out_shape=outs,
        in_specs=[pl.BlockSpec(memory_space=pltpu.SMEM)]
        + [far] * far_in
        + [whole] * (len(args) - 1 - far_in),
        out_specs=[far if far_out else whole] * len(outs),
        scratch_shapes=scratch,
        compiler_params=pltpu.CompilerParams(vmem_limit_bytes=limit * MIB),
        cost_estimate=pl.CostEstimate(
            flops=int(time * 1e9), bytes_accessed=int(time * 3.5e6), transcendentals=0
        ),
    )(*args)


def shape(dims, dtype=F32):
    return jax.ShapeDtypeStruct(dims, dtype)


def after(value, *others):
    return lax.optimization_barrier((value, *others))[0]


def joined(*parts):
    return jnp.concatenate(parts, axis=0)


def gather_blocks(plan, first, summed, second, cover):
    count, width = plan.count, second.shape[1]
    tensor_bits = log2(plan.tensor)
    other = None

    def first_step(bit):
        rows = first.shape[0]
        if bit < tensor_bits:
            got = flip(first, bit, count)
            return got, joined(first, got), summed
        got = flip(joined(first, summed), bit, count)
        if other is None:
            got = after(got, cover, second_other)
        return got, joined(first, got[:rows]), summed + got[rows:]

    for bit in plan.far:
        second_other = flip(second if other is None else after(second, other), bit, count)
        other, first, summed = first_step(bit)
        second = joined(second, second_other)
    second = joined(second, flip(after(second, other), 1, count))
    other, first, summed = first_step(3)
    blocks = second.reshape(-1, plan.own_rows, width)
    size = plan.own_rows // plan.halves
    halves = [
        after(blocks[:, half * size : half * size + size].reshape(-1, width), other)
        for half in range(plan.halves)
    ]
    halves = [joined(part, flip(part, bit, count)) for part, bit in zip(halves, (3, 2))]
    other, first, summed = first_step(2)
    halves = [(part, flip(part, bit, count)) for part, bit in zip(halves, (2, 3))]
    other, first, summed = first_step(1)
    return first, flip(first, 0, count), summed, halves


def cut(value):
    count = value.shape[0] // 2
    return value[:count].astype(BF16), value[count:].astype(BF16)


def added(keep, other):
    return keep.astype(F32) + other.astype(F32)


def summed_step(keep, send, other):
    count = keep.shape[0]
    summed = added(send[count:], other[count:]).astype(BF16)
    keep, send = cut(added(keep, other[:count]))
    return keep, joined(send, summed)


def together(*values):
    return lax.optimization_barrier(values)


def shards(
    mesh,
    block_input,
    segments,
    ln_gain,
    ln_bias,
    b_real,
    b_imag,
    c_real,
    c_imag,
    nu_log,
    theta_log,
    gamma_log,
    d_skip,
    w_value,
    w_gate,
    b_value,
    b_gate,
    out_grad,
):
    band = lax.axis_index("fsdp")
    shard = lax.axis_index("tensor")
    rows, features = block_input.shape
    own = b_real.shape[1]
    plan = Plan(
        mesh, rows, segments.shape[0], features, own * mesh.shape["tensor"], w_value.shape[1]
    )
    states, units, chunks = plan.states, plan.units, plan.chunks
    me = (band * plan.tensor + shard).astype(jnp.int32).reshape(1)
    long, short = plan.own_rows, states // plan.fsdp
    vector_rows = 8 * features // LANES
    matrices = (b_real, b_imag, c_real, c_imag, w_value, w_gate)
    lines = [
        v.reshape(1, -1)
        for v in (ln_gain, ln_bias, d_skip, b_value, b_gate, nu_log, theta_log, gamma_log)
    ]
    block = 2 * own + 2 * units
    first, second = call(
        pack_kernel,
        plan,
        [shape((long + vector_rows, 2 * own), BF16), shape((long, block), BF16)],
        [pltpu.VMEM(v.shape, BF16) for v in (*matrices, *lines)] + [pltpu.SemaphoreType.DMA((14,))],
        4,
        1.5,
        me, *matrices, *lines,
        far_in=14,
    )
    stats, masks, turn, regroup = call(
        token_kernel,
        plan,
        [
            shape((2, rows, LANES)),
            shape((4, rows, LANES)),
            shape((TILE, TILE), BF16),
            shape((2 * states, 2 * states), BF16),
        ],
        [pltpu.VMEM((3, plan.group_rows // LANES, LANES), F32)],
        8,
        2,
        me, block_input, segments.reshape(-1, LANES),
    )
    b0, b1, vectors, halves = gather_blocks(plan, first[:long], first[long:], second, masks)

    pack_type = BF16 if long % 16 == 0 else F32
    full = (rows, 2 * states)
    normed, source, ends, hold, carry, input_map, params = call(
        enter_kernel,
        plan,
        [
            shape((rows, features), BF16),
            shape(full),
            shape((chunks, 2 * states)),
            shape((chunks, LANES)),
            shape((8, 2 * states)),
            shape((features, 2 * states), BF16),
            shape((8, 2 * states)),
        ],
        [pltpu.VMEM((features, 2 * states), pack_type)],
        8,
        0.3,
        me, block_input, stats, b0, b1, vectors, masks, turn, regroup,
    )

    left = carry
    carry = flip(carry, 0, plan.count) if plan.pieces == 2 else jnp.zeros_like(carry)
    held = joined(*(part for part, _ in halves))
    held_other = flip(held, 0, plan.count)
    came = joined(*(after(got, left) for _, got in halves))
    came_other = flip(came, 0, plan.count)
    (
        mixed, hidden, lru_grad, state_grad, act, unit_grad, low, sums,
    ) = call(
        middle_kernel,
        plan,
        [
            shape((rows, features), BF16),
            shape(full),
            shape((rows, features), BF16),
            shape(full),
            shape((rows, features), BF16),
            shape((rows, 2 * features), BF16),
            shape(full, BF16),
            shape((24, features)),
        ],
        [
            pltpu.VMEM((features, 2 * states), pack_type),
            pltpu.VMEM((features, 2 * features), pack_type),
            pltpu.VMEM((features, 2 * states), BF16),
        ],
        24,
        10,
        me, block_input, out_grad, normed, source, ends, hold, carry,
        held, came, held_other, came_other, vectors, params, masks, turn, regroup,
    )
    half_rows = plan.count // 2 * long
    pieces = plan.halves
    outs = call(
        weight_kernel,
        plan,
        [shape((half_rows // pieces, block), BF16)] * (2 * pieces),
        [
            pltpu.VMEM((features, 2 * features), F32),
            pltpu.VMEM((features, 2 * states), F32),
        ],
        10,
        2.5,
        me, act, unit_grad, lru_grad, low, regroup,
    )
    w_keeps, w_sends = outs[::2], outs[1::2]
    w_others = [flip(send, 0, plan.count) for send in w_sends]
    back_ends, back_hold, back = call(
        back_kernel,
        plan,
        [shape((chunks, 2 * states)), shape((chunks, LANES)), shape((8, 2 * states))],
        [],
        8,
        1,
        me, after(state_grad, *w_sends), params, masks,
    )
    back = flip(back, 0, plan.count) if plan.pieces == 2 else jnp.zeros_like(back)
    halves = [
        cut(added(keep, after(other, back_ends))) for keep, other in zip(w_keeps, w_others)
    ]
    w_others = [flip(half[1], bit, plan.count) for half, bit in zip(halves, (2, 3))]
    back_ends = after(back_ends, *(half[1] for half in halves))
    b_keep, b_send, normed_grad = call(
        leave_kernel,
        plan,
        [
            shape((half_rows, 2 * own), BF16),
            shape((half_rows + vector_rows, 2 * own), BF16),
            shape((rows, features)),
        ],
        [
            pltpu.VMEM(full, F32),
            pltpu.VMEM(full, BF16),
            pltpu.VMEM((features, 2 * states), F32),
        ],
        14,
        4.5,
        me, block_input, stats, normed, source, back_ends, back_hold, back, hidden,
        state_grad, lru_grad, input_map, vectors, params, masks, sums, turn, regroup,
    )
    w_others = [after(other, b_keep) for other in w_others]
    halves = [cut(added(half[0], other)) for half, other in zip(halves, w_others)]
    b_other = after(flip(b_send, 0, plan.count), *(half[1] for half in halves))
    b_keep, b_send = summed_step(b_keep, b_send, b_other)
    b_other = flip(b_send, 1, plan.count)
    w_others = [flip(half[1], bit, plan.count) for half, bit in zip(halves, (3, 2))]
    b_keep, b_send = summed_step(b_keep, b_send, b_other)
    halves = [cut(added(half[0], after(other, b_send))) for half, other in zip(halves, w_others)]
    w_keep = joined(*(half[0] for half in halves))
    w_send = joined(*(half[1] for half in halves))
    for bit in range(2, plan.bits - 1):
        w_bit = 1 if bit == 2 else bit + 1
        b_other = flip(b_send, bit, plan.count)
        w_other = flip(w_send, w_bit, plan.count)
        b_keep, b_send = summed_step(b_keep, b_send, b_other)
        if w_bit < plan.bits - 1:
            w_other = after(w_other, b_send)
            total = added(w_keep, w_other).reshape(pieces, -1, block)
            size = total.shape[1] // 2
            w_keep = total[:, :size].reshape(-1, block).astype(BF16)
            w_send = total[:, size:].reshape(-1, block).astype(BF16)
    (input_grad,) = call(
        input_kernel,
        plan,
        [shape((rows, features))],
        [],
        8,
        2.5,
        me, block_input, stats, out_grad, after(normed_grad, b_send), vectors,
    )
    w_mine = added(w_keep, w_other)
    b_other = after(flip(b_send, plan.bits - 1, plan.count), w_mine, input_grad)
    b_other, tail = b_other[:long], joined(b_send[long:], b_other[long:])
    small = (
        [(long, own)] * 4 + [(long, units)] * 2 + [(1, long)] * 5 + [(1, short)] * 3
    )
    (
        b_real_grad, b_imag_grad, c_real_grad, c_imag_grad, value_grad, gate_grad, *lines
    ) = call(
        last_kernel,
        plan,
        [shape(dims) for dims in small],
        [pltpu.VMEM(dims, F32) for dims in small] + [pltpu.SemaphoreType.DMA((14,))],
        4,
        2,
        me, b_keep, b_other, w_mine, tail,
        far_out=True,
    )
    gain_grad, bias_grad, skip_grad, value_line, gate_line, nu_grad, theta_grad, gamma_grad = (
        line.reshape(-1) for line in lines
    )
    return (
        mixed,
        input_grad,
        gain_grad,
        bias_grad,
        b_real_grad,
        b_imag_grad,
        c_real_grad,
        c_imag_grad,
        nu_grad,
        theta_grad,
        gamma_grad,
        skip_grad,
        value_grad,
        gate_grad,
        value_line,
        gate_line,
    )


def solution(mesh):
    in_specs = (
        P(("fsdp", "tensor"), None),
        P("fsdp"),
        P("fsdp"),
        P("fsdp"),
        P("fsdp", "tensor"),
        P("fsdp", "tensor"),
        P("fsdp", "tensor"),
        P("fsdp", "tensor"),
        P("fsdp"),
        P("fsdp"),
        P("fsdp"),
        P("fsdp"),
        P("fsdp", "tensor"),
        P("fsdp", "tensor"),
        P("fsdp"),
        P("fsdp"),
        P(("fsdp", "tensor"), None),
    )
    out_specs = (
        P(("fsdp", "tensor"), None),
        P(("fsdp", "tensor"), None),
        P("fsdp"),
        P("fsdp"),
        P("fsdp", "tensor"),
        P("fsdp", "tensor"),
        P("fsdp", "tensor"),
        P("fsdp", "tensor"),
        P("fsdp"),
        P("fsdp"),
        P("fsdp"),
        P("fsdp"),
        P("fsdp", "tensor"),
        P("fsdp", "tensor"),
        P("fsdp"),
        P("fsdp"),
    )
    return jax.shard_map(
        functools.partial(shards, mesh),
        mesh=mesh,
        in_specs=in_specs,
        out_specs=out_specs,
        check_vma=False,
    )
```

```python
import functools
import math

import jax
import jax.numpy as jnp
from jax import lax
from jax.experimental import pallas as pl
from jax.experimental.pallas import tpu as pltpu
from jax.sharding import PartitionSpec as P

SEQ_LEN = 2048
LANES = 128
TILE = 256
SIDE = 16
BLOCK = 1024
AXES = ("fsdp", "tensor")
norm_epsilon = 1e-05
GELU_SCALE = math.sqrt(2.0 / math.pi)
GELU_CUBE = 0.044715
F32 = jnp.float32
BF16 = jnp.bfloat16
MIB = 1024 * 1024


def log2(value):
    return value.bit_length() - 1


def flip(value, bit, count):
    return lax.ppermute(value, AXES, [(i, i ^ (1 << bit)) for i in range(count)])


def dot(left, right, left_dim=1, right_dim=0):
    return lax.dot_general(
        left, right, (((left_dim,), (right_dim,)), ((), ())), preferred_element_type=F32
    )


def fold_rows(value):
    rows, width = value.shape
    return jnp.sum(value.reshape(rows // 8, 8, width), axis=0)


def wide(mask, width):
    return jnp.concatenate([mask] * (width // LANES), axis=1)


def grid_index(dims, axis):
    return lax.broadcasted_iota(jnp.int32, dims, axis)


def regroup_matrix(states, shards):
    own = log2(states // shards)
    width = 2 * states
    source = grid_index((width, width), 0)
    target = grid_index((width, width), 1)
    part = (source >> own) & 1
    place = part * states + ((source >> (own + 1)) << own) + (source & ((1 << own) - 1))
    return jnp.where(place == target, 1.0, 0.0).astype(BF16)


def turn_matrix():
    source = grid_index((TILE, TILE), 0)
    target = grid_index((TILE, TILE), 1)
    bits = log2(SIDE)
    place = ((source & (SIDE - 1)) << bits) + (source >> bits)
    return jnp.where(place == target, 1.0, 0.0)


def turn_rows(turn, value):
    parts = [dot(turn, value[at : at + TILE]) for at in range(0, value.shape[0], TILE)]
    return jnp.concatenate(parts, axis=0).astype(BF16)


class Plan:
    def __init__(self, mesh, rows, group_rows, features, states, units):
        self.fsdp = mesh.shape["fsdp"]
        self.tensor = mesh.shape["tensor"]
        self.count = self.fsdp * self.tensor
        self.bits = log2(self.count)
        far = list(range(self.bits - 1, 3, -1))
        self.far = far
        self.up = [*far, 3, 2, 1, 0]
        self.up_crossed = ([*far, 1, 3, 2, 0], [*far, 1, 2, 3, 0])
        self.down = [0, 1, 2, 3, *far[::-1]]
        self.down_crossed = ([0, 2, 3, 1, *far[::-1]], [0, 3, 2, 1, *far[::-1]])
        self.halves = 2 if features // self.fsdp >= 32 else 1
        self.rows = rows
        self.group_rows = group_rows
        self.features = features
        self.states = states
        self.units = units
        self.own_states = states // self.tensor
        self.own_rows = features // self.fsdp
        self.pieces = SEQ_LEN // rows
        self.tiles = rows // TILE
        self.chunks = self.tiles * SIDE
        self.block = BLOCK if rows % BLOCK == 0 else TILE
        self.blocks = rows // self.block

    def slot_owner(self, slot, me, order):
        owner = me
        for place, bit in enumerate(order):
            owner = owner ^ (((slot >> (self.bits - 1 - place)) & 1) << bit)
        shift = log2(self.tensor)
        return owner >> shift, owner & (self.tensor - 1)

    def block_rows(self, index):
        return pl.ds(pl.multiple_of(index * self.block, self.block), self.block)


def step_rows(tile, place):
    return pl.ds(pl.multiple_of(tile * TILE + place * SIDE, SIDE), SIDE)


def scan_pass(plan, keep_ref, start, extra, reverse, visit):
    def step(index, carried):
        now, extra = carried
        place = SIDE - 1 - index if reverse else index
        after = []
        for tile in range(plan.tiles):
            at = step_rows(tile, place)
            state, extra = visit(tile, at, keep_ref[at, :], now[tile], extra)
            after.append(state)
        return after, extra

    return lax.fori_loop(0, SIDE, step, (start, extra), unroll=True)


def local_ends(plan, source_ref, keep_ref, rate, reverse):
    states = plan.states
    zero = jnp.zeros((SIDE, states), F32)
    rate_re = jnp.broadcast_to(rate[0], zero.shape)
    rate_im = jnp.broadcast_to(rate[1], zero.shape)
    one = jnp.ones((SIDE, LANES), F32)

    def visit(tile, at, keep, state, extra):
        now_re, now_im, hold = state
        held = wide(keep, states)
        pass_re, pass_im = held * rate_re, held * rate_im
        source = source_ref[at, :]
        next_re = (source[:, :states] + pass_re * now_re) - pass_im * now_im
        next_im = (source[:, states:] + pass_re * now_im) + pass_im * now_re
        return (next_re, next_im, hold * keep), extra

    ends, _ = scan_pass(plan, keep_ref, [(zero, zero, one)] * plan.tiles, 0, reverse, visit)
    return tuple(jnp.concatenate([end[part] for end in ends], axis=0) for part in range(3))


def shifted(value, distance, reverse):
    count = value.shape[0]
    row = grid_index(value.shape, 0)
    if reverse:
        moved = pltpu.roll(value, count - distance, 0)
        return jnp.where(row < count - distance, moved, 0.0)
    moved = pltpu.roll(value, distance, 0)
    return jnp.where(row >= distance, moved, 0.0)


def chunk_entries(plan, ends_re, ends_im, hold, rate, start, reverse):
    states, count = plan.states, plan.chunks
    power_re, power_im = rate
    for _ in range(log2(SIDE)):
        power_re, power_im = power_re * power_re - power_im * power_im, 2.0 * power_re * power_im
    first = count - 1 if reverse else 0
    if start is not None:
        at_first = grid_index((count, states), 0) == first
        held = jnp.where(at_first, wide(hold, states), 0.0)
        pass_re, pass_im = held * power_re, held * power_im
        ends_re = ends_re + (pass_re * start[0] - pass_im * start[1])
        ends_im = ends_im + (pass_re * start[1] + pass_im * start[0])
    distance = 1
    while distance < count:
        earlier_re = shifted(ends_re, distance, reverse)
        earlier_im = shifted(ends_im, distance, reverse)
        held = wide(hold, states)
        pass_re, pass_im = held * power_re, held * power_im
        ends_re = ends_re + (pass_re * earlier_re - pass_im * earlier_im)
        ends_im = ends_im + (pass_re * earlier_im + pass_im * earlier_re)
        hold = hold * shifted(hold, distance, reverse)
        power_re, power_im = power_re * power_re - power_im * power_im, 2.0 * power_re * power_im
        distance *= 2
    last = slice(0, 1) if reverse else slice(count - 1, count)
    leaving = jnp.concatenate([ends_re[last], ends_im[last]], axis=1)
    if start is None:
        return None, leaving
    entry_re = shifted(ends_re, 1, reverse) + jnp.where(at_first, start[0], 0.0)
    entry_im = shifted(ends_im, 1, reverse) + jnp.where(at_first, start[1], 0.0)
    entries = []
    for tile in range(plan.tiles):
        at = slice(tile * SIDE, (tile + 1) * SIDE)
        entries.append((entry_re[at], entry_im[at]))
    return entries, leaving


def block_places(plan, me, order, refs, base, rows, start):
    slot = 0
    for ref in refs:
        for place in range(plan.count // len(refs)):
            band, shard = plan.slot_owner(slot, me, order)
            slot += 1
            first = pl.multiple_of(band * plan.own_rows + start, rows)
            yield ref, base + place * rows, pl.ds(first, rows), shard


def collect(plan, me, order, refs, base, rows, start, targets):
    for ref, row, at, shard in block_places(plan, me, order, refs, base, rows, start):
        for first, width, out_ref, lanes in targets:
            column = pl.multiple_of(lanes + shard * width, LANES)
            out_ref[at, pl.ds(column, width)] = ref[row : row + rows, first : first + width].astype(
                out_ref.dtype
            )


def distribute(plan, me, order, refs, base, rows, start, targets):
    for ref, row, at, shard in block_places(plan, me, order, refs, base, rows, start):
        for first, width, full_ref, lanes in targets:
            column = pl.multiple_of(lanes + shard * width, LANES)
            ref[row : row + rows, first : first + width] = full_ref[at, pl.ds(column, width)].astype(
                ref.dtype
            )


def half_blocks(plan, orders, arrays):
    rows = plan.own_rows // plan.halves
    for half in range(plan.halves):
        yield orders[half], half * plan.count // arrays * rows, rows, half * rows


def start_copies(pairs, sems):
    copies = [
        pltpu.make_async_copy(source, target, sems.at[place])
        for place, (source, target) in enumerate(pairs)
    ]
    for copy in copies:
        copy.start()
    return copies


def pack_kernel(plan, me_ref, *refs):
    sources, outs, held, sems = refs[:14], refs[14:16], refs[16:30], refs[30]
    copies = start_copies(list(zip(sources, held)), sems)
    first_ref, second_ref = outs
    band = me_ref[0] >> log2(plan.tensor)
    rows, features = plan.own_rows, plan.features
    for copy in copies:
        copy.wait()
    first_ref[:rows, :] = jnp.concatenate([held[0][...], held[1][...]], axis=1)
    second_ref[...] = jnp.concatenate([ref[...] for ref in held[2:6]], axis=1)
    placed = []
    lane = grid_index((1, features), 1)
    for ref in held[6:]:
        length = ref.shape[1]
        value = ref[...].astype(F32)
        value = jnp.concatenate([value] * (features // length), axis=1)
        placed.append(jnp.where((lane >> log2(length)) == band, value, 0.0))
    placed = jnp.concatenate(placed, axis=0).astype(BF16)
    for part in range(features // LANES):
        first_ref[rows + 8 * part : rows + 8 * part + 8, :] = placed[
            :, part * LANES : (part + 1) * LANES
        ]


def token_kernel(
    plan, me_ref, x_ref, segments_ref, stats_ref, masks_ref, turn_ref, regroup_ref, standard_ref,
    flags_ref,
):
    shard = me_ref[0] & (plan.tensor - 1)
    ids = segments_ref[...]
    count = ids.shape[0]
    lane = grid_index(ids.shape, 1)
    position = (grid_index(ids.shape, 0) * LANES + lane) & (SEQ_LEN - 1)
    turned = pltpu.roll(ids, 1, 1)
    before = jnp.where(lane == 0, pltpu.roll(turned, 1, 0), turned)
    turned = pltpu.roll(ids, LANES - 1, 1)
    after = jnp.where(lane == LANES - 1, pltpu.roll(turned, count - 1, 0), turned)
    flags_ref[0] = jnp.where((position > 0) & (ids == before), 1.0, 0.0)
    flags_ref[1] = jnp.where((position < SEQ_LEN - 1) & (ids == after), 1.0, 0.0)
    flags_ref[2] = jnp.where(ids > 0, 1.0, 0.0)
    turn = turn_matrix()
    turn_ref[...] = turn.astype(BF16)
    regroup_ref[...] = regroup_matrix(plan.states, plan.tensor)
    plain = jnp.where(grid_index((TILE, TILE), 0) == grid_index((TILE, TILE), 1), 1.0, 0.0)
    ones = jnp.ones((TILE, LANES), BF16)
    per_tile = TILE // LANES
    own = plan.rows // LANES
    flags = [flags_ref[kind, pl.ds(pl.multiple_of(shard * own, own), own), :] for kind in range(3)]
    for tile in range(plan.tiles):
        at = slice(tile * TILE, (tile + 1) * TILE)
        for kind in range(4):
            rows = flags[min(kind, 2)][tile * per_tile : (tile + 1) * per_tile, :]
            line = jnp.concatenate([rows[part : part + 1, :] for part in range(per_tile)], axis=1)
            spread = (plain if kind == 3 else turn) * line
            masks_ref[kind, at, :] = dot(spread.astype(BF16), ones)

    def rows_step(index, _):
        at = plan.block_rows(index)
        values = x_ref[at, :].astype(F32)
        mean = jnp.mean(values, axis=1, keepdims=True)
        centred = values - mean
        inverse = lax.rsqrt(jnp.mean(centred * centred, axis=1, keepdims=True) + norm_epsilon)
        standard_ref[at, :] = centred * inverse
        stats_ref[0, at, :] = jnp.broadcast_to(inverse, (plan.block, LANES))
        return 0

    lax.fori_loop(0, plan.blocks, rows_step, 0)


def standard_rows(plan, standard_ref, stats_ref, at):
    return standard_ref[at, :], wide(stats_ref[0, at, :], plan.features)


def read_vectors(vec_ref):
    count = vec_ref.shape[0] // 8
    parts = [vec_ref[8 * part : 8 * part + 8, :].astype(F32) for part in range(count)]
    return jnp.concatenate(parts, axis=1)


def received(carry_ref, wanted, states):
    value = jnp.where(wanted, carry_ref[0:1, :], 0.0)
    return value[:, :states], value[:, states:]


def enter_kernel(
    plan, me_ref, x_ref, stats_ref, b0_ref, b1_ref, vec_ref, masks_ref, turn_ref, regroup_ref,
    normed_ref, source_ref, ends_ref, hold_ref, carry_ref, input_map_ref, params_ref,
    pack_ref,
):
    states = plan.states
    collect(
        plan, me_ref[0], plan.up[::-1], (b0_ref, b1_ref), 0, plan.own_rows, 0,
        [(0, 2 * plan.own_states, pack_ref, 0)],
    )
    input_map_ref[...] = dot(
        pack_ref[...].astype(BF16), regroup_ref[...]
    ).astype(BF16)
    vectors = read_vectors(vec_ref)
    gain, shift = vectors[0:1], vectors[1:2]
    speed = jnp.exp(vectors[5:6, :states])
    modulus = jnp.exp(-speed)
    rotation = jnp.exp(vectors[6:7, :states])
    rate = (modulus * jnp.cos(rotation), modulus * jnp.sin(rotation))
    rest = 1.0 - modulus * modulus
    gamma = jnp.exp(vectors[7:8, :states]) * jnp.sqrt(rest)
    params_ref[...] = jnp.concatenate(
        [
            jnp.concatenate(rate, axis=1),
            jnp.concatenate([gamma, speed], axis=1),
            jnp.concatenate([modulus, rest], axis=1),
            jnp.concatenate([rotation, rotation], axis=1),
            jnp.zeros((4, 2 * states), F32),
        ],
        axis=0,
    )
    gamma_pair = jnp.concatenate([gamma, gamma], axis=1)
    turn = turn_ref[...]

    def rows_step(index, _):
        at = plan.block_rows(index)
        standard, _ = standard_rows(plan, x_ref, stats_ref, at)
        normed = (standard * gain + shift).astype(BF16)
        normed_ref[at, :] = normed
        turned = turn_rows(turn, normed)
        drive = dot(turned, input_map_ref[...])
        source_ref[at, :] = drive * gamma_pair * wide(masks_ref[2, at, :], 2 * states)
        return 0

    lax.fori_loop(0, plan.blocks, rows_step, 0)
    ends_re, ends_im, hold = local_ends(plan, source_ref, masks_ref.at[0], rate, False)
    ends_ref[...] = jnp.concatenate([ends_re, ends_im], axis=1)
    hold_ref[...] = hold
    _, leaving = chunk_entries(plan, ends_re, ends_im, hold, rate, None, False)
    carry_ref[...] = jnp.broadcast_to(leaving, carry_ref.shape)


def middle_kernel(
    plan, me_ref, x_ref, grad_ref, normed_ref, source_ref, ends_ref, hold_ref, carry_ref,
    g0_ref, g1_ref, g2_ref, g3_ref, vec_ref, params_ref, masks_ref, turn_ref, regroup_ref,
    mixed_ref, hidden_ref, lru_grad_ref, state_grad_ref, act_ref, unit_grad_ref, low_ref, sums_ref,
    pack_ref, wpack_ref, out_map_ref,
):
    states, features, units = plan.states, plan.features, plan.units
    pair = 2 * plan.own_states
    targets = [
        (0, pair, pack_ref, 0),
        (pair, units, wpack_ref, 0),
        (pair + units, units, wpack_ref, features),
    ]
    block_refs = (g0_ref, g1_ref, g2_ref, g3_ref)
    for order, base, rows, first in half_blocks(plan, plan.up_crossed, len(block_refs)):
        collect(plan, me_ref[0], order[::-1], block_refs, base, rows, first, targets)
    sign = jnp.where(grid_index((1, 2 * states), 1) < states, 1.0, -1.0)
    regroup = regroup_ref[...]
    out_map_ref[...] = (dot(pack_ref[...].astype(BF16), regroup) * sign).astype(BF16)
    rate = (params_ref[0:1, :states], params_ref[0:1, states:])
    start = received(carry_ref, me_ref[0] & 1 == 1, states)
    entries, _ = chunk_entries(
        plan, ends_ref[:, :states], ends_ref[:, states:], hold_ref[...], rate, start, False
    )
    rate_re = jnp.broadcast_to(rate[0], (SIDE, states))
    rate_im = jnp.broadcast_to(rate[1], (SIDE, states))

    def visit(tile, at, keep, state, extra):
        now_re, now_im = state
        held = wide(keep, states)
        pass_re, pass_im = held * rate_re, held * rate_im
        source = source_ref[at, :]
        next_re = (source[:, :states] + pass_re * now_re) - pass_im * now_im
        next_im = (source[:, states:] + pass_re * now_im) + pass_im * now_re
        hidden_ref[at, :states] = next_re
        hidden_ref[at, states:] = next_im
        return (next_re, next_im), extra

    scan_pass(plan, masks_ref.at[0], entries, 0, False, visit)
    vectors = read_vectors(vec_ref)
    skip = vectors[2:3]
    biases = jnp.concatenate([vectors[3:4], vectors[4:5]], axis=1)
    sums_ref[...] = jnp.zeros_like(sums_ref)
    turn = turn_ref[...]

    def rows_step(index, _):
        at = plan.block_rows(index)
        low = turn_rows(turn, hidden_ref[at, :].astype(BF16))
        low_ref[at, :] = low
        normed = normed_ref[at, :].astype(F32)
        lru = dot(low, out_map_ref[...], 1, 1) + skip * normed
        square = lru * lru
        bent = jnp.tanh(lru * (GELU_SCALE + (GELU_SCALE * GELU_CUBE) * square))
        half = 0.5 + 0.5 * bent
        act_wide = lru * half
        slope = half + act_wide * (1.0 - half) * (
            2.0 * GELU_SCALE + (6.0 * GELU_SCALE * GELU_CUBE) * square
        )
        act = act_wide.astype(BF16)
        act_ref[at, :] = act
        mapped = dot(act, wpack_ref[...].astype(BF16)) + biases
        value = mapped[:, :features]
        live_half = wide(0.5 * masks_ref[3, at, :], features)
        opening = live_half + live_half * jnp.tanh(0.5 * mapped[:, features:])
        gated = value * opening
        mixed_ref[at, :] = (x_ref[at, :].astype(F32) + gated).astype(BF16)
        value_grad = grad_ref[at, :].astype(F32) * opening
        gate_grad = value_grad * (value - gated)
        sums_ref[8:16, :] += fold_rows(value_grad)
        sums_ref[16:24, :] += fold_rows(gate_grad)
        unit_grad = jnp.concatenate([value_grad, gate_grad], axis=1).astype(BF16)
        unit_grad_ref[at, :] = unit_grad
        act_grad = dot(unit_grad, wpack_ref[...].astype(BF16), 1, 1)
        lru_grad = act_grad * slope
        sums_ref[0:8, :] += fold_rows(lru_grad * normed)
        lru_grad = lru_grad.astype(BF16)
        lru_grad_ref[at, :] = lru_grad
        turned = turn_rows(turn, lru_grad)
        state_grad_ref[at, :] = dot(turned, out_map_ref[...])
        return 0

    lax.fori_loop(0, plan.blocks, rows_step, 0)


def back_kernel(
    plan, me_ref, state_grad_ref, params_ref, masks_ref, back_ends_ref, back_hold_ref, back_ref
):
    states = plan.states
    back_rate = (params_ref[0:1, :states], -params_ref[0:1, states:])
    ends_re, ends_im, hold = local_ends(plan, state_grad_ref, masks_ref.at[1], back_rate, True)
    back_ends_ref[...] = jnp.concatenate([ends_re, ends_im], axis=1)
    back_hold_ref[...] = hold
    _, leaving = chunk_entries(plan, ends_re, ends_im, hold, back_rate, None, True)
    back_ref[...] = jnp.broadcast_to(leaving, back_ref.shape)


def weight_kernel(
    plan, me_ref, act_ref, unit_grad_ref, lru_grad_ref, low_ref, regroup_ref, *refs
):
    outs, (full_ref, out_ref) = refs[:-2], refs[-2:]
    states, features, units = plan.states, plan.features, plan.units
    pair = 2 * plan.own_states
    sign = jnp.where(grid_index((1, 2 * states), 1) < states, 1.0, -1.0)
    full_ref[...] = dot(act_ref[...], unit_grad_ref[...], 0, 0)
    out_grad = dot(lru_grad_ref[...], low_ref[...], 0, 0) * sign
    out_ref[...] = dot(out_grad.astype(BF16), regroup_ref[...], 1, 1)
    targets = [
        (0, pair, out_ref, 0),
        (pair, units, full_ref, 0),
        (pair + units, units, full_ref, features),
    ]
    for half, (order, _, rows, first) in enumerate(half_blocks(plan, plan.down_crossed, 2)):
        pair_refs = outs[2 * half : 2 * half + 2]
        distribute(plan, me_ref[0], order, pair_refs, 0, rows, first, targets)


def leave_kernel(
    plan, me_ref, x_ref, stats_ref, normed_ref, source_ref, ends_ref, hold_ref, carry_ref, hidden_ref,
    state_grad_ref, lru_grad_ref, input_map_ref, vec_ref, params_ref, masks_ref, sums_ref,
    turn_ref, regroup_ref,
    keep_ref, send_ref, normed_grad_ref,
    drive_grad_ref, low_ref, full_ref,
):
    states, features = plan.states, plan.features
    params = params_ref[...]
    rate = (params[0:1, :states], params[0:1, states:])
    gamma, speed = params[1:2, :states], params[1:2, states:]
    modulus, rest = params[2:3, :states], params[2:3, states:]
    rotation = params[3:4, :states]
    back_rate = (rate[0], -rate[1])
    start = received(carry_ref, me_ref[0] & 1 == 0, states)
    entries, _ = chunk_entries(
        plan, ends_ref[:, :states], ends_ref[:, states:], hold_ref[...], back_rate, start, True
    )
    zero = jnp.zeros((SIDE, states), F32)
    rate_re = jnp.broadcast_to(back_rate[0], zero.shape)
    rate_im = jnp.broadcast_to(back_rate[1], zero.shape)
    gamma_wide = jnp.broadcast_to(gamma, zero.shape)

    def visit(tile, at, keep, state, sums):
        now_re, now_im = state
        held = wide(keep, states)
        next_re, next_im = held * now_re, held * now_im
        hidden_re, hidden_im = hidden_ref[at, :states], hidden_ref[at, states:]
        now_re = (state_grad_ref[at, :states] + rate_re * next_re) - rate_im * next_im
        now_im = (state_grad_ref[at, states:] + rate_re * next_im) + rate_im * next_re
        sums = (
            sums[0] + (hidden_re * next_re + hidden_im * next_im),
            sums[1] + (hidden_re * next_im - hidden_im * next_re),
            sums[2] + (source_ref[at, :states] * now_re + source_ref[at, states:] * now_im),
        )
        scale = gamma_wide * wide(masks_ref[2, at, :], states)
        drive_grad_ref[at, :states] = scale * now_re
        drive_grad_ref[at, states:] = scale * now_im
        return (now_re, now_im), sums

    _, sums = scan_pass(plan, masks_ref.at[1], entries, (zero, zero, zero), True, visit)
    rate_sum_re, rate_sum_im, gamma_sum = (jnp.sum(part, axis=0, keepdims=True) for part in sums)
    nu_grad = speed * (
        gamma_sum * modulus * modulus / rest - (rate_sum_re * rate[0] + rate_sum_im * rate[1])
    )
    theta_grad = rotation * (rate_sum_im * rate[0] - rate_sum_re * rate[1])
    vectors = read_vectors(vec_ref)
    skip = vectors[2:3]
    gain_sum = jnp.zeros((8, features), F32)
    turn = turn_ref[...]

    def rows_step(index, sums):
        gain_sum, shift_sum = sums
        at = plan.block_rows(index)
        low = turn_rows(turn, drive_grad_ref[at, :].astype(BF16))
        low_ref[at, :] = low
        normed_grad = dot(low, input_map_ref[...], 1, 1) + skip * lru_grad_ref[at, :].astype(F32)
        normed_grad_ref[at, :] = normed_grad
        standard, _ = standard_rows(plan, x_ref, stats_ref, at)
        return gain_sum + fold_rows(normed_grad * standard), shift_sum + fold_rows(normed_grad)

    gain_sum, shift_sum = lax.fori_loop(0, plan.blocks, rows_step, (gain_sum, gain_sum))
    into = dot(normed_ref[...], low_ref[...], 0, 0)
    full_ref[...] = dot(into.astype(BF16), regroup_ref[...], 1, 1)
    distribute(
        plan, me_ref[0], plan.down, (keep_ref, send_ref), 0, plan.own_rows, 0,
        [(0, 2 * plan.own_states, full_ref, 0)],
    )
    empty = jnp.zeros((1, features - states), F32)
    vector_sums = jnp.concatenate(
        [jnp.sum(part, axis=0, keepdims=True) for part in (gain_sum, shift_sum)]
        + [
            jnp.sum(sums_ref[8 * place : 8 * place + 8, :], axis=0, keepdims=True)
            for place in range(3)
        ]
        + [jnp.concatenate([part, empty], axis=1) for part in (nu_grad, theta_grad, gamma_sum)],
        axis=0,
    )
    base = plan.own_rows * plan.count // 2
    for part in range(features // LANES):
        piece = vector_sums[:, part * LANES : (part + 1) * LANES]
        send_ref[base + 8 * part : base + 8 * part + 8, :] = piece.astype(BF16)


def last_kernel(plan, me_ref, *refs):
    b_keep, b_other, w_mine_ref, tail_ref = refs[:4]
    outs, held, sems = refs[4:18], refs[18:32], refs[32]
    own, units = plan.own_states, plan.units
    b_mine = b_keep[...].astype(F32) + b_other[...].astype(F32)
    w_mine = w_mine_ref[...]
    half = tail_ref.shape[0] // 2
    vectors = tail_ref[:half, :].astype(F32) + tail_ref[half:, :].astype(F32)
    count = half // 8
    vectors = jnp.concatenate([vectors[8 * part : 8 * part + 8] for part in range(count)], axis=1)
    band = me_ref[0] >> log2(plan.tensor)
    at = grid_index((plan.features, LANES), 0)
    lane = grid_index((plan.features, LANES), 1)

    def pick(length):
        chosen = jnp.where(at == band * length + lane, 1.0, 0.0)
        return lax.dot_general(
            vectors,
            chosen,
            (((1,), (0,)), ((), ())),
            precision=lax.Precision.HIGHEST,
            preferred_element_type=F32,
        )

    long, short = plan.own_rows, plan.states // plan.fsdp
    long_part, short_part = pick(long), pick(short)
    held[0][...] = b_mine[:, :own]
    held[1][...] = b_mine[:, own:]
    held[2][...] = w_mine[:, :own]
    held[3][...] = w_mine[:, own : 2 * own]
    held[4][...] = w_mine[:, 2 * own : 2 * own + units]
    held[5][...] = w_mine[:, 2 * own + units :]
    for place in range(8):
        part, length = (long_part, long) if place < 5 else (short_part, short)
        held[6 + place][...] = part[place : place + 1, :length]
    for copy in start_copies(list(zip(held, outs)), sems):
        copy.wait()


def input_kernel(plan, me_ref, x_ref, stats_ref, grad_ref, normed_grad_ref, vec_ref, input_grad_ref):
    gain = read_vectors(vec_ref)[0:1]

    def rows_step(index, _):
        at = plan.block_rows(index)
        standard, inverse = standard_rows(plan, x_ref, stats_ref, at)
        scaled = normed_grad_ref[at, :] * gain
        input_grad_ref[at, :] = grad_ref[at, :].astype(F32) + inverse * (
            scaled
            - jnp.mean(scaled, axis=1, keepdims=True)
            - standard * jnp.mean(scaled * standard, axis=1, keepdims=True)
        )
        return 0

    lax.fori_loop(0, plan.blocks, rows_step, 0)


def call(kernel, plan, outs, scratch, limit, time, *args, far_in=0, far_out=False):
    args = [*args[:1], *(pltpu.with_memory_space_constraint(a, pltpu.HBM) for a in args[1 : 1 + far_in]), *args[1 + far_in :]]
    whole = pl.BlockSpec(memory_space=pltpu.VMEM)
    far = pl.BlockSpec(memory_space=pltpu.HBM)
    return pl.pallas_call(
        functools.partial(kernel, plan),
        out_shape=outs,
        in_specs=[pl.BlockSpec(memory_space=pltpu.SMEM)]
        + [far] * far_in
        + [whole] * (len(args) - 1 - far_in),
        out_specs=[far if far_out else whole] * len(outs),
        scratch_shapes=scratch,
        compiler_params=pltpu.CompilerParams(vmem_limit_bytes=limit * MIB),
        cost_estimate=pl.CostEstimate(
            flops=int(time * 1e9), bytes_accessed=int(time * 3.5e6), transcendentals=0
        ),
    )(*args)


def shape(dims, dtype=F32):
    return jax.ShapeDtypeStruct(dims, dtype)


def after(value, *others):
    return lax.optimization_barrier((value, *others))[0]


def joined(*parts):
    return jnp.concatenate(parts, axis=0)


def gather_blocks(plan, first, summed, second, cover):
    count, width = plan.count, second.shape[1]
    tensor_bits = log2(plan.tensor)
    other = None

    def first_step(bit):
        rows = first.shape[0]
        if bit < tensor_bits:
            got = flip(first, bit, count)
            return got, joined(first, got), summed
        got = flip(joined(first, summed), bit, count)
        if other is None:
            got = after(got, cover, second_other)
        return got, joined(first, got[:rows]), summed + got[rows:]

    for bit in plan.far:
        second_other = flip(second if other is None else after(second, other), bit, count)
        other, first, summed = first_step(bit)
        second = joined(second, second_other)
    second = joined(second, flip(after(second, other), 1, count))
    other, first, summed = first_step(3)
    blocks = second.reshape(-1, plan.own_rows, width)
    size = plan.own_rows // plan.halves
    halves = [
        after(blocks[:, half * size : half * size + size].reshape(-1, width), other)
        for half in range(plan.halves)
    ]
    halves = [joined(part, flip(part, bit, count)) for part, bit in zip(halves, (3, 2))]
    other, first, summed = first_step(2)
    halves = [(part, flip(part, bit, count)) for part, bit in zip(halves, (2, 3))]
    other, first, summed = first_step(1)
    return first, flip(first, 0, count), summed, halves


def cut(value):
    count = value.shape[0] // 2
    return value[:count].astype(BF16), value[count:].astype(BF16)


def added(keep, other):
    return keep.astype(F32) + other.astype(F32)


def summed_step(keep, send, other):
    count = keep.shape[0]
    summed = added(send[count:], other[count:]).astype(BF16)
    keep, send = cut(added(keep, other[:count]))
    return keep, joined(send, summed)


def together(*values):
    return lax.optimization_barrier(values)


def shards(
    mesh,
    block_input,
    segments,
    ln_gain,
    ln_bias,
    b_real,
    b_imag,
    c_real,
    c_imag,
    nu_log,
    theta_log,
    gamma_log,
    d_skip,
    w_value,
    w_gate,
    b_value,
    b_gate,
    out_grad,
):
    band = lax.axis_index("fsdp")
    shard = lax.axis_index("tensor")
    rows, features = block_input.shape
    own = b_real.shape[1]
    plan = Plan(
        mesh, rows, segments.shape[0], features, own * mesh.shape["tensor"], w_value.shape[1]
    )
    states, units, chunks = plan.states, plan.units, plan.chunks
    me = (band * plan.tensor + shard).astype(jnp.int32).reshape(1)
    long, short = plan.own_rows, states // plan.fsdp
    vector_rows = 8 * features // LANES
    matrices = (b_real, b_imag, c_real, c_imag, w_value, w_gate)
    lines = [
        v.reshape(1, -1)
        for v in (ln_gain, ln_bias, d_skip, b_value, b_gate, nu_log, theta_log, gamma_log)
    ]
    block = 2 * own + 2 * units
    first, second = call(
        pack_kernel,
        plan,
        [shape((long + vector_rows, 2 * own), BF16), shape((long, block), BF16)],
        [pltpu.VMEM(v.shape, BF16) for v in (*matrices, *lines)] + [pltpu.SemaphoreType.DMA((14,))],
        4,
        1.5,
        me, *matrices, *lines,
        far_in=14,
    )
    stats, masks, turn, regroup, standard = call(
        token_kernel,
        plan,
        [
            shape((1, rows, LANES)),
            shape((4, rows, LANES)),
            shape((TILE, TILE), BF16),
            shape((2 * states, 2 * states), BF16),
            shape((rows, features)),
        ],
        [pltpu.VMEM((3, plan.group_rows // LANES, LANES), F32)],
        8,
        2,
        me, block_input, segments.reshape(-1, LANES),
    )
    b0, b1, vectors, halves = gather_blocks(plan, first[:long], first[long:], second, masks)

    pack_type = BF16 if long % 16 == 0 else F32
    full = (rows, 2 * states)
    normed, source, ends, hold, carry, input_map, params = call(
        enter_kernel,
        plan,
        [
            shape((rows, features), BF16),
            shape(full),
            shape((chunks, 2 * states)),
            shape((chunks, LANES)),
            shape((8, 2 * states)),
            shape((features, 2 * states), BF16),
            shape((8, 2 * states)),
        ],
        [pltpu.VMEM((features, 2 * states), pack_type)],
        8,
        0.3,
        me, standard, stats, b0, b1, vectors, masks, turn, regroup,
    )

    left = carry
    carry = flip(carry, 0, plan.count) if plan.pieces == 2 else jnp.zeros_like(carry)
    held = joined(*(part for part, _ in halves))
    held_other = flip(held, 0, plan.count)
    came = joined(*(after(got, left) for _, got in halves))
    came_other = flip(came, 0, plan.count)
    (
        mixed, hidden, lru_grad, state_grad, act, unit_grad, low, sums,
    ) = call(
        middle_kernel,
        plan,
        [
            shape((rows, features), BF16),
            shape(full),
            shape((rows, features), BF16),
            shape(full),
            shape((rows, features), BF16),
            shape((rows, 2 * features), BF16),
            shape(full, BF16),
            shape((24, features)),
        ],
        [
            pltpu.VMEM((features, 2 * states), pack_type),
            pltpu.VMEM((features, 2 * features), pack_type),
            pltpu.VMEM((features, 2 * states), BF16),
        ],
        24,
        10,
        me, block_input, out_grad, normed, source, ends, hold, carry,
        held, came, held_other, came_other, vectors, params, masks, turn, regroup,
    )
    half_rows = plan.count // 2 * long
    pieces = plan.halves
    outs = call(
        weight_kernel,
        plan,
        [shape((half_rows // pieces, block), BF16)] * (2 * pieces),
        [
            pltpu.VMEM((features, 2 * features), F32),
            pltpu.VMEM((features, 2 * states), F32),
        ],
        10,
        2.5,
        me, act, unit_grad, lru_grad, low, regroup,
    )
    w_keeps, w_sends = outs[::2], outs[1::2]
    w_others = [flip(send, 0, plan.count) for send in w_sends]
    back_ends, back_hold, back = call(
        back_kernel,
        plan,
        [shape((chunks, 2 * states)), shape((chunks, LANES)), shape((8, 2 * states))],
        [],
        8,
        1,
        me, after(state_grad, *w_sends), params, masks,
    )
    back = flip(back, 0, plan.count) if plan.pieces == 2 else jnp.zeros_like(back)
    halves = [
        cut(added(keep, after(other, back_ends))) for keep, other in zip(w_keeps, w_others)
    ]
    w_others = [flip(half[1], bit, plan.count) for half, bit in zip(halves, (2, 3))]
    back_ends = after(back_ends, *(half[1] for half in halves))
    b_keep, b_send, normed_grad = call(
        leave_kernel,
        plan,
        [
            shape((half_rows, 2 * own), BF16),
            shape((half_rows + vector_rows, 2 * own), BF16),
            shape((rows, features)),
        ],
        [
            pltpu.VMEM(full, F32),
            pltpu.VMEM(full, BF16),
            pltpu.VMEM((features, 2 * states), F32),
        ],
        14,
        4.5,
        me, standard, stats, normed, source, back_ends, back_hold, back, hidden,
        state_grad, lru_grad, input_map, vectors, params, masks, sums, turn, regroup,
    )
    w_others = [after(other, b_keep) for other in w_others]
    halves = [cut(added(half[0], other)) for half, other in zip(halves, w_others)]
    b_other = after(flip(b_send, 0, plan.count), *(half[1] for half in halves))
    b_keep, b_send = summed_step(b_keep, b_send, b_other)
    b_other = flip(b_send, 1, plan.count)
    w_others = [flip(half[1], bit, plan.count) for half, bit in zip(halves, (3, 2))]
    b_keep, b_send = summed_step(b_keep, b_send, b_other)
    halves = [cut(added(half[0], after(other, b_send))) for half, other in zip(halves, w_others)]
    w_keep = joined(*(half[0] for half in halves))
    w_send = joined(*(half[1] for half in halves))
    for bit in range(2, plan.bits - 1):
        w_bit = 1 if bit == 2 else bit + 1
        b_other = flip(b_send, bit, plan.count)
        w_other = flip(w_send, w_bit, plan.count)
        b_keep, b_send = summed_step(b_keep, b_send, b_other)
        if w_bit < plan.bits - 1:
            w_other = after(w_other, b_send)
            total = added(w_keep, w_other).reshape(pieces, -1, block)
            size = total.shape[1] // 2
            w_keep = total[:, :size].reshape(-1, block).astype(BF16)
            w_send = total[:, size:].reshape(-1, block).astype(BF16)
    (input_grad,) = call(
        input_kernel,
        plan,
        [shape((rows, features))],
        [],
        8,
        2.5,
        me, standard, stats, out_grad, after(normed_grad, b_send), vectors,
    )
    w_mine = added(w_keep, w_other)
    b_other = after(flip(b_send, plan.bits - 1, plan.count), w_mine, input_grad)
    b_other, tail = b_other[:long], joined(b_send[long:], b_other[long:])
    small = (
        [(long, own)] * 4 + [(long, units)] * 2 + [(1, long)] * 5 + [(1, short)] * 3
    )
    (
        b_real_grad, b_imag_grad, c_real_grad, c_imag_grad, value_grad, gate_grad, *lines
    ) = call(
        last_kernel,
        plan,
        [shape(dims) for dims in small],
        [pltpu.VMEM(dims, F32) for dims in small] + [pltpu.SemaphoreType.DMA((14,))],
        4,
        2,
        me, b_keep, b_other, w_mine, tail,
        far_out=True,
    )
    gain_grad, bias_grad, skip_grad, value_line, gate_line, nu_grad, theta_grad, gamma_grad = (
        line.reshape(-1) for line in lines
    )
    return (
        mixed,
        input_grad,
        gain_grad,
        bias_grad,
        b_real_grad,
        b_imag_grad,
        c_real_grad,
        c_imag_grad,
        nu_grad,
        theta_grad,
        gamma_grad,
        skip_grad,
        value_grad,
        gate_grad,
        value_line,
        gate_line,
    )


def solution(mesh):
    in_specs = (
        P(("fsdp", "tensor"), None),
        P("fsdp"),
        P("fsdp"),
        P("fsdp"),
        P("fsdp", "tensor"),
        P("fsdp", "tensor"),
        P("fsdp", "tensor"),
        P("fsdp", "tensor"),
        P("fsdp"),
        P("fsdp"),
        P("fsdp"),
        P("fsdp"),
        P("fsdp", "tensor"),
        P("fsdp", "tensor"),
        P("fsdp"),
        P("fsdp"),
        P(("fsdp", "tensor"), None),
    )
    out_specs = (
        P(("fsdp", "tensor"), None),
        P(("fsdp", "tensor"), None),
        P("fsdp"),
        P("fsdp"),
        P("fsdp", "tensor"),
        P("fsdp", "tensor"),
        P("fsdp", "tensor"),
        P("fsdp", "tensor"),
        P("fsdp"),
        P("fsdp"),
        P("fsdp"),
        P("fsdp"),
        P("fsdp", "tensor"),
        P("fsdp", "tensor"),
        P("fsdp"),
        P("fsdp"),
    )
    return jax.shard_map(
        functools.partial(shards, mesh),
        mesh=mesh,
        in_specs=in_specs,
        out_specs=out_specs,
        check_vma=False,
    )
```
